32 devices in a mesh: row: 2 (over y), col: 4 (over x, core), band: 4 (over z).
Axes of the slice: x: 2, y: 2, z: 4, core: 2. Of those that a mesh axis runs over, the one named last changes fastest.
Arguments:
- vis: bfloat16 [64, 4, 2, 512, 512], P('band', None, None, 'row', 'col'), may hold values from -200 to 200
- flags: int32 [64, 4, 512], P('band'), may hold values 0 or 1
- positions: float32 [4, 3, 512], replicated, may hold values from -4 to 4
- lmn: float32 [3, 8], replicated, may hold values from -3 to 3
- flux: float32 [64, 8], P('band'), may hold values from 0.5 to 2
- gains: float32 [64, 4, 2, 8, 512], P('band', None, None, None, ('row', 'col')), may hold values from -6 to 6
- duals: float32 [64, 4, 2, 8, 512], P('band', None, None, None, ('row', 'col')), may hold values from -2 to 2
Outputs:
- gains_out: float32 [64, 4, 2, 8, 512], P('band', None, None, None, ('row', 'col'))
- duals_out: float32 [64, 4, 2, 8, 512], P('band', None, None, None, ('row', 'col'))
The draws below stay inside these ranges and needn't reach their ends.
All inputs are finite; a program needn't handle non-finite values. No bound on the sum of `flags` on one device may be relied on, other than what follows from the above.
Results may differ from the reference program's by a relative error of at most 0.0003.
Values sent between devices are 32-bit elements; how exact they have to be, the bound alone decides.
No kernel may reach another device: no remote copies, remote signals or barrier semaphores. Data moves between devices by JAX's collectives and lax.ppermute only.
A program may use at most 128 MiB of HBM per device.

```python
import math
import jax
import jax.numpy as jnp
from jax import lax

S = 512
DIRS = 8
F = 64
TSTEP = 4
ITERS = 2


def draw_vis(key, part):
    shape = (F, TSTEP, 2, S, S)
    base = jnp.clip(jax.random.normal(jax.random.fold_in(key, 11), shape, jnp.float32), -6.0, 6.0)
    station = 1.0 + 2.0 * jnp.arange(S, dtype=jnp.float32) / (S - 1)
    channel = 1.0 + 2.0 * jnp.arange(F, dtype=jnp.float32) / (F - 1)
    return (base * station[:, None] * channel[:, None, None, None, None]).astype(jnp.bfloat16)


def with_ends(values, rng, low, top_value):
    dims = values.shape
    place = [jax.random.randint(jax.random.fold_in(rng, axis), (), 0, dims[axis]) for axis in range(len(dims))]
    values = values.at[tuple(place)].set(low)
    longest = dims.index(max(dims))
    place[longest] = (place[longest] + 1) % dims[longest]
    return values.at[tuple(place)].set(top_value)


def shard_levels(key, extent, split, least, largest):
    level, own = 1.0, jax.random.fold_in(key, 6)
    for dim, blocks in split:
        heights = jnp.exp(jax.random.uniform(jax.random.fold_in(own, dim), (blocks,), jnp.float32, least / len(split), largest / len(split)))
        level = level * jnp.repeat(heights, extent[dim] // blocks).reshape([-1 if axis == dim else 1 for axis in range(len(extent))])
    return level


def bell_draw(own_key, dims, width, limit, shards=(), held_as=jnp.bfloat16):
    loudness = shard_levels(own_key, dims, shards, -0.22, 0.18) if shards else 1.0
    drawn = jax.random.normal(own_key, dims, jnp.float32) * width * loudness
    return jnp.minimum(jnp.maximum(drawn, -limit), limit).astype(held_as)


def setup_inputs(seed: int = 0) -> dict:
    arg_keys = jax.random.split(jax.random.key(seed), 8)
    vis = draw_vis(jax.random.fold_in(arg_keys[7], 71), 0)
    flags = with_ends((jax.random.randint(arg_keys[1], (F, TSTEP, S), 0, 8) < 7).astype(jnp.int32), jax.random.fold_in(arg_keys[1], 1), 0, 1)
    positions = bell_draw(arg_keys[2], (TSTEP, 3, S), 1.0, 4.0, (), jnp.float32)
    lmn = bell_draw(arg_keys[3], (3, DIRS), 0.5, 3.0, (), jnp.float32)
    flux = jnp.clip(jnp.exp(math.log(2.0) - 1.3862944 * jax.random.uniform(arg_keys[4], (F, DIRS), jnp.float32) ** shard_levels(arg_keys[4], (F, DIRS), ((0, 4),), -0.2, 0.2)), 0.5, 2.0)
    gains = bell_draw(arg_keys[5], (F, TSTEP, 2, DIRS, S), 1.0, 6.0, ((0, 4), (4, 8)), jnp.float32)
    duals = bell_draw(arg_keys[6], (F, TSTEP, 2, DIRS, S), 0.3, 2.0, ((0, 4), (4, 8)), jnp.float32)
    return dict(vis=vis, flags=flags, positions=positions, lmn=lmn, flux=flux, gains=gains, duals=duals)


PENALTY = 0.05
HIGH = lax.Precision.HIGHEST

def basis(count):
    grid = 2.0 * jnp.arange(count, dtype=jnp.float32) / (count - 1) - 1.0
    return jnp.stack([grid ** power for power in range(4)], axis=1)

def rotate(positions, lmn, freq):
    geometry = jnp.einsum('tks,kd->tds', positions, lmn, precision=HIGH)
    angle = 2.0 * math.pi * freq[:, None, None, None] * geometry[None]
    return (jnp.cos(angle), -jnp.sin(angle))

def complex_mul(a_re, a_im, b_re, b_im):
    return (a_re * b_re - a_im * b_im, a_re * b_im + a_im * b_re)

def solve_fit(rhs):
    full = basis(F)
    gram = jnp.dot(full.T, full, precision=HIGH)
    factor = jnp.linalg.cholesky(gram)
    flat = rhs.reshape(rhs.shape[0], -1)
    return jax.scipy.linalg.cho_solve((factor, True), flat).reshape(rhs.shape)

def reference(vis, flags, positions, lmn, flux, gains, duals):
    full = basis(F)
    freq = 1.0 + jnp.arange(F, dtype=jnp.float32) / F
    cos_all, sin_all = rotate(positions, lmn, freq)
    ids = jnp.arange(S, dtype=jnp.int32)
    distinct = (ids[:, None] != ids[None, :]).astype(jnp.float32)
    live = flags.astype(jnp.float32)

    def fit(gain, dual):
        rhs = jnp.einsum('fk,ftcds->ktcds', full, gain + dual, precision=HIGH)
        return solve_fit(rhs)

    def per_channel(items):
        visible, alive, row_re, row_im, col_re, col_im = items
        vis_re = visible[:, 0].astype(jnp.float32)
        vis_im = visible[:, 1].astype(jnp.float32)
        weight = alive[:, :, None] * alive[:, None, :] * distinct
        model_re = jnp.einsum('tdp,tdq->tpq', row_re, col_re, precision=HIGH) + jnp.einsum('tdp,tdq->tpq', row_im, col_im, precision=HIGH)
        model_im = jnp.einsum('tdp,tdq->tpq', row_im, col_re, precision=HIGH) - jnp.einsum('tdp,tdq->tpq', row_re, col_im, precision=HIGH)
        resid_re = weight * (vis_re - model_re)
        resid_im = weight * (vis_im - model_im)
        squares = jnp.sum(resid_re * resid_re + resid_im * resid_im)
        samples = jnp.sum(weight)
        sum_re = jnp.einsum('tpq,tdq->tdp', resid_re, col_re, precision=HIGH) - jnp.einsum('tpq,tdq->tdp', resid_im, col_im, precision=HIGH)
        sum_im = jnp.einsum('tpq,tdq->tdp', resid_re, col_im, precision=HIGH) + jnp.einsum('tpq,tdq->tdp', resid_im, col_re, precision=HIGH)
        denom = jnp.einsum('tpq,tdq->tdp', weight, col_re * col_re + col_im * col_im, precision=HIGH)
        return (jnp.stack([sum_re, sum_im, denom], axis=1), squares, samples)
    gain, dual = (gains, duals)
    coeffs = fit(gain, dual)
    for step in range(ITERS):
        target = jnp.einsum('fk,ktcds->ftcds', full, coeffs, precision=HIGH) - dual
        row_re, row_im = complex_mul(gain[:, :, 0], gain[:, :, 1], cos_all, sin_all)
        scale = flux[:, None, :, None]
        col_re = scale * row_re
        col_im = scale * row_im
        terms, squares, samples = lax.map(per_channel, (vis, live, row_re, row_im, col_re, col_im))
        rho = PENALTY * S * (jnp.sum(squares) / jnp.sum(samples) + 1e-06)
        num_re, num_im = complex_mul(cos_all, -sin_all, terms[:, :, 0], terms[:, :, 1])
        numer = jnp.stack([num_re, num_im], axis=2)
        denom = terms[:, :, 2:3]
        fresh = (numer + denom * gain + rho * target) / (denom + rho)
        gain = 0.5 * (gain + fresh)
        coeffs = fit(gain, dual)
        dual = dual + gain - jnp.einsum('fk,ktcds->ftcds', full, coeffs, precision=HIGH)
    return (gain, dual)
```

```python
import functools
import math

import jax
import jax.numpy as jnp
import numpy as np
from jax import lax
from jax.experimental import pallas as pl
from jax.experimental.pallas import tpu as pltpu
from jax.sharding import PartitionSpec as P

ITERS = 2
PENALTY = 0.05
HIGH = lax.Precision.HIGHEST
CHUNKS = 2
AXES = ("row", "col", "band")


def swap(x):
    half = x.shape[-1] // 2
    return pltpu.roll(x, half, x.ndim - 1)


def low_lanes(shape):
    return lax.broadcasted_iota(jnp.int32, shape, len(shape) - 1) < shape[-1] // 2


def join_low(a, b):
    return jnp.where(low_lanes(a.shape), a, swap(b))


def join_high(a, b):
    return jnp.where(low_lanes(a.shape), swap(a), b)


def column(ref, index, dirs, lanes):
    rows = lax.broadcasted_iota(jnp.int32, (dirs, lanes), 0)
    out = jnp.full((dirs, lanes), ref[0, index], jnp.float32)
    for d in range(1, dirs):
        out = jnp.where(rows == d, ref[d, index], out)
    return out


def cos_turns(r):
    t = 0.25 - jnp.abs(r)
    x = t * t
    coef = [(-1) ** n * (2.0 * math.pi) ** (2 * n + 1) / math.factorial(2 * n + 1) for n in range(7)]
    out = jnp.full_like(x, coef[-1])
    for c in coef[-2::-1]:
        out = out * x + c
    return out * t


def rotated(g, e):
    low = low_lanes(e.shape)
    turned = swap(e)
    cos2 = jnp.where(low, e, turned)
    sin2 = jnp.where(low, -turned, e)
    return g * cos2 + swap(g) * sin2


def counter_rotated(g, e):
    low = low_lanes(e.shape)
    turned = swap(e)
    cos2 = jnp.where(low, e, turned)
    sin2 = jnp.where(low, -turned, e)
    return g * cos2 - swap(g) * sin2


def start_kernel(dims, pos_ref, lmn_ref, freq_ref, gains_ref, e_ref, g_ref, *p_refs):
    F, T, D, O, R, C = dims
    W = 2 * O
    own = lax.axis_index("row") * C + lax.axis_index("col")
    first = lax.axis_index("band") * F
    low = low_lanes((D, W))
    shape = pos_ref[:, :, :O].shape
    pos = jnp.zeros(shape, jnp.float32)
    for k in range(R * C):
        pos = jnp.where(own == k, pos_ref[:, :, k * O : (k + 1) * O], pos)
    pos = jnp.concatenate([pos, pos], axis=-1)
    geometry = []
    for t in range(T):
        total = jnp.zeros((D, W), jnp.float32)
        for k in range(3):
            rows = lax.broadcasted_iota(jnp.int32, (D, W), 0)
            lm = jnp.full((D, W), lmn_ref[k, 0], jnp.float32)
            for d in range(1, D):
                lm = jnp.where(rows == d, lmn_ref[k, d], lm)
            total = total + lm * pos[k, t : t + 1, :]
        geometry.append(total)
    shift = jnp.where(low, 0.0, 0.25)
    per = F * T // len(p_refs)
    for f in range(F):
        nu = freq_ref[first + f]
        for t in range(T):
            ft = f * T + t
            turns = nu * geometry[t]
            r = turns - jnp.round(turns) + shift
            e = cos_turns(r - jnp.round(r))
            g = jnp.concatenate([gains_ref[f, t, 0], gains_ref[f, t, 1]], axis=-1)
            e_ref[ft] = e
            g_ref[ft] = g
            p_refs[ft // per][ft % per] = rotated(g, e)


def fit_kernel(dims, basis_ref, duals_ref, g_ref, u_ref, rhs_ref):
    F, T, D, O, R, C = dims
    first = lax.axis_index("band") * F
    for t in range(T):
        acc = [jnp.zeros((D, 2 * O), jnp.float32) for _ in range(4)]
        for f in range(F):
            ft = f * T + t
            u = jnp.concatenate([duals_ref[f, t, 0], duals_ref[f, t, 1]], axis=-1)
            u_ref[ft] = u
            total = u + g_ref[ft]
            for k in range(4):
                acc[k] = acc[k] + basis_ref[first + f, k] * total
        for k in range(4):
            rhs_ref[k * T + t] = acc[k]


def sum_kernel(dims, offset, flux_ref, live_ref, vis_ref, *refs):
    F, T, D, O, R, C = dims
    blocks, (keep_ref, send_ref, distinct) = refs[:R], refs[R:]
    rows, cols = vis_ref.shape[3], vis_ref.shape[4]
    step = pl.program_id(0)
    row = lax.axis_index("row")
    col = lax.axis_index("col")
    parity = col % 2

    @pl.when(step == 0)
    def _():
        p = lax.broadcasted_iota(jnp.int32, (rows, cols), 0) + row * rows
        q = lax.broadcasted_iota(jnp.int32, (rows, cols), 1) + col * cols
        distinct[...] = jnp.where(p == q, 0.0, 1.0).astype(jnp.bfloat16)

    group = vis_ref.shape[0]
    highs, lows = [], []
    mask = distinct[...]
    for i in range(group):
        scale = column(flux_ref, (offset + step) * group + i, D, cols)
        for t in range(T):
            ft = i * T + t
            a, b = blocks[0][ft], blocks[1][ft]
            first = jnp.where(row == 0, a, b)
            second = jnp.where(row == 0, b, a)
            weight = scale * live_ref[ft : ft + 1, :]
            re = join_low(first, second) * weight
            im = join_high(first, second) * weight
            x = jnp.concatenate(
                [jnp.concatenate([re, -im], axis=1), jnp.concatenate([im, re], axis=1)], axis=0
            )
            high = x.astype(jnp.bfloat16)
            low = (x - high.astype(jnp.float32)).astype(jnp.bfloat16)
            highs.append(high)
            lows.append(low)
            both = jnp.concatenate([high, low], axis=0)
            seen = jnp.concatenate([vis_ref[i, t, 0] * mask, vis_ref[i, t, 1] * mask], axis=1)
            v = lax.dot_general(
                both, seen, (((1,), (1,)), ((), ())), preferred_element_type=jnp.float32
            )
            v = v[: 2 * D] + v[2 * D :]
            v0, v1 = v[:, : 2 * O], v[:, 2 * O :]
            even, odd = join_low(v0, v1), join_high(v0, v1)
            keep_ref[ft] = jnp.where(parity == 0, even, odd)
            send_ref[ft] = jnp.where(parity == 0, odd, even)
    high = jnp.concatenate(highs, axis=0)
    low = jnp.concatenate(lows, axis=0)
    nt = (((1,), (1,)), ((), ()))
    gram = lax.dot_general(high, high, nt, preferred_element_type=jnp.float32)
    gram = gram + lax.dot_general(high, low, nt, preferred_element_type=jnp.float32)
    gram = gram + lax.dot_general(low, high, nt, preferred_element_type=jnp.float32)
    gram = jnp.where(block_mask(2 * D), gram, 0.0)
    folded = gram[: 2 * D]
    for i in range(1, 8):
        folded = folded + gram[i * 2 * D : (i + 1) * 2 * D]
    keep_ref[8] = folded
    send_ref[8] = folded


def block_mask(size):
    shape = (8 * size, 8 * size)
    a = lax.broadcasted_iota(jnp.int32, shape, 0) // size
    b = lax.broadcasted_iota(jnp.int32, shape, 1) // size
    return a == b


def residual_kernel(dims, live_ref, extra_ref, *refs):
    F, T, D, O, R, C = dims
    n = CHUNKS
    keeps, others, mine, theirs = refs[:n], refs[n : 2 * n], refs[2 * n : 3 * n], refs[3 * n : 4 * n]
    keep_ref, send_ref, scalar_ref = refs[4 * n :]
    W = 2 * O
    near = (lax.axis_index("col") // 2) == 0
    mask = block_mask(2 * D)
    eye = lax.broadcasted_iota(jnp.int32, (2 * D, W), 0) == (
        lax.broadcasted_iota(jnp.int32, (2 * D, W), 1) % (2 * D)
    )
    groups = F * T // 8
    per = groups // n
    total = jnp.zeros((2 * D, W), jnp.float32)
    for group in range(groups):
        ch, base = group // per, group % per
        gram = keeps[ch][base * 9 + 8] + others[ch][base * 9 + 8]
        diagonal = jnp.sum(jnp.where(eye, gram, 0.0), axis=0, keepdims=True)
        keep_ref[F * T, group : group + 1, :] = diagonal
        send_ref[F * T, group : group + 1, :] = diagonal
        spread = jnp.where(mask, jnp.concatenate([gram] * 8, axis=0), 0.0)
        station = []
        for i in range(8):
            a, b = mine[ch][base * 8 + i], theirs[ch][base * 8 + i]
            first = jnp.where(near, a, b)
            second = jnp.where(near, b, a)
            station += [join_low(first, second), join_high(first, second)]
        model = jnp.dot(
            spread, jnp.concatenate(station, axis=0), precision=HIGH,
            preferred_element_type=jnp.float32,
        )
        for i in range(8):
            ft = group * 8 + i
            live = live_ref[ft : ft + 1, :]
            v = keeps[ch][base * 9 + i] + others[ch][base * 9 + i]
            num = (v - model[i * 2 * D : (i + 1) * 2 * D]) * live
            z = jnp.concatenate(station[2 * i : 2 * i + 2], axis=0)
            total = total + z * (v * live + num)
            low, high = join_low(num[:D], num[D:]), join_high(num[:D], num[D:])
            keep_ref[ft] = jnp.where(near, low, high)
            send_ref[ft] = jnp.where(near, high, low)
    squares = -jnp.sum(total, axis=0, keepdims=True)
    squares = squares + swap(squares)
    scalar = jnp.where(low_lanes(squares.shape), squares, 0.0) + extra_ref[...]
    scalar_ref[...] = jnp.broadcast_to(scalar, scalar_ref.shape)


def update_kernel(dims, last, full, *refs):
    F, T, D, O, R, C = dims
    n = CHUNKS
    (flux_ref, basis_ref, coef_ref, keep_ref, come_ref, scalar_ref, live_ref, e_ref, g_ref,
     u_ref) = refs[:10]
    refs = refs[10:]
    p_refs, refs = refs[:n], refs[n:]
    rhs_refs, refs = refs[:4], refs[4:]
    first = lax.axis_index("band") * F
    W = 2 * O
    sums = jnp.sum(scalar_ref[...], axis=0, keepdims=True)
    low = low_lanes(sums.shape)
    squares = jnp.sum(jnp.where(low, sums, 0.0), axis=1, keepdims=True)
    samples = jnp.sum(jnp.where(low, 0.0, sums), axis=1, keepdims=True)
    squares = jnp.maximum(squares, 0.0)
    rho = PENALTY * full * (squares / samples + 1e-06)
    rho = jnp.broadcast_to(rho, (D, W))
    eye = lax.broadcasted_iota(jnp.int32, (8 * 2 * D, W), 0) == lax.broadcasted_iota(
        jnp.int32, (8 * 2 * D, W), 1
    )
    rhs_sum = []
    for k in range(4):
        rhs_sum.append([rhs_refs[0][k * T + t] + rhs_refs[1][k * T + t]
                        + rhs_refs[2][k * T + t] + rhs_refs[3][k * T + t] for t in range(T)])
    acc = [[jnp.zeros((D, W), jnp.float32) for _ in range(T)] for _ in range(4)]
    per = F * T // n
    for group in range(F * T // 8):
        diagonal = keep_ref[F * T, group : group + 1, :] + come_ref[F * T, group : group + 1, :]
        spread = jnp.sum(jnp.where(eye, jnp.broadcast_to(diagonal, eye.shape), 0.0), axis=1, keepdims=True)
        for i in range(8):
            ft = group * 8 + i
            f, t = ft // T, ft % T
            live = live_ref[ft : ft + 1, :]
            flux = column(flux_ref, f, D, W)
            p = p_refs[ft // per][ft % per]
            e = e_ref[ft]
            g = g_ref[ft]
            u = u_ref[ft]
            power = p * p
            power = power + swap(power)
            own = jnp.sum(flux * power, axis=0, keepdims=True)
            num = keep_ref[ft] + come_ref[ft] + live * own * flux * p
            num = counter_rotated(num, e)
            den = live * (spread[i * 2 * D : i * 2 * D + D] - flux * flux * power)
            smooth = coef_ref[first + f, 0] * rhs_sum[0][t]
            for k in range(1, 4):
                smooth = smooth + coef_ref[first + f, k] * rhs_sum[k][t]
            if last:
                u = u + g - smooth
            target = smooth - u
            fresh = (num + den * g + rho * target) / (den + rho)
            g = 0.5 * (g + fresh)
            total = u + g
            for k in range(4):
                acc[k][t] = acc[k][t] + basis_ref[first + f, k] * total
            if last:
                out_ref, total_ref, rhs_ref = refs
                out_ref[f, t, 0] = g[:, :O]
                out_ref[f, t, 1] = g[:, O:]
                total_ref[ft] = total
            else:
                g_out, rhs_ref = refs[:2]
                g_out[ft] = g
                refs[2 + ft // per][ft % per] = rotated(g, e)
    for k in range(4):
        for t in range(T):
            rhs_ref[k * T + t] = acc[k][t]


def final_kernel(dims, coef_ref, total_ref, *refs):
    F, T, D, O, R, C = dims
    rhs_refs, out_ref = refs[:4], refs[4]
    first = lax.axis_index("band") * F
    for t in range(T):
        rhs = [rhs_refs[0][k * T + t] + rhs_refs[1][k * T + t]
               + rhs_refs[2][k * T + t] + rhs_refs[3][k * T + t] for k in range(4)]
        for f in range(F):
            dual = total_ref[f * T + t]
            for k in range(4):
                dual = dual - coef_ref[first + f, k] * rhs[k]
            out_ref[f, t, 0] = dual[:, :O]
            out_ref[f, t, 1] = dual[:, O:]


def shards(sizes, vis, flags, positions, lmn, flux, gains, duals):
    R, C, Z = sizes
    F, T, _, D, O = gains.shape
    rows, cols = vis.shape[3], vis.shape[4]
    full = flags.shape[2]
    total_f = F * Z
    FT, W = F * T, 2 * O
    dims = (F, T, D, O, R, C)
    row = lax.axis_index("row")
    col = lax.axis_index("col")
    f32 = jnp.float32
    sds = jax.ShapeDtypeStruct
    smem = pl.BlockSpec(memory_space=pltpu.SMEM)
    vmem = pl.BlockSpec(memory_space=pltpu.VMEM)

    grid = 2.0 * np.arange(total_f, dtype=np.float64) / (total_f - 1) - 1.0
    basis = np.stack([grid**k for k in range(4)], axis=1)
    solved = basis @ np.linalg.inv(basis.T @ basis)
    basis_t = jnp.asarray(basis, f32)
    coef_t = jnp.asarray(solved, f32)
    freq_t = jnp.asarray(1.0 + np.arange(total_f) / total_f, f32)

    def where(r, c, z):
        return (r * C + c) * Z + z

    def permute(x, move):
        pairs = [
            (where(r, c, z), where(*move(r, c, z)))
            for r in range(R) for c in range(C) for z in range(Z)
        ]
        return lax.ppermute(x, AXES, pairs)

    def gather(x, m):
        return permute(x, lambda r, c, z: (((r * C + c) % R + m) % R, (r * C + c) // R, z))

    def bands(x):
        return [x] + [permute(x, lambda r, c, z, k=k: (r, c, (z + k) % Z)) for k in range(1, Z)]

    live_all = flags.astype(f32).reshape(FT, full)
    own_start = (row * C + col) * O
    live_own = lax.dynamic_slice_in_dim(live_all, own_start, O, 1)
    live_own = jnp.concatenate([live_own, live_own], axis=1)
    halves = [lax.dynamic_slice_in_dim(live_all, row * rows + (col % 2 + 2 * k) * O, O, 1) for k in range(2)]
    live_half = jnp.concatenate(halves, axis=1)
    live_row = lax.dynamic_slice_in_dim(live_all, row * rows, rows, 1)
    live_col = lax.dynamic_slice_in_dim(live_all, col * cols, cols, 1)

    part = sds((FT // CHUNKS, D, W), f32)
    whole = sds((FT, D, W), f32)
    rhs_shape = sds((4 * T, D, W), f32)
    flux_t = flux.T
    rot, g, *p = pl.pallas_call(
        functools.partial(start_kernel, dims),
        out_shape=[whole, whole] + [part] * CHUNKS,
        in_specs=[vmem, smem, smem, vmem],
        out_specs=[vmem] * (2 + CHUNKS),
        name="start",
    )(positions.transpose(1, 0, 2), lmn, freq_t, gains)
    u, rhs = pl.pallas_call(
        functools.partial(fit_kernel, dims),
        out_shape=[whole, rhs_shape],
        in_specs=[smem, vmem, vmem],
        out_specs=[vmem] * 2,
        name="fit",
    )(basis_t, duals, g)

    ids_p = row * rows + jnp.arange(rows, dtype=jnp.int32)
    ids_q = col * cols + jnp.arange(cols, dtype=jnp.int32)
    weight = (
        live_row.reshape(F, T, rows, 1) * live_col.reshape(F, T, 1, cols)
        * (ids_p[:, None] != ids_q[None, :]).astype(f32)
    )
    vis_re, vis_im = vis[:, :, 0].astype(f32), vis[:, :, 1].astype(f32)
    power = jnp.sum(weight * (vis_re * vis_re + vis_im * vis_im))
    counts = jnp.sum(live_all, axis=1)
    samples = jnp.sum(counts * counts - counts) / (R * C)

    group = 8 // T
    steps = F // CHUNKS // group
    lanes = lax.broadcasted_iota(jnp.int32, (1, W), 1)
    for step in range(ITERS):
        last = step == ITERS - 1
        got = [[gather(x, m) for m in range(R)] for x in p]
        theirs = [permute(x, lambda r, c, z: (r, c ^ 2, z)) for x in p]
        rhs_all = bands(rhs)
        keeps, comes = [], []
        for ch in range(CHUNKS):
            off = ch * steps
            pair = sds((steps * 9, 2 * D, W), f32)
            keep, send = pl.pallas_call(
                functools.partial(sum_kernel, dims, off),
                grid=(steps,),
                out_shape=[pair, pair],
                in_specs=[
                    smem,
                    pl.BlockSpec((8, cols), lambda i, off=off: (off + i, 0)),
                    pl.BlockSpec((group, T, 2, rows, cols), lambda i, off=off: (off + i, 0, 0, 0, 0)),
                ] + [pl.BlockSpec((8, D, W), lambda i: (i, 0, 0))] * R,
                out_specs=[pl.BlockSpec((9, 2 * D, W), lambda i: (i, 0, 0))] * 2,
                scratch_shapes=[pltpu.VMEM((rows, cols), jnp.bfloat16)],
                name="sums",
            )(flux_t, live_col, vis, *got[ch])
            keeps.append(keep)
            comes.append(permute(send, lambda r, c, z: (r, c ^ 1, z)))
        own_model = []
        for ch in range(CHUNKS):
            x = p[ch].reshape(F // CHUNKS, T, D, 2, O)
            fl = lax.dynamic_slice_in_dim(flux, ch * (F // CHUNKS), F // CHUNKS, 0)
            m = jnp.einsum("ftdco,fd->fto", x * x, fl, precision=HIGH)
            lv = live_own.reshape(F, T, 2 * O)[ch * (F // CHUNKS) : (ch + 1) * (F // CHUNKS), :, :O]
            own_model.append(jnp.sum(m * m * lv))
        extra = power - sum(own_model)
        extra = jnp.where(lanes == 0, extra, 0.0) + jnp.where(lanes == O, samples, 0.0)
        line = sds((FT + 1, D, W), f32)
        keep, send, scalar = pl.pallas_call(
            functools.partial(residual_kernel, dims),
            out_shape=[line, line, sds((R * C * Z, W), f32)],
            in_specs=[vmem] * (2 + 4 * CHUNKS),
            out_specs=[vmem] * 3,
            name="residual",
        )(live_half, extra, *keeps, *comes, *p, *theirs)
        come = permute(send, lambda r, c, z: (r, c ^ 2, z))
        scalar = lax.all_to_all(scalar, AXES, 0, 0, tiled=True)
        outs = (
            [sds(gains.shape, f32), whole, rhs_shape] if last
            else [whole, rhs_shape] + [part] * CHUNKS
        )
        result = pl.pallas_call(
            functools.partial(update_kernel, dims, last, float(full)),
            out_shape=outs,
            in_specs=[smem] * 3 + [vmem] * (7 + CHUNKS + 4),
            out_specs=[vmem] * len(outs),
            name="update",
        )(flux_t, basis_t, coef_t, keep, come, scalar, live_own, rot, g, u, *p, *rhs_all)
        if last:
            gain, total, rhs = result
        else:
            g, rhs, *p = result
    dual = pl.pallas_call(
        functools.partial(final_kernel, dims),
        out_shape=sds(gains.shape, f32),
        in_specs=[smem] + [vmem] * 5,
        out_specs=vmem,
        name="final",
    )(coef_t, total, *bands(rhs))
    return (gain, dual)


def basis(count):
    grid = 2.0 * jnp.arange(count, dtype=jnp.float32) / (count - 1) - 1.0
    return jnp.stack([grid**power for power in range(4)], axis=1)


def rotate(positions, lmn, freq):
    geometry = jnp.einsum("tks,kd->tds", positions, lmn, precision=HIGH)
    angle = 2.0 * math.pi * freq[:, None, None, None] * geometry[None]
    return (jnp.cos(angle), -jnp.sin(angle))


def complex_mul(a_re, a_im, b_re, b_im):
    return (a_re * b_re - a_im * b_im, a_re * b_im + a_im * b_re)


def solve_fit(rhs, total_f):
    full = basis(total_f)
    gram = jnp.dot(full.T, full, precision=HIGH)
    factor = jnp.linalg.cholesky(gram)
    flat = rhs.reshape(rhs.shape[0], -1)
    return jax.scipy.linalg.cho_solve((factor, True), flat).reshape(rhs.shape)


def plain_shards(vis, flags, positions, lmn, flux, gains, duals):
    width = gains.shape[0]
    total_f = width * lax.axis_size("band")
    first = lax.axis_index("band") * width
    local_basis = lax.dynamic_slice_in_dim(basis(total_f), first, width, 0)
    freq = 1.0 + (first + jnp.arange(width, dtype=jnp.int32)).astype(jnp.float32) / total_f
    row_index = lax.axis_index("row")
    col_index = lax.axis_index("col")
    row_count = vis.shape[3]
    col_count = vis.shape[4]
    owned = gains.shape[4]
    own_start = (row_index * lax.axis_size("col") + col_index) * owned
    row_start = row_index * row_count
    col_start = col_index * col_count
    own_cos, own_sin = rotate(lax.dynamic_slice_in_dim(positions, own_start, owned, 2), lmn, freq)
    row_cos, row_sin = rotate(
        lax.dynamic_slice_in_dim(positions, row_start, row_count, 2), lmn, freq
    )
    col_cos, col_sin = rotate(
        lax.dynamic_slice_in_dim(positions, col_start, col_count, 2), lmn, freq
    )
    all_live = flags.astype(jnp.float32)
    row_live = lax.dynamic_slice_in_dim(all_live, row_start, row_count, 2)
    col_live = lax.dynamic_slice_in_dim(all_live, col_start, col_count, 2)
    own_live = lax.dynamic_slice_in_dim(all_live, own_start, owned, 2)
    row_ids = row_start + jnp.arange(row_count, dtype=jnp.int32)
    col_ids = col_start + jnp.arange(col_count, dtype=jnp.int32)
    distinct = (row_ids[:, None] != col_ids[None, :]).astype(jnp.float32)
    weight = row_live[:, :, :, None] * col_live[:, :, None, :] * distinct
    vis_re = vis[:, :, 0].astype(jnp.float32)
    vis_im = vis[:, :, 1].astype(jnp.float32)
    scale = flux[:, None, :, None]

    def fit(gain, dual):
        rhs = jnp.einsum("fk,ftcds->ktcds", local_basis, gain + dual, precision=HIGH)
        return solve_fit(lax.psum(rhs, "band"), total_f)

    gain, dual = (gains, duals)
    coeffs = fit(gain, dual)
    for step in range(ITERS):
        target = jnp.einsum("fk,ktcds->ftcds", local_basis, coeffs, precision=HIGH) - dual
        every = lax.all_gather(gain, ("row", "col"), axis=4, tiled=True)
        row_gain = lax.dynamic_slice_in_dim(every, row_start, row_count, 4)
        col_gain = lax.dynamic_slice_in_dim(every, col_start, col_count, 4)
        row_re, row_im = complex_mul(row_gain[:, :, 0], row_gain[:, :, 1], row_cos, row_sin)
        col_re, col_im = complex_mul(col_gain[:, :, 0], col_gain[:, :, 1], col_cos, col_sin)
        col_re = scale * col_re
        col_im = scale * col_im
        model_re = jnp.einsum("ftdp,ftdq->ftpq", row_re, col_re, precision=HIGH) + jnp.einsum(
            "ftdp,ftdq->ftpq", row_im, col_im, precision=HIGH
        )
        model_im = jnp.einsum("ftdp,ftdq->ftpq", row_im, col_re, precision=HIGH) - jnp.einsum(
            "ftdp,ftdq->ftpq", row_re, col_im, precision=HIGH
        )
        resid_re = weight * (vis_re - model_re)
        resid_im = weight * (vis_im - model_im)
        squares, samples = lax.psum(
            (jnp.sum(resid_re * resid_re + resid_im * resid_im), jnp.sum(weight)),
            ("row", "col", "band"),
        )
        sum_re = jnp.einsum("ftpq,ftdq->ftdp", resid_re, col_re, precision=HIGH) - jnp.einsum(
            "ftpq,ftdq->ftdp", resid_im, col_im, precision=HIGH
        )
        sum_im = jnp.einsum("ftpq,ftdq->ftdp", resid_re, col_im, precision=HIGH) + jnp.einsum(
            "ftpq,ftdq->ftdp", resid_im, col_re, precision=HIGH
        )
        pairs = lax.psum_scatter(
            jnp.stack([sum_re, sum_im], axis=2), "col", scatter_dimension=4, tiled=True
        )
        every_mag = every[:, :, 0] * every[:, :, 0] + every[:, :, 1] * every[:, :, 1]
        total_mag = jnp.einsum("ftds,fts->ftd", every_mag, all_live, precision=HIGH)
        own_mag = gain[:, :, 0] * gain[:, :, 0] + gain[:, :, 1] * gain[:, :, 1]
        own_flag = own_live[:, :, None, :]
        own_denom = (scale * scale * own_flag * (total_mag[:, :, :, None] - own_flag * own_mag))[
            :, :, None
        ]
        num_re, num_im = complex_mul(own_cos, -own_sin, pairs[:, :, 0], pairs[:, :, 1])
        numer = jnp.stack([num_re, num_im], axis=2)
        rho = PENALTY * flags.shape[2] * (squares / samples + 1e-06)
        fresh = (numer + own_denom * gain + rho * target) / (own_denom + rho)
        gain = 0.5 * (gain + fresh)
        coeffs = fit(gain, dual)
        dual = dual + gain - jnp.einsum("fk,ktcds->ftcds", local_basis, coeffs, precision=HIGH)
    return (gain, dual)


def solution(mesh):
    sizes = tuple(mesh.shape[a] for a in AXES)

    def body(*args):
        vis, gains = args[0], args[5]
        if sizes[0] == 2 and sizes[1:] == (4, 4) and gains.shape[4] == 64 and gains.shape[3] == 8 and 8 % gains.shape[1] == 0:
            return shards(sizes, *args)
        return plain_shards(*args)

    return jax.shard_map(
        body,
        mesh=mesh,
        in_specs=(
            P("band", None, None, "row", "col"),
            P("band", None, None),
            P(),
            P(),
            P("band", None),
            P("band", None, None, None, ("row", "col")),
            P("band", None, None, None, ("row", "col")),
        ),
        out_specs=(
            P("band", None, None, None, ("row", "col")),
            P("band", None, None, None, ("row", "col")),
        ),
        check_vma=False,
    )
```

```python
import functools
import math

import jax
import jax.numpy as jnp
import numpy as np
from jax import lax
from jax.experimental import pallas as pl
from jax.experimental.pallas import tpu as pltpu
from jax.sharding import PartitionSpec as P

ITERS = 2
PENALTY = 0.05
HIGH = lax.Precision.HIGHEST
AXES = ("row", "col", "band")
LIMIT = pltpu.CompilerParams(vmem_limit_bytes=16 * 2**20)


def swap(x):
    half = x.shape[-1] // 2
    return pltpu.roll(x, half, x.ndim - 1)


def low_lanes(shape):
    return lax.broadcasted_iota(jnp.int32, shape, len(shape) - 1) < shape[-1] // 2


def join_low(a, b):
    return jnp.where(low_lanes(a.shape), a, swap(b))


def join_high(a, b):
    return jnp.where(low_lanes(a.shape), swap(a), b)


def column(ref, index, dirs, lanes):
    rows = lax.broadcasted_iota(jnp.int32, (dirs, lanes), 0)
    out = jnp.full((dirs, lanes), ref[0, index], jnp.float32)
    for d in range(1, dirs):
        out = jnp.where(rows == d, ref[d, index], out)
    return out


def cos_turns(r):
    t = 0.25 - jnp.abs(r)
    x = t * t
    coef = [(-1) ** n * (2.0 * math.pi) ** (2 * n + 1) / math.factorial(2 * n + 1) for n in range(7)]
    out = jnp.full_like(x, coef[-1])
    for c in coef[-2::-1]:
        out = out * x + c
    return out * t


def rotated(g, e):
    low = low_lanes(e.shape)
    turned = swap(e)
    cos2 = jnp.where(low, e, turned)
    sin2 = jnp.where(low, -turned, e)
    return g * cos2 + swap(g) * sin2


def counter_rotated(g, e):
    low = low_lanes(e.shape)
    turned = swap(e)
    cos2 = jnp.where(low, e, turned)
    sin2 = jnp.where(low, -turned, e)
    return g * cos2 - swap(g) * sin2


def start_kernel(dims, pos_ref, lmn_ref, freq_ref, gains_ref, e_ref, g_ref, p_ref):
    F, T, D, O, R, C = dims
    W = 2 * O
    own = lax.axis_index("row") * C + lax.axis_index("col")
    first = lax.axis_index("band") * F
    low = low_lanes((D, W))
    shape = pos_ref[:, :, :O].shape
    pos = jnp.zeros(shape, jnp.float32)
    for k in range(R * C):
        pos = jnp.where(own == k, pos_ref[:, :, k * O : (k + 1) * O], pos)
    pos = jnp.concatenate([pos, pos], axis=-1)
    geometry = []
    for t in range(T):
        total = jnp.zeros((D, W), jnp.float32)
        for k in range(3):
            rows = lax.broadcasted_iota(jnp.int32, (D, W), 0)
            lm = jnp.full((D, W), lmn_ref[k, 0], jnp.float32)
            for d in range(1, D):
                lm = jnp.where(rows == d, lmn_ref[k, d], lm)
            total = total + lm * pos[k, t : t + 1, :]
        geometry.append(total)
    shift = jnp.where(low, 0.0, 0.25)
    for f in range(F):
        nu = freq_ref[first + f]
        for t in range(T):
            ft = f * T + t
            turns = nu * geometry[t]
            r = turns - jnp.round(turns) + shift
            e = cos_turns(r - jnp.round(r))
            g = jnp.concatenate([gains_ref[f, t, 0], gains_ref[f, t, 1]], axis=-1)
            e_ref[ft] = e
            g_ref[ft] = g
            p_ref[ft] = rotated(g, e)


def own_terms(dims, flux_ref, live_ref, g_ref, held_ref, slope_ref):
    F, T, D, O, _, _ = dims
    total = jnp.zeros((1, 2 * O), jnp.float32)
    for f in range(F):
        flux = column(flux_ref, f, D, 2 * O)
        for t in range(T):
            ft = f * T + t
            live = live_ref[ft : ft + 1, :]
            g = g_ref[ft]
            power = g * g
            power = (power + swap(power)) * flux
            own = jnp.sum(power, axis=0, keepdims=True)
            total = total + live * own * own
            power = power * flux
            slope_ref[ft] = -live * power
            held_ref[ft] = live * (own * flux - power) * g
    return total


def fit_sums(dims, basis_ref, value, rhs_ref):
    F, T, D, O, _, _ = dims
    first = lax.axis_index("band") * F
    for t in range(T):
        acc = [jnp.zeros((D, 2 * O), jnp.float32) for _ in range(4)]
        for f in range(F):
            total = value(f, t)
            for k in range(4):
                acc[k] = acc[k] + basis_ref[first + f, k] * total
        for k in range(4):
            rhs_ref[k * T + t] = acc[k]


def pick(index, parts):
    out = parts[0]
    for k in range(1, len(parts)):
        out = jnp.where(index == k, parts[k], out)
    return out


def setup_kernel(dims, flux_ref, basis_ref, flags_ref, vis_ref, duals_ref, g_ref,
                 live_col_ref, live_half_ref, live_own_ref, u_ref, rhs_ref, held_ref, slope_ref,
                 power_ref, extra_ref, distinct):
    F, T, _, O, R, C = dims
    rows, cols = vis_ref.shape[3], vis_ref.shape[4]
    row = lax.axis_index("row")
    col = lax.axis_index("col")
    p = lax.broadcasted_iota(jnp.int32, (rows, cols), 0) + row * rows
    q = lax.broadcasted_iota(jnp.int32, (rows, cols), 1) + col * cols
    distinct[...] = jnp.where(p == q, 0.0, 1.0).astype(jnp.bfloat16)
    counts = jnp.zeros((T, 1), jnp.float32)
    for f in range(F):
        live = flags_ref[f].astype(jnp.float32)
        count = jnp.sum(live, axis=1, keepdims=True)
        counts = counts + count * (count - 1.0)
        at = slice(f * T, (f + 1) * T)
        mine = pick(row, [live[:, r * rows : (r + 1) * rows] for r in range(R)])
        blocks = [mine[:, c * O : (c + 1) * O] for c in range(C)]
        live_col_ref[at, :] = pick(col, [live[:, c * cols : (c + 1) * cols] for c in range(C)])
        even = jnp.concatenate([blocks[0], blocks[2]], axis=1)
        odd = jnp.concatenate([blocks[1], blocks[3]], axis=1)
        live_half_ref[at, :] = pick(col % 2, [even, odd])
        own = pick(col, blocks)
        live_own_ref[at, :] = jnp.concatenate([own, own], axis=1)
    samples = jnp.sum(counts) / (R * C)

    def channel(f, acc):
        live = flags_ref[f].astype(jnp.float32)
        mine = pick(row, [live[:, r * rows : (r + 1) * rows] for r in range(R)])
        pair = pick(col, [live[:, c * cols : (c + 1) * cols] for c in range(C)])
        upright = jnp.transpose(jnp.concatenate([mine] * (8 // T), axis=0))
        for t in range(T):
            weight = jnp.broadcast_to(upright[:, t : t + 1], (rows, cols)) * pair[t : t + 1, :]
            weight = weight.astype(jnp.bfloat16) * distinct[...]
            for part in range(2):
                seen = (vis_ref[f, t, part] * weight).astype(jnp.float32)
                acc = acc + jnp.sum((seen * seen).reshape(rows // 32, 32, cols), axis=0)
        return acc

    power = lax.fori_loop(0, F, channel, jnp.zeros((32, cols), jnp.float32))
    power = jnp.sum(power, axis=0, keepdims=True)
    low = low_lanes(power.shape)
    lanes = lax.broadcasted_iota(jnp.int32, power.shape, 1)
    row_power = jnp.where(low, power + swap(power), jnp.where(lanes == O, samples, 0.0))
    power_ref[...] = row_power
    for f in range(F):
        for t in range(T):
            u_ref[f * T + t] = jnp.concatenate([duals_ref[f, t, 0], duals_ref[f, t, 1]], axis=-1)
    fit_sums(dims, basis_ref, lambda f, t: u_ref[f * T + t] + g_ref[f * T + t], rhs_ref)
    own = own_terms(dims, flux_ref, live_own_ref, g_ref, held_ref, slope_ref)
    extra_ref[...] = row_power - jnp.where(low, own, 0.0)


def again_kernel(dims, flux_ref, basis_ref, power_ref, live_ref, u_ref, g_ref,
                 rhs_ref, held_ref, slope_ref, extra_ref):
    _, T, _, _, _, _ = dims
    fit_sums(dims, basis_ref, lambda f, t: u_ref[f * T + t] + g_ref[f * T + t], rhs_ref)
    own = own_terms(dims, flux_ref, live_ref, g_ref, held_ref, slope_ref)
    extra_ref[...] = power_ref[...] - jnp.where(low_lanes(own.shape), own, 0.0)


def target_kernel(dims, first_pass, coef_ref, u_ref, g_ref, *refs):
    F, T, _, _, _, _ = dims
    rhs_refs, outs = refs[:4], refs[4:]
    first = lax.axis_index("band") * F
    for t in range(T):
        rhs = [rhs_refs[0][k * T + t] + rhs_refs[1][k * T + t]
               + rhs_refs[2][k * T + t] + rhs_refs[3][k * T + t] for k in range(4)]
        for f in range(F):
            ft = f * T + t
            smooth = coef_ref[first + f, 0] * rhs[0]
            for k in range(1, 4):
                smooth = smooth + coef_ref[first + f, k] * rhs[k]
            u = u_ref[ft]
            if not first_pass:
                u = u + g_ref[ft] - smooth
                outs[1][ft] = u
            outs[0][ft] = smooth - u


def block_mask(size):
    shape = (8 * size, 8 * size)
    a = lax.broadcasted_iota(jnp.int32, shape, 0) // size
    b = lax.broadcasted_iota(jnp.int32, shape, 1) // size
    return a == b


def sum_kernel(dims, flux_ref, live_ref, vis_ref, a_ref, b_ref, keep_ref, send_ref, distinct):
    F, T, D, O, _, _ = dims
    rows, cols = vis_ref.shape[3], vis_ref.shape[4]
    row = lax.axis_index("row")
    col = lax.axis_index("col")
    parity = col % 2
    p = lax.broadcasted_iota(jnp.int32, (rows, cols), 0) + row * rows
    q = lax.broadcasted_iota(jnp.int32, (rows, cols), 1) + col * cols
    distinct[...] = jnp.where(p == q, 0.0, 1.0).astype(jnp.bfloat16)
    group = 8 // T
    blocks = block_mask(2 * D)
    nt = (((1,), (1,)), ((), ()))

    def body(step, carry):
        highs, lows = [], []
        lives = live_ref[pl.ds(step * 8, 8), :]
        for i in range(group):
            f = step * group + i
            scale = column(flux_ref, f, D, cols)
            for t in range(T):
                j = i * T + t
                ft = step * 8 + j
                a, b = a_ref[ft], b_ref[ft]
                first = jnp.where(row == 0, a, b)
                second = jnp.where(row == 0, b, a)
                weight = scale * lives[j : j + 1, :]
                re = join_low(first, second) * weight
                im = join_high(first, second) * weight
                x = jnp.concatenate(
                    [jnp.concatenate([re, -im], axis=1), jnp.concatenate([im, re], axis=1)], axis=0
                )
                high = x.astype(jnp.bfloat16)
                low = (x - high.astype(jnp.float32)).astype(jnp.bfloat16)
                highs.append(high)
                lows.append(low)
                both = jnp.concatenate([high, low], axis=0)
                mask = distinct[...]
                seen = jnp.concatenate([vis_ref[f, t, 0] * mask, vis_ref[f, t, 1] * mask], axis=1)
                v = lax.dot_general(both, seen, nt, preferred_element_type=jnp.float32)
                v = v[: 2 * D] + v[2 * D :]
                v0, v1 = v[:, : 2 * O], v[:, 2 * O :]
                even, odd = join_low(v0, v1), join_high(v0, v1)
                keep_ref[step * 9 + j] = jnp.where(parity == 0, even, odd)
                send_ref[step * 9 + j] = jnp.where(parity == 0, odd, even)
        high = jnp.concatenate(highs, axis=0)
        low = jnp.concatenate(lows, axis=0)
        gram = lax.dot_general(high, high, nt, preferred_element_type=jnp.float32)
        gram = gram + lax.dot_general(high, low, nt, preferred_element_type=jnp.float32)
        gram = gram + lax.dot_general(low, high, nt, preferred_element_type=jnp.float32)
        gram = jnp.where(blocks, gram, 0.0)
        folded = gram[: 2 * D]
        for i in range(1, 8):
            folded = folded + gram[i * 2 * D : (i + 1) * 2 * D]
        keep_ref[step * 9 + 8] = folded
        send_ref[step * 9 + 8] = folded
        return carry

    lax.fori_loop(0, F * T // 8, body, 0)


def residual_kernel(dims, live_ref, extra_ref, kept_ref, other_ref, mine_ref, theirs_ref,
                    keep_ref, send_ref, scalar_ref):
    F, T, D, O, _, _ = dims
    W = 2 * O
    near = (lax.axis_index("col") // 2) == 0
    mask = block_mask(2 * D)
    eye = lax.broadcasted_iota(jnp.int32, (2 * D, W), 0) == (
        lax.broadcasted_iota(jnp.int32, (2 * D, W), 1) % (2 * D)
    )
    total = jnp.zeros((2 * D, W), jnp.float32)
    for group in range(F * T // 8):
        gram = kept_ref[group * 9 + 8] + other_ref[group * 9 + 8]
        diagonal = jnp.sum(jnp.where(eye, gram, 0.0), axis=0, keepdims=True)
        keep_ref[F * T, group : group + 1, :] = diagonal
        send_ref[F * T, group : group + 1, :] = diagonal
        spread = jnp.where(mask, jnp.concatenate([gram] * 8, axis=0), 0.0)
        station = []
        for i in range(8):
            a, b = mine_ref[group * 8 + i], theirs_ref[group * 8 + i]
            first = jnp.where(near, a, b)
            second = jnp.where(near, b, a)
            station += [join_low(first, second), join_high(first, second)]
        model = jnp.dot(
            spread, jnp.concatenate(station, axis=0), precision=HIGH,
            preferred_element_type=jnp.float32,
        )
        for i in range(8):
            ft = group * 8 + i
            live = live_ref[ft : ft + 1, :]
            v = kept_ref[group * 9 + i] + other_ref[group * 9 + i]
            num = (v - model[i * 2 * D : (i + 1) * 2 * D]) * live
            z = jnp.concatenate(station[2 * i : 2 * i + 2], axis=0)
            total = total + z * (v * live + num)
            low, high = join_low(num[:D], num[D:]), join_high(num[:D], num[D:])
            keep_ref[ft] = jnp.where(near, low, high)
            send_ref[ft] = jnp.where(near, high, low)
    squares = -jnp.sum(total, axis=0, keepdims=True)
    squares = squares + swap(squares)
    scalar = jnp.where(low_lanes(squares.shape), squares, 0.0) + extra_ref[...]
    scalar_ref[...] = jnp.broadcast_to(scalar, scalar_ref.shape)


def update_kernel(dims, last, full, basis_ref, keep_ref, come_ref, scalar_ref, live_ref, e_ref,
                  g_ref, held_ref, slope_ref, target_ref, *refs):
    F, T, D, O, _, _ = dims
    first = lax.axis_index("band") * F
    W = 2 * O
    sums = jnp.sum(scalar_ref[...], axis=0, keepdims=True)
    low = low_lanes(sums.shape)
    squares = jnp.sum(jnp.where(low, sums, 0.0), axis=1, keepdims=True)
    samples = jnp.sum(jnp.where(low, 0.0, sums), axis=1, keepdims=True)
    squares = jnp.maximum(squares, 0.0)
    rho = PENALTY * full * (squares / samples + 1e-06)
    rho = jnp.broadcast_to(rho, (D, W))
    shape = (8 * D, W)
    a = lax.broadcasted_iota(jnp.int32, shape, 0)
    b = lax.broadcasted_iota(jnp.int32, shape, 1)
    eye = a // D * (2 * D) + a % D == b
    acc = [[jnp.zeros((D, W), jnp.float32) for _ in range(T)] for _ in range(4)]
    for group in range(F * T // 8):
        diagonal = keep_ref[F * T, group : group + 1, :] + come_ref[F * T, group : group + 1, :]
        spread = jnp.sum(jnp.where(eye, diagonal, 0.0), axis=1, keepdims=True)
        for i in range(8):
            ft = group * 8 + i
            f, t = ft // T, ft % T
            e = e_ref[ft]
            g = g_ref[ft]
            around = live_ref[ft : ft + 1, :] * spread[i * D : (i + 1) * D]
            num = counter_rotated(keep_ref[ft] + come_ref[ft], e) + held_ref[ft]
            fresh = (num + around * g + rho * target_ref[ft]) / (around + slope_ref[ft] + rho)
            g = 0.5 * (g + fresh)
            if last:
                u_ref, out_ref, total_ref, rhs_ref = refs
                out_ref[f, t, 0] = g[:, :O]
                out_ref[f, t, 1] = g[:, O:]
                total = u_ref[ft] + g
                total_ref[ft] = total
                for k in range(4):
                    acc[k][t] = acc[k][t] + basis_ref[first + f, k] * total
            else:
                g_out, p_out = refs
                g_out[ft] = g
                p_out[ft] = rotated(g, e)
    if last:
        for k in range(4):
            for t in range(T):
                rhs_ref[k * T + t] = acc[k][t]


def final_kernel(dims, coef_ref, total_ref, *refs):
    F, T, _, O, _, _ = dims
    rhs_refs, out_ref = refs[:4], refs[4]
    first = lax.axis_index("band") * F
    for t in range(T):
        rhs = [rhs_refs[0][k * T + t] + rhs_refs[1][k * T + t]
               + rhs_refs[2][k * T + t] + rhs_refs[3][k * T + t] for k in range(4)]
        for f in range(F):
            dual = total_ref[f * T + t]
            for k in range(4):
                dual = dual - coef_ref[first + f, k] * rhs[k]
            out_ref[f, t, 0] = dual[:, :O]
            out_ref[f, t, 1] = dual[:, O:]


def shards(sizes, vis, flags, positions, lmn, flux, gains, duals):
    R, C, Z = sizes
    F, T, _, D, O = gains.shape
    rows, cols = vis.shape[3], vis.shape[4]
    full = flags.shape[2]
    total_f = F * Z
    FT, W = F * T, 2 * O
    dims = (F, T, D, O, R, C)
    f32 = jnp.float32
    smem = pl.BlockSpec(memory_space=pltpu.SMEM)
    vmem = pl.BlockSpec(memory_space=pltpu.VMEM)

    def array(*shape):
        return jax.ShapeDtypeStruct(shape, f32)

    def call(kernel, outs, scalars, arrays, scratch=()):
        return pl.pallas_call(
            kernel,
            out_shape=outs,
            in_specs=[smem] * len(scalars) + [vmem] * len(arrays),
            out_specs=[vmem] * len(outs),
            scratch_shapes=list(scratch),
            compiler_params=LIMIT,
        )(*scalars, *arrays)

    grid = 2.0 * np.arange(total_f, dtype=np.float64) / (total_f - 1) - 1.0
    basis = np.stack([grid**k for k in range(4)], axis=1)
    solved = basis @ np.linalg.inv(basis.T @ basis)
    basis_t = jnp.asarray(basis, f32)
    coef_t = jnp.asarray(solved, f32)
    freq_t = jnp.asarray(1.0 + np.arange(total_f) / total_f, f32)

    def where(r, c, z):
        return (r * C + c) * Z + z

    def permute(x, move):
        pairs = [
            (where(r, c, z), where(*move(r, c, z)))
            for r in range(R) for c in range(C) for z in range(Z)
        ]
        return lax.ppermute(x, AXES, pairs)

    def gather(x, m):
        return permute(x, lambda r, c, z: (((r * C + c) % R + m) % R, (r * C + c) // R, z))

    def bands(x):
        return [x] + [permute(x, lambda r, c, z, k=k: (r, c, (z + k) % Z)) for k in range(1, Z)]

    whole, line, fit = array(FT, D, W), array(FT + 1, D, W), array(4 * T, D, W)
    pair, text, mask = array(FT // 8 * 9, 2 * D, W), array(1, W), pltpu.VMEM((rows, cols), jnp.bfloat16)
    flux_t = flux.T
    rot, g, p = pl.pallas_call(
        functools.partial(start_kernel, dims),
        out_shape=[whole] * 3,
        in_specs=[vmem, smem, smem, vmem],
        out_specs=[vmem] * 3,
        compiler_params=LIMIT,
        name="start",
    )(positions.transpose(1, 0, 2), lmn, freq_t, gains)
    for step in range(ITERS):
        last = step == ITERS - 1
        got = [gather(p, m) for m in range(R)]
        if step == 0:
            (live_col, live_half, live_own, u, rhs, held, slope, power, extra) = call(
                functools.partial(setup_kernel, dims),
                [array(FT, cols), array(FT, W), array(FT, W), whole, fit, whole, whole, text, text],
                [flux_t, basis_t], [flags, vis, duals, g], [mask],
            )
        else:
            rhs, held, slope, extra = call(
                functools.partial(again_kernel, dims),
                [fit, whole, whole, text], [flux_t, basis_t], [power, live_own, u, g],
            )
        rhs_all = bands(rhs)
        theirs = permute(p, lambda r, c, z: (r, c ^ 2, z))
        keep, send = call(
            functools.partial(sum_kernel, dims), [pair, pair], [flux_t],
            [live_col, vis, *got], [mask],
        )
        other = permute(send, lambda r, c, z: (r, c ^ 1, z))
        keep, send, scalar = call(
            functools.partial(residual_kernel, dims), [line, line, array(R * C * Z, W)],
            [], [live_half, extra, keep, other, p, theirs],
        )
        come = permute(send, lambda r, c, z: (r, c ^ 2, z))
        scalar = lax.all_to_all(scalar, AXES, 0, 0, tiled=True)
        target = call(
            functools.partial(target_kernel, dims, step == 0),
            [whole] * (1 if step == 0 else 2), [coef_t], [u, g, *rhs_all],
        )
        update = functools.partial(update_kernel, dims, last, float(full))
        arrays = [keep, come, scalar, live_own, rot, g, held, slope, target[0]]
        if last:
            gain, total, rhs = call(
                update, [array(*gains.shape), whole, fit], [basis_t], arrays + [target[1]]
            )
        else:
            g, p = call(update, [whole, whole], [basis_t], arrays)
    (dual,) = call(
        functools.partial(final_kernel, dims), [array(*gains.shape)], [coef_t],
        [total, *bands(rhs)],
    )
    return (gain, dual)


def basis(count):
    grid = 2.0 * jnp.arange(count, dtype=jnp.float32) / (count - 1) - 1.0
    return jnp.stack([grid**power for power in range(4)], axis=1)


def rotate(positions, lmn, freq):
    geometry = jnp.einsum("tks,kd->tds", positions, lmn, precision=HIGH)
    angle = 2.0 * math.pi * freq[:, None, None, None] * geometry[None]
    return (jnp.cos(angle), -jnp.sin(angle))


def complex_mul(a_re, a_im, b_re, b_im):
    return (a_re * b_re - a_im * b_im, a_re * b_im + a_im * b_re)


def solve_fit(rhs, total_f):
    full = basis(total_f)
    gram = jnp.dot(full.T, full, precision=HIGH)
    factor = jnp.linalg.cholesky(gram)
    flat = rhs.reshape(rhs.shape[0], -1)
    return jax.scipy.linalg.cho_solve((factor, True), flat).reshape(rhs.shape)


def plain_shards(vis, flags, positions, lmn, flux, gains, duals):
    width = gains.shape[0]
    total_f = width * lax.axis_size("band")
    first = lax.axis_index("band") * width
    local_basis = lax.dynamic_slice_in_dim(basis(total_f), first, width, 0)
    freq = 1.0 + (first + jnp.arange(width, dtype=jnp.int32)).astype(jnp.float32) / total_f
    row_index = lax.axis_index("row")
    col_index = lax.axis_index("col")
    row_count = vis.shape[3]
    col_count = vis.shape[4]
    owned = gains.shape[4]
    own_start = (row_index * lax.axis_size("col") + col_index) * owned
    row_start = row_index * row_count
    col_start = col_index * col_count
    own_cos, own_sin = rotate(lax.dynamic_slice_in_dim(positions, own_start, owned, 2), lmn, freq)
    row_cos, row_sin = rotate(
        lax.dynamic_slice_in_dim(positions, row_start, row_count, 2), lmn, freq
    )
    col_cos, col_sin = rotate(
        lax.dynamic_slice_in_dim(positions, col_start, col_count, 2), lmn, freq
    )
    all_live = flags.astype(jnp.float32)
    row_live = lax.dynamic_slice_in_dim(all_live, row_start, row_count, 2)
    col_live = lax.dynamic_slice_in_dim(all_live, col_start, col_count, 2)
    own_live = lax.dynamic_slice_in_dim(all_live, own_start, owned, 2)
    row_ids = row_start + jnp.arange(row_count, dtype=jnp.int32)
    col_ids = col_start + jnp.arange(col_count, dtype=jnp.int32)
    distinct = (row_ids[:, None] != col_ids[None, :]).astype(jnp.float32)
    weight = row_live[:, :, :, None] * col_live[:, :, None, :] * distinct
    vis_re = vis[:, :, 0].astype(jnp.float32)
    vis_im = vis[:, :, 1].astype(jnp.float32)
    scale = flux[:, None, :, None]

    def fit(gain, dual):
        rhs = jnp.einsum("fk,ftcds->ktcds", local_basis, gain + dual, precision=HIGH)
        return solve_fit(lax.psum(rhs, "band"), total_f)

    gain, dual = (gains, duals)
    coeffs = fit(gain, dual)
    for _ in range(ITERS):
        target = jnp.einsum("fk,ktcds->ftcds", local_basis, coeffs, precision=HIGH) - dual
        every = lax.all_gather(gain, ("row", "col"), axis=4, tiled=True)
        row_gain = lax.dynamic_slice_in_dim(every, row_start, row_count, 4)
        col_gain = lax.dynamic_slice_in_dim(every, col_start, col_count, 4)
        row_re, row_im = complex_mul(row_gain[:, :, 0], row_gain[:, :, 1], row_cos, row_sin)
        col_re, col_im = complex_mul(col_gain[:, :, 0], col_gain[:, :, 1], col_cos, col_sin)
        col_re = scale * col_re
        col_im = scale * col_im
        model_re = jnp.einsum("ftdp,ftdq->ftpq", row_re, col_re, precision=HIGH) + jnp.einsum(
            "ftdp,ftdq->ftpq", row_im, col_im, precision=HIGH
        )
        model_im = jnp.einsum("ftdp,ftdq->ftpq", row_im, col_re, precision=HIGH) - jnp.einsum(
            "ftdp,ftdq->ftpq", row_re, col_im, precision=HIGH
        )
        resid_re = weight * (vis_re - model_re)
        resid_im = weight * (vis_im - model_im)
        squares, samples = lax.psum(
            (jnp.sum(resid_re * resid_re + resid_im * resid_im), jnp.sum(weight)),
            ("row", "col", "band"),
        )
        sum_re = jnp.einsum("ftpq,ftdq->ftdp", resid_re, col_re, precision=HIGH) - jnp.einsum(
            "ftpq,ftdq->ftdp", resid_im, col_im, precision=HIGH
        )
        sum_im = jnp.einsum("ftpq,ftdq->ftdp", resid_re, col_im, precision=HIGH) + jnp.einsum(
            "ftpq,ftdq->ftdp", resid_im, col_re, precision=HIGH
        )
        pairs = lax.psum_scatter(
            jnp.stack([sum_re, sum_im], axis=2), "col", scatter_dimension=4, tiled=True
        )
        every_mag = every[:, :, 0] * every[:, :, 0] + every[:, :, 1] * every[:, :, 1]
        total_mag = jnp.einsum("ftds,fts->ftd", every_mag, all_live, precision=HIGH)
        own_mag = gain[:, :, 0] * gain[:, :, 0] + gain[:, :, 1] * gain[:, :, 1]
        own_flag = own_live[:, :, None, :]
        own_denom = (scale * scale * own_flag * (total_mag[:, :, :, None] - own_flag * own_mag))[
            :, :, None
        ]
        num_re, num_im = complex_mul(own_cos, -own_sin, pairs[:, :, 0], pairs[:, :, 1])
        numer = jnp.stack([num_re, num_im], axis=2)
        rho = PENALTY * flags.shape[2] * (squares / samples + 1e-06)
        fresh = (numer + own_denom * gain + rho * target) / (own_denom + rho)
        gain = 0.5 * (gain + fresh)
        coeffs = fit(gain, dual)
        dual = dual + gain - jnp.einsum("fk,ktcds->ftcds", local_basis, coeffs, precision=HIGH)
    return (gain, dual)


def solution(mesh):
    sizes = tuple(mesh.shape[a] for a in AXES)

    fits = sizes == (2, 4, 4)

    def body(*args):
        gains = args[5]
        if fits and gains.shape[3:] == (8, 64) and 8 % gains.shape[1] == 0:
            return shards(sizes, *args)
        return plain_shards(*args)

    return jax.shard_map(
        body,
        mesh=mesh,
        in_specs=(
            P("band", None, None, "row", "col"),
            P("band", None, None),
            P(),
            P(),
            P("band", None),
            P("band", None, None, None, ("row", "col")),
            P("band", None, None, None, ("row", "col")),
        ),
        out_specs=(
            P("band", None, None, None, ("row", "col")),
            P("band", None, None, None, ("row", "col")),
        ),
        check_vma=False,
    )
```

```python
import functools
import math

import jax
import jax.numpy as jnp
import numpy as np
from jax import lax
from jax.experimental import pallas as pl
from jax.experimental.pallas import tpu as pltpu
from jax.sharding import PartitionSpec as P

ITERS = 2
PENALTY = 0.05
HIGH = lax.Precision.HIGHEST
AXES = ("row", "col", "band")
LIMIT = pltpu.CompilerParams(vmem_limit_bytes=16 * 2**20)


def swap(x):
    half = x.shape[-1] // 2
    return pltpu.roll(x, half, x.ndim - 1)


def low_lanes(shape):
    return lax.broadcasted_iota(jnp.int32, shape, len(shape) - 1) < shape[-1] // 2


def join_low(a, b):
    return jnp.where(low_lanes(a.shape), a, swap(b))


def join_high(a, b):
    return jnp.where(low_lanes(a.shape), swap(a), b)


def column(ref, index, dirs, lanes):
    rows = lax.broadcasted_iota(jnp.int32, (dirs, lanes), 0)
    out = jnp.full((dirs, lanes), ref[0, index], jnp.float32)
    for d in range(1, dirs):
        out = jnp.where(rows == d, ref[d, index], out)
    return out


def cos_turns(r):
    t = 0.25 - jnp.abs(r)
    x = t * t
    coef = [(-1) ** n * (2.0 * math.pi) ** (2 * n + 1) / math.factorial(2 * n + 1) for n in range(7)]
    out = jnp.full_like(x, coef[-1])
    for c in coef[-2::-1]:
        out = out * x + c
    return out * t


def rotated(g, e):
    low = low_lanes(e.shape)
    turned = swap(e)
    cos2 = jnp.where(low, e, turned)
    sin2 = jnp.where(low, -turned, e)
    return g * cos2 + swap(g) * sin2


def counter_rotated(g, e):
    low = low_lanes(e.shape)
    turned = swap(e)
    cos2 = jnp.where(low, e, turned)
    sin2 = jnp.where(low, -turned, e)
    return g * cos2 - swap(g) * sin2


def start_kernel(dims, pos_hbm, lmn_hbm, gains_hbm, e_ref, g_ref, p_ref, pos_ref, lmn_ref, gains_ref, sems):
    F, T, D, O, R, C = dims
    W = 2 * O
    copies = [
        pltpu.make_async_copy(pos_hbm, pos_ref, sems.at[0]),
        pltpu.make_async_copy(lmn_hbm, lmn_ref, sems.at[1]),
        pltpu.make_async_copy(gains_hbm, gains_ref, sems.at[2]),
    ]
    for copy in copies:
        copy.start()
    own = lax.axis_index("row") * C + lax.axis_index("col")
    first = lax.axis_index("band") * F
    low = low_lanes((D, W))
    rows = lax.broadcasted_iota(jnp.int32, (D, W), 0)
    shift = jnp.where(low, 0.0, 0.25)
    copies[0].wait()
    copies[1].wait()
    pos = pos_ref[:, :, :O]
    for k in range(1, R * C):
        pos = jnp.where(own == k, pos_ref[:, :, k * O : (k + 1) * O], pos)
    pos = jnp.concatenate([pos, pos], axis=-1)
    geometry = []
    for t in range(T):
        total = jnp.zeros((D, W), jnp.float32)
        for k in range(3):
            lm = jnp.full((D, W), lmn_ref[k, 0], jnp.float32)
            for d in range(1, D):
                lm = jnp.where(rows == d, lmn_ref[k, d], lm)
            total = total + lm * pos[k, t : t + 1, :]
        geometry.append(total)
    copies[2].wait()
    total_f = F * lax.axis_size("band")
    for f in range(F):
        nu = 1.0 + (first + f).astype(jnp.float32) * (1.0 / total_f)
        for t in range(T):
            ft = f * T + t
            turns = nu * geometry[t]
            r = turns - jnp.round(turns) + shift
            e = cos_turns(r - jnp.round(r))
            g = jnp.concatenate([gains_ref[f, t, 0], gains_ref[f, t, 1]], axis=-1)
            e_ref[ft] = e
            g_ref[ft] = g
            p_ref[ft] = rotated(g, e)


def own_terms(dims, flux_ref, live_ref, g_ref, held_ref, slope_ref):
    F, T, D, O, _, _ = dims
    total = jnp.zeros((1, 2 * O), jnp.float32)
    for f in range(F):
        flux = column(flux_ref, f, D, 2 * O)
        for t in range(T):
            ft = f * T + t
            live = live_ref[ft : ft + 1, :]
            g = g_ref[ft]
            power = g * g
            power = (power + swap(power)) * flux
            own = jnp.sum(power, axis=0, keepdims=True)
            total = total + live * own * own
            power = power * flux
            slope_ref[ft] = -live * power
            held_ref[ft] = live * (own * flux - power) * g
    return total


def place(dims, f):
    F = dims[0]
    full = F * lax.axis_size("band")
    at = (lax.axis_index("band") * F + f).astype(jnp.float32)
    return at * (2.0 / (full - 1)) - 1.0


def fit_sums(dims, value, rhs_ref):
    F, T, D, O, _, _ = dims
    for t in range(T):
        acc = [jnp.zeros((D, 2 * O), jnp.float32) for _ in range(4)]
        for f in range(F):
            total = value(f, t)
            x = place(dims, f)
            for k in range(4):
                acc[k] = acc[k] + total
                total = total * x if k < 3 else total
        for k in range(4):
            rhs_ref[k * T + t] = acc[k]


def solve(dims, rhs_refs, t):
    T = dims[1]
    full = dims[0] * lax.axis_size("band")
    grid = 2.0 * np.arange(full, dtype=np.float64) / (full - 1) - 1.0
    basis = np.stack([grid**k for k in range(4)], axis=1)
    inverse = np.linalg.inv(basis.T @ basis)
    rhs = [sum(ref[k * T + t] for ref in rhs_refs) for k in range(4)]
    out = []
    for k in range(4):
        total = float(inverse[k, 0]) * rhs[0]
        for j in range(1, 4):
            total = total + float(inverse[k, j]) * rhs[j]
        out.append(total)
    return out


def curve(coeffs, x):
    return coeffs[0] + x * (coeffs[1] + x * (coeffs[2] + x * coeffs[3]))


def pick(index, parts):
    out = parts[0]
    for k in range(1, len(parts)):
        out = jnp.where(index == k, parts[k], out)
    return out


def setup_kernel(dims, flux_ref, flags_hbm, vis_hbm, duals_hbm, g_ref,
                 live_col_ref, live_half_ref, live_own_ref, u_ref, rhs_ref, held_ref,
                 slope_ref, power_ref, extra_ref, vis_ref, flags_ref, duals_ref, sems):
    F, T, _, O, R, C = dims
    rows, cols = vis_ref.shape[3], vis_ref.shape[4]
    row = lax.axis_index("row")
    col = lax.axis_index("col")
    flags_copy = pltpu.make_async_copy(flags_hbm, flags_ref, sems.at[F])
    duals_copy = pltpu.make_async_copy(duals_hbm, duals_ref, sems.at[F + 1])
    flags_copy.start()
    duals_copy.start()

    def vis_copy(f):
        return pltpu.make_async_copy(vis_hbm.at[f], vis_ref.at[f], sems.at[f])

    for f in range(F):
        vis_copy(f).start()
    flags_copy.wait()
    counts = jnp.zeros((T, full_lanes(flags_ref)), jnp.float32)
    for f in range(F):
        live = flags_ref[f].astype(jnp.float32)
        at = slice(f * T, (f + 1) * T)
        mine = pick(row, [live[:, r * rows : (r + 1) * rows] for r in range(R)])
        blocks = [mine[:, c * O : (c + 1) * O] for c in range(C)]
        live_col_ref[at, :] = pick(col, [live[:, c * cols : (c + 1) * cols] for c in range(C)])
        even = jnp.concatenate([blocks[0], blocks[2]], axis=1)
        odd = jnp.concatenate([blocks[1], blocks[3]], axis=1)
        live_half_ref[at, :] = pick(col % 2, [even, odd])
        own = pick(col, blocks)
        live_own_ref[at, :] = jnp.concatenate([own, own], axis=1)
        count = jnp.sum(live, axis=1, keepdims=True)
        counts = counts + live * (count - 1.0)
    samples = jnp.sum(counts) / (R * C)
    duals_copy.wait()
    for f in range(F):
        for t in range(T):
            u_ref[f * T + t] = jnp.concatenate([duals_ref[f, t, 0], duals_ref[f, t, 1]], axis=-1)
    fit_sums(dims, lambda f, t: u_ref[f * T + t] + g_ref[f * T + t], rhs_ref)
    own = own_terms(dims, flux_ref, live_own_ref, g_ref, held_ref, slope_ref)
    per = rows // cols
    p = lax.broadcasted_iota(jnp.int32, (cols, cols), 0)
    q = lax.broadcasted_iota(jnp.int32, (cols, cols), 1)
    distinct = jnp.where(p == q, 0.0, 1.0).astype(jnp.bfloat16)
    corner = pl.multiple_of((col % per) * cols, cols)

    def channel(f, acc):
        vis_copy(f).wait()

        @pl.when(col // per == row)
        def _():
            for t in range(T):
                for part in range(2):
                    at = vis_ref.at[f, t, part, pl.ds(corner, cols), :]
                    at[...] = at[...] * distinct

        live = flags_ref[f].astype(jnp.float32)
        mine = pick(row, [live[:, r * rows : (r + 1) * rows] for r in range(R)])
        pair = pick(col, [live[:, c * cols : (c + 1) * cols] for c in range(C)])
        upright = jnp.transpose(jnp.concatenate([mine] * (8 // T), axis=0))
        for t in range(T):
            weight = jnp.broadcast_to(upright[:, t : t + 1], (rows, cols)).astype(jnp.bfloat16)
            total = jnp.zeros((16, cols), jnp.float32)
            for part in range(2):
                seen = (vis_ref[f, t, part] * weight).astype(jnp.float32)
                total = total + jnp.sum((seen * seen).reshape(rows // 16, 16, cols), axis=0)
            acc = acc + total * pair[t : t + 1, :]
        return acc

    power = lax.fori_loop(0, F, channel, jnp.zeros((16, cols), jnp.float32))
    power = jnp.sum(power, axis=0, keepdims=True)
    low = low_lanes(power.shape)
    lanes = lax.broadcasted_iota(jnp.int32, power.shape, 1)
    row_power = jnp.where(low, power + swap(power), jnp.where(lanes == O, samples, 0.0))
    power_ref[...] = row_power
    extra_ref[...] = row_power - jnp.where(low, own, 0.0)


def full_lanes(ref):
    return ref.shape[-1]


def again_kernel(dims, flux_ref, power_ref, live_ref, u_ref, g_ref,
                 rhs_ref, held_ref, slope_ref, extra_ref):
    _, T, _, _, _, _ = dims
    fit_sums(dims, lambda f, t: u_ref[f * T + t] + g_ref[f * T + t], rhs_ref)
    own = own_terms(dims, flux_ref, live_ref, g_ref, held_ref, slope_ref)
    extra_ref[...] = power_ref[...] - jnp.where(low_lanes(own.shape), own, 0.0)


def target_kernel(dims, first_pass, u_ref, g_ref, *refs):
    F, T, _, _, _, _ = dims
    rhs_refs, outs = refs[:4], refs[4:]
    for t in range(T):
        coeffs = solve(dims, rhs_refs, t)
        for f in range(F):
            ft = f * T + t
            smooth = curve(coeffs, place(dims, f))
            u = u_ref[ft]
            if not first_pass:
                u = u + g_ref[ft] - smooth
                outs[1][ft] = u
            outs[0][ft] = smooth - u


def block_mask(size):
    shape = (8 * size, 8 * size)
    a = lax.broadcasted_iota(jnp.int32, shape, 0) // size
    b = lax.broadcasted_iota(jnp.int32, shape, 1) // size
    return a == b


def sum_kernel(dims, flux_ref, vis_hbm, live_ref, a_ref, b_ref, keep_ref, send_ref, vis_ref, distinct, sems):
    F, T, D, O, _, _ = dims
    rows, cols = vis_ref.shape[3], vis_ref.shape[4]
    row = lax.axis_index("row")
    col = lax.axis_index("col")
    parity = col % 2

    def vis_copy(f):
        return pltpu.make_async_copy(vis_hbm.at[f], vis_ref.at[f], sems.at[f])

    for f in range(F):
        vis_copy(f).start()
    p = lax.broadcasted_iota(jnp.int32, (rows, cols), 0) + row * rows
    q = lax.broadcasted_iota(jnp.int32, (rows, cols), 1) + col * cols
    distinct[...] = jnp.where(p == q, 0.0, 1.0).astype(jnp.bfloat16)
    group = 8 // T
    blocks = block_mask(2 * D)
    nt = (((1,), (1,)), ((), ()))

    def body(step, carry):
        highs, lows = [], []
        lives = live_ref[pl.ds(step * 8, 8), :]
        for i in range(group):
            f = step * group + i
            vis_copy(f).wait()
            scale = column(flux_ref, f, D, cols)
            for t in range(T):
                j = i * T + t
                ft = step * 8 + j
                a, b = a_ref[ft], b_ref[ft]
                first = jnp.where(row == 0, a, b)
                second = jnp.where(row == 0, b, a)
                weight = scale * lives[j : j + 1, :]
                re = join_low(first, second) * weight
                im = join_high(first, second) * weight
                x = jnp.concatenate(
                    [jnp.concatenate([re, -im], axis=1), jnp.concatenate([im, re], axis=1)], axis=0
                )
                high = x.astype(jnp.bfloat16)
                low = (x - high.astype(jnp.float32)).astype(jnp.bfloat16)
                highs.append(high)
                lows.append(low)
                both = jnp.concatenate([high, low], axis=0)
                mask = distinct[...]
                seen = jnp.concatenate([vis_ref[f, t, 0] * mask, vis_ref[f, t, 1] * mask], axis=1)
                v = lax.dot_general(both, seen, nt, preferred_element_type=jnp.float32)
                v = v[: 2 * D] + v[2 * D :]
                v0, v1 = v[:, : 2 * O], v[:, 2 * O :]
                even, odd = join_low(v0, v1), join_high(v0, v1)
                keep_ref[step * 9 + j] = jnp.where(parity == 0, even, odd)
                send_ref[step * 9 + j] = jnp.where(parity == 0, odd, even)
        high = jnp.concatenate(highs, axis=0)
        low = jnp.concatenate(lows, axis=0)
        gram = lax.dot_general(high, high, nt, preferred_element_type=jnp.float32)
        gram = gram + lax.dot_general(high, low, nt, preferred_element_type=jnp.float32)
        gram = gram + lax.dot_general(low, high, nt, preferred_element_type=jnp.float32)
        gram = jnp.where(blocks, gram, 0.0)
        folded = gram[: 2 * D]
        for i in range(1, 8):
            folded = folded + gram[i * 2 * D : (i + 1) * 2 * D]
        keep_ref[step * 9 + 8] = folded
        send_ref[step * 9 + 8] = folded
        return carry

    lax.fori_loop(0, F * T // 8, body, 0, unroll=2)


def residual_kernel(dims, live_ref, extra_ref, kept_ref, other_ref, mine_ref, theirs_ref,
                    keep_ref, send_ref, scalar_ref):
    F, T, D, O, _, _ = dims
    W = 2 * O
    near = (lax.axis_index("col") // 2) == 0
    mask = block_mask(2 * D)
    eye = lax.broadcasted_iota(jnp.int32, (2 * D, W), 0) == (
        lax.broadcasted_iota(jnp.int32, (2 * D, W), 1) % (2 * D)
    )
    total = jnp.zeros((2 * D, W), jnp.float32)
    for group in range(F * T // 8):
        gram = kept_ref[group * 9 + 8] + other_ref[group * 9 + 8]
        diagonal = jnp.sum(jnp.where(eye, gram, 0.0), axis=0, keepdims=True)
        keep_ref[F * T, group : group + 1, :] = diagonal
        send_ref[F * T, group : group + 1, :] = diagonal
        spread = jnp.where(mask, jnp.concatenate([gram] * 8, axis=0), 0.0)
        station = []
        for i in range(8):
            a, b = mine_ref[group * 8 + i], theirs_ref[group * 8 + i]
            first = jnp.where(near, a, b)
            second = jnp.where(near, b, a)
            station += [join_low(first, second), join_high(first, second)]
        model = jnp.dot(
            spread, jnp.concatenate(station, axis=0), precision=HIGH,
            preferred_element_type=jnp.float32,
        )
        for i in range(8):
            ft = group * 8 + i
            live = live_ref[ft : ft + 1, :]
            v = kept_ref[group * 9 + i] + other_ref[group * 9 + i]
            num = (v - model[i * 2 * D : (i + 1) * 2 * D]) * live
            z = jnp.concatenate(station[2 * i : 2 * i + 2], axis=0)
            total = total + z * (v * live + num)
            low, high = join_low(num[:D], num[D:]), join_high(num[:D], num[D:])
            keep_ref[ft] = jnp.where(near, low, high)
            send_ref[ft] = jnp.where(near, high, low)
    squares = -jnp.sum(total, axis=0, keepdims=True)
    squares = squares + swap(squares)
    scalar = jnp.where(low_lanes(squares.shape), squares, 0.0) + extra_ref[...]
    scalar_ref[...] = jnp.broadcast_to(scalar, scalar_ref.shape)


def merge_kernel(dims, keep_ref, come_ref, live_ref, e_ref, g_ref, held_ref, slope_ref,
                 num_ref, den_ref):
    F, T, D, O, _, _ = dims
    W = 2 * O
    shape = (8 * D, W)
    a = lax.broadcasted_iota(jnp.int32, shape, 0)
    b = lax.broadcasted_iota(jnp.int32, shape, 1)
    eye = a // D * (2 * D) + a % D == b
    ones = jnp.ones((W, W), jnp.float32)
    for group in range(F * T // 8):
        diagonal = keep_ref[F * T, group : group + 1, :] + come_ref[F * T, group : group + 1, :]
        spread = jnp.dot(
            jnp.where(eye, diagonal, 0.0), ones, precision=HIGH, preferred_element_type=jnp.float32
        )
        for i in range(8):
            ft = group * 8 + i
            around = live_ref[ft : ft + 1, :] * spread[i * D : (i + 1) * D]
            num = counter_rotated(keep_ref[ft] + come_ref[ft], e_ref[ft])
            num_ref[ft] = num + held_ref[ft] + around * g_ref[ft]
            den_ref[ft] = around + slope_ref[ft]


def update_kernel(dims, last, full, *refs):
    F, T, D, O, _, _ = dims
    scalar_ref, num_ref, den_ref, target_ref, g_ref, other_ref = refs[:6]
    W = 2 * O
    sums = jnp.sum(scalar_ref[...], axis=0, keepdims=True)
    low = low_lanes(sums.shape)
    squares = jnp.sum(jnp.where(low, sums, 0.0), axis=1, keepdims=True)
    samples = jnp.sum(jnp.where(low, 0.0, sums), axis=1, keepdims=True)
    squares = jnp.maximum(squares, 0.0)
    rho = PENALTY * full * (squares / samples + 1e-06)
    rho = jnp.broadcast_to(rho, (D, W))
    for t in range(T):
        acc = [jnp.zeros((D, W), jnp.float32) for _ in range(4)]
        for f in range(F):
            ft = f * T + t
            fresh = (num_ref[ft] + rho * target_ref[ft]) / (den_ref[ft] + rho)
            g = 0.5 * (g_ref[ft] + fresh)
            if last:
                out_ref, total_ref, rhs_ref = refs[6:]
                out_ref[f, t, 0] = g[:, :O]
                out_ref[f, t, 1] = g[:, O:]
                total = other_ref[ft] + g
                total_ref[ft] = total
                x = place(dims, f)
                for k in range(4):
                    acc[k] = acc[k] + total
                    total = total * x if k < 3 else total
            else:
                g_out, p_out = refs[6:]
                g_out[ft] = g
                p_out[ft] = rotated(g, other_ref[ft])
        if last:
            for k in range(4):
                rhs_ref[k * T + t] = acc[k]


def final_kernel(dims, total_ref, *refs):
    F, T, _, O, _, _ = dims
    rhs_refs, out_ref = refs[:-1], refs[-1]
    for t in range(T):
        coeffs = solve(dims, rhs_refs, t)
        for f in range(F):
            dual = total_ref[f * T + t] - curve(coeffs, place(dims, f))
            out_ref[f, t, 0] = dual[:, :O]
            out_ref[f, t, 1] = dual[:, O:]


def shards(sizes, vis, flags, positions, lmn, flux, gains, duals):
    R, C, Z = sizes
    F, T, _, D, O = gains.shape
    rows, cols = vis.shape[3], vis.shape[4]
    full = flags.shape[2]
    FT, W = F * T, 2 * O
    dims = (F, T, D, O, R, C)
    f32 = jnp.float32
    smem = pl.BlockSpec(memory_space=pltpu.SMEM)
    vmem = pl.BlockSpec(memory_space=pltpu.VMEM)
    hbm = pl.BlockSpec(memory_space=pltpu.HBM)

    def array(*shape):
        return jax.ShapeDtypeStruct(shape, f32)

    def far(x):
        return pltpu.with_memory_space_constraint(x, pltpu.HBM)

    def call(kernel, outs, scalars, arrays, scratch=()):
        return pl.pallas_call(
            kernel,
            out_shape=outs,
            in_specs=[smem] * len(scalars) + [vmem] * len(arrays),
            out_specs=[vmem] * len(outs),
            scratch_shapes=list(scratch),
            compiler_params=LIMIT,
        )(*scalars, *arrays)

    def where(r, c, z):
        return (r * C + c) * Z + z

    def permute(x, move):
        pairs = [
            (where(r, c, z), where(*move(r, c, z)))
            for r in range(R) for c in range(C) for z in range(Z)
        ]
        return lax.ppermute(x, AXES, pairs)

    def gather(x, m):
        return permute(x, lambda r, c, z: (((r * C + c) % R + m) % R, (r * C + c) // R, z))

    def bands(x):
        return [x] + [permute(x, lambda r, c, z, k=k: (r, c, (z + k) % Z)) for k in range(1, Z)]

    whole, line, fit = array(FT, D, W), array(FT + 1, D, W), array(4 * T, D, W)
    pair, text = array(FT // 8 * 9, 2 * D, W), array(1, W)
    flux_t = flux.T
    rot, g, p = pl.pallas_call(
        functools.partial(start_kernel, dims),
        out_shape=[whole] * 3,
        in_specs=[hbm] * 3,
        out_specs=[vmem] * 3,
        scratch_shapes=[
            pltpu.VMEM((3, T, full), f32),
            pltpu.SMEM(lmn.shape, f32),
            pltpu.VMEM(gains.shape, f32),
            pltpu.SemaphoreType.DMA((3,)),
        ],
        compiler_params=LIMIT,
        name="start",
    )(far(positions.transpose(1, 0, 2)), far(lmn), far(gains))
    for step in range(ITERS):
        last = step == ITERS - 1
        got = [gather(p, m) for m in range(R)]
        if step == 0:
            (live_col, live_half, live_own, u, rhs, held, slope, power, extra) = (
                pl.pallas_call(
                    functools.partial(setup_kernel, dims),
                    out_shape=[
                        array(FT, cols), array(FT, W), array(FT, W), whole, fit, whole, whole,
                        text, text,
                    ],
                    in_specs=[smem] + [hbm] * 3 + [vmem],
                    out_specs=[vmem] * 9,
                    scratch_shapes=[
                        pltpu.VMEM(vis.shape, vis.dtype),
                        pltpu.VMEM(flags.shape, flags.dtype),
                        pltpu.VMEM(duals.shape, f32),
                        pltpu.SemaphoreType.DMA((F + 2,)),
                    ],
                    compiler_params=LIMIT,
                    name="setup",
                )(flux_t, far(flags), far(vis), far(duals), g)
            )
        else:
            rhs, held, slope, extra = call(
                functools.partial(again_kernel, dims),
                [fit, whole, whole, text], [flux_t], [power, live_own, u, g],
            )
        rhs_all = bands(rhs)
        theirs = permute(p, lambda r, c, z: (r, c ^ 2, z))
        keep, send = pl.pallas_call(
            functools.partial(sum_kernel, dims),
            out_shape=[pair, pair],
            in_specs=[smem, hbm] + [vmem] * 3,
            out_specs=[vmem] * 2,
            scratch_shapes=[
                pltpu.VMEM(vis.shape, vis.dtype),
                pltpu.VMEM((rows, cols), vis.dtype),
                pltpu.SemaphoreType.DMA((F,)),
            ],
            compiler_params=LIMIT,
            name="sums",
        )(flux_t, far(vis), live_col, *got)
        other = permute(send, lambda r, c, z: (r, c ^ 1, z))
        keep, send, scalar = call(
            functools.partial(residual_kernel, dims), [line, line, array(R * C * Z, W)],
            [], [live_half, extra, keep, other, p, theirs],
        )
        come = permute(send, lambda r, c, z: (r, c ^ 2, z))
        scalar = lax.all_to_all(scalar, AXES, 0, 0, tiled=True)
        target = call(
            functools.partial(target_kernel, dims, step == 0),
            [whole] * (1 if step == 0 else 2), [], [u, g, *rhs_all],
        )
        num, den = call(
            functools.partial(merge_kernel, dims), [whole, whole], [],
            [keep, come, live_own, rot, g, held, slope],
        )
        update = functools.partial(update_kernel, dims, last, float(full))
        arrays = [scalar, num, den, target[0], g]
        if last:
            gain, total, rhs = call(
                update, [array(*gains.shape), whole, fit], [],
                arrays + [target[1]],
            )
        else:
            g, p = call(update, [whole, whole], [], arrays + [rot])
    (dual,) = call(
        functools.partial(final_kernel, dims), [array(*gains.shape)], [],
        [total, *bands(rhs)],
    )
    return (gain, dual)


def basis(count):
    grid = 2.0 * jnp.arange(count, dtype=jnp.float32) / (count - 1) - 1.0
    return jnp.stack([grid**power for power in range(4)], axis=1)


def rotate(positions, lmn, freq):
    geometry = jnp.einsum("tks,kd->tds", positions, lmn, precision=HIGH)
    angle = 2.0 * math.pi * freq[:, None, None, None] * geometry[None]
    return (jnp.cos(angle), -jnp.sin(angle))


def complex_mul(a_re, a_im, b_re, b_im):
    return (a_re * b_re - a_im * b_im, a_re * b_im + a_im * b_re)


def solve_fit(rhs, total_f):
    full = basis(total_f)
    gram = jnp.dot(full.T, full, precision=HIGH)
    factor = jnp.linalg.cholesky(gram)
    flat = rhs.reshape(rhs.shape[0], -1)
    return jax.scipy.linalg.cho_solve((factor, True), flat).reshape(rhs.shape)


def plain_shards(vis, flags, positions, lmn, flux, gains, duals):
    width = gains.shape[0]
    total_f = width * lax.axis_size("band")
    first = lax.axis_index("band") * width
    local_basis = lax.dynamic_slice_in_dim(basis(total_f), first, width, 0)
    freq = 1.0 + (first + jnp.arange(width, dtype=jnp.int32)).astype(jnp.float32) / total_f
    row_index = lax.axis_index("row")
    col_index = lax.axis_index("col")
    row_count = vis.shape[3]
    col_count = vis.shape[4]
    owned = gains.shape[4]
    own_start = (row_index * lax.axis_size("col") + col_index) * owned
    row_start = row_index * row_count
    col_start = col_index * col_count
    own_cos, own_sin = rotate(lax.dynamic_slice_in_dim(positions, own_start, owned, 2), lmn, freq)
    row_cos, row_sin = rotate(
        lax.dynamic_slice_in_dim(positions, row_start, row_count, 2), lmn, freq
    )
    col_cos, col_sin = rotate(
        lax.dynamic_slice_in_dim(positions, col_start, col_count, 2), lmn, freq
    )
    all_live = flags.astype(jnp.float32)
    row_live = lax.dynamic_slice_in_dim(all_live, row_start, row_count, 2)
    col_live = lax.dynamic_slice_in_dim(all_live, col_start, col_count, 2)
    own_live = lax.dynamic_slice_in_dim(all_live, own_start, owned, 2)
    row_ids = row_start + jnp.arange(row_count, dtype=jnp.int32)
    col_ids = col_start + jnp.arange(col_count, dtype=jnp.int32)
    distinct = (row_ids[:, None] != col_ids[None, :]).astype(jnp.float32)
    weight = row_live[:, :, :, None] * col_live[:, :, None, :] * distinct
    vis_re = vis[:, :, 0].astype(jnp.float32)
    vis_im = vis[:, :, 1].astype(jnp.float32)
    scale = flux[:, None, :, None]

    def fit(gain, dual):
        rhs = jnp.einsum("fk,ftcds->ktcds", local_basis, gain + dual, precision=HIGH)
        return solve_fit(lax.psum(rhs, "band"), total_f)

    gain, dual = (gains, duals)
    coeffs = fit(gain, dual)
    for _ in range(ITERS):
        target = jnp.einsum("fk,ktcds->ftcds", local_basis, coeffs, precision=HIGH) - dual
        every = lax.all_gather(gain, ("row", "col"), axis=4, tiled=True)
        row_gain = lax.dynamic_slice_in_dim(every, row_start, row_count, 4)
        col_gain = lax.dynamic_slice_in_dim(every, col_start, col_count, 4)
        row_re, row_im = complex_mul(row_gain[:, :, 0], row_gain[:, :, 1], row_cos, row_sin)
        col_re, col_im = complex_mul(col_gain[:, :, 0], col_gain[:, :, 1], col_cos, col_sin)
        col_re = scale * col_re
        col_im = scale * col_im
        model_re = jnp.einsum("ftdp,ftdq->ftpq", row_re, col_re, precision=HIGH) + jnp.einsum(
            "ftdp,ftdq->ftpq", row_im, col_im, precision=HIGH
        )
        model_im = jnp.einsum("ftdp,ftdq->ftpq", row_im, col_re, precision=HIGH) - jnp.einsum(
            "ftdp,ftdq->ftpq", row_re, col_im, precision=HIGH
        )
        resid_re = weight * (vis_re - model_re)
        resid_im = weight * (vis_im - model_im)
        squares, samples = lax.psum(
            (jnp.sum(resid_re * resid_re + resid_im * resid_im), jnp.sum(weight)),
            ("row", "col", "band"),
        )
        sum_re = jnp.einsum("ftpq,ftdq->ftdp", resid_re, col_re, precision=HIGH) - jnp.einsum(
            "ftpq,ftdq->ftdp", resid_im, col_im, precision=HIGH
        )
        sum_im = jnp.einsum("ftpq,ftdq->ftdp", resid_re, col_im, precision=HIGH) + jnp.einsum(
            "ftpq,ftdq->ftdp", resid_im, col_re, precision=HIGH
        )
        pairs = lax.psum_scatter(
            jnp.stack([sum_re, sum_im], axis=2), "col", scatter_dimension=4, tiled=True
        )
        every_mag = every[:, :, 0] * every[:, :, 0] + every[:, :, 1] * every[:, :, 1]
        total_mag = jnp.einsum("ftds,fts->ftd", every_mag, all_live, precision=HIGH)
        own_mag = gain[:, :, 0] * gain[:, :, 0] + gain[:, :, 1] * gain[:, :, 1]
        own_flag = own_live[:, :, None, :]
        own_denom = (scale * scale * own_flag * (total_mag[:, :, :, None] - own_flag * own_mag))[
            :, :, None
        ]
        num_re, num_im = complex_mul(own_cos, -own_sin, pairs[:, :, 0], pairs[:, :, 1])
        numer = jnp.stack([num_re, num_im], axis=2)
        rho = PENALTY * flags.shape[2] * (squares / samples + 1e-06)
        fresh = (numer + own_denom * gain + rho * target) / (own_denom + rho)
        gain = 0.5 * (gain + fresh)
        coeffs = fit(gain, dual)
        dual = dual + gain - jnp.einsum("fk,ktcds->ftcds", local_basis, coeffs, precision=HIGH)
    return (gain, dual)


def solution(mesh):
    sizes = tuple(mesh.shape[a] for a in AXES)

    fits = sizes == (2, 4, 4)

    def body(*args):
        gains = args[5]
        if fits and gains.shape[3:] == (8, 64) and 8 % gains.shape[1] == 0:
            return shards(sizes, *args)
        return plain_shards(*args)

    return jax.shard_map(
        body,
        mesh=mesh,
        in_specs=(
            P("band", None, None, "row", "col"),
            P("band", None, None),
            P(),
            P(),
            P("band", None),
            P("band", None, None, None, ("row", "col")),
            P("band", None, None, None, ("row", "col")),
        ),
        out_specs=(
            P("band", None, None, None, ("row", "col")),
            P("band", None, None, None, ("row", "col")),
        ),
        check_vma=False,
    )
```

```python
import functools
import math

import jax
import jax.numpy as jnp
import numpy as np
from jax import lax
from jax.experimental import pallas as pl
from jax.experimental.pallas import tpu as pltpu
from jax.sharding import PartitionSpec as P

ITERS = 2
PENALTY = 0.05
HIGH = lax.Precision.HIGHEST
AXES = ("row", "col", "band")
CHUNK = 4
LIMIT = pltpu.CompilerParams(vmem_limit_bytes=16 * 2**20)


def swap(x):
    half = x.shape[-1] // 2
    return pltpu.roll(x, half, x.ndim - 1)


def low_lanes(shape):
    return lax.broadcasted_iota(jnp.int32, shape, len(shape) - 1) < shape[-1] // 2


def join_low(a, b):
    return jnp.where(low_lanes(a.shape), a, swap(b))


def join_high(a, b):
    return jnp.where(low_lanes(a.shape), swap(a), b)


def column(ref, index, dirs, lanes):
    rows = lax.broadcasted_iota(jnp.int32, (dirs, lanes), 0)
    out = jnp.full((dirs, lanes), ref[0, index], jnp.float32)
    for d in range(1, dirs):
        out = jnp.where(rows == d, ref[d, index], out)
    return out


def cos_turns(r):
    t = 0.25 - jnp.abs(r)
    x = t * t
    coef = [(-1) ** n * (2.0 * math.pi) ** (2 * n + 1) / math.factorial(2 * n + 1) for n in range(7)]
    out = jnp.full_like(x, coef[-1])
    for c in coef[-2::-1]:
        out = out * x + c
    return out * t


def rotated(g, e):
    low = low_lanes(e.shape)
    turned = swap(e)
    cos2 = jnp.where(low, e, turned)
    sin2 = jnp.where(low, -turned, e)
    return g * cos2 + swap(g) * sin2


def counter_rotated(g, e):
    low = low_lanes(e.shape)
    turned = swap(e)
    cos2 = jnp.where(low, e, turned)
    sin2 = jnp.where(low, -turned, e)
    return g * cos2 - swap(g) * sin2


def start_kernel(dims, pos_hbm, lmn_hbm, gains_hbm, e_ref, g_ref, p_ref, pos_ref, lmn_ref, gains_ref, sems):
    F, T, D, O, R, C = dims
    W = 2 * O
    copies = [
        pltpu.make_async_copy(pos_hbm, pos_ref, sems.at[0]),
        pltpu.make_async_copy(lmn_hbm, lmn_ref, sems.at[1]),
        pltpu.make_async_copy(gains_hbm, gains_ref, sems.at[2]),
    ]
    for copy in copies:
        copy.start()
    own = lax.axis_index("row") * C + lax.axis_index("col")
    first = lax.axis_index("band") * F
    low = low_lanes((D, W))
    rows = lax.broadcasted_iota(jnp.int32, (D, W), 0)
    shift = jnp.where(low, 0.0, 0.25)
    copies[0].wait()
    copies[1].wait()
    pos = pos_ref[:, :, :O]
    for k in range(1, R * C):
        pos = jnp.where(own == k, pos_ref[:, :, k * O : (k + 1) * O], pos)
    pos = jnp.concatenate([pos, pos], axis=-1)
    geometry = []
    for t in range(T):
        total = jnp.zeros((D, W), jnp.float32)
        for k in range(3):
            lm = jnp.full((D, W), lmn_ref[k, 0], jnp.float32)
            for d in range(1, D):
                lm = jnp.where(rows == d, lmn_ref[k, d], lm)
            total = total + lm * pos[k, t : t + 1, :]
        geometry.append(total)
    total_f = F * lax.axis_size("band")
    for f in range(F):
        nu = 1.0 + (first + f).astype(jnp.float32) * (1.0 / total_f)
        for t in range(T):
            ft = f * T + t
            turns = nu * geometry[t]
            r = turns - jnp.round(turns) + shift
            e_ref[ft] = cos_turns(r - jnp.round(r))
    copies[2].wait()
    for f in range(F):
        for t in range(T):
            ft = f * T + t
            g = jnp.concatenate([gains_ref[f, t, 0], gains_ref[f, t, 1]], axis=-1)
            g_ref[ft] = g
            p_ref[ft] = rotated(g, e_ref[ft])


def own_terms(dims, flux_ref, live_ref, g_ref, held_ref, slope_ref):
    F, T, D, O, _, _ = dims
    total = jnp.zeros((1, 2 * O), jnp.float32)
    for f in range(F):
        flux = column(flux_ref, f, D, 2 * O)
        for t in range(T):
            ft = f * T + t
            live = live_ref[ft : ft + 1, :]
            g = g_ref[ft]
            power = g * g
            power = (power + swap(power)) * flux
            own = jnp.sum(power, axis=0, keepdims=True)
            total = total + live * own * own
            power = power * flux
            slope_ref[ft] = -live * power
            held_ref[ft] = live * (own * flux - power) * g
    return total


def place(dims, f):
    F = dims[0]
    full = F * lax.axis_size("band")
    at = (lax.axis_index("band") * F + f).astype(jnp.float32)
    return at * (2.0 / (full - 1)) - 1.0


def fit_sums(dims, value, rhs_ref):
    F, T, D, O, _, _ = dims
    for t in range(T):
        acc = [jnp.zeros((D, 2 * O), jnp.float32) for _ in range(4)]
        for f in range(F):
            total = value(f, t)
            x = place(dims, f)
            for k in range(4):
                acc[k] = acc[k] + total
                total = total * x if k < 3 else total
        for k in range(4):
            rhs_ref[k * T + t] = acc[k]


def solve(dims, rhs_refs, t):
    T = dims[1]
    full = dims[0] * lax.axis_size("band")
    grid = 2.0 * np.arange(full, dtype=np.float64) / (full - 1) - 1.0
    basis = np.stack([grid**k for k in range(4)], axis=1)
    inverse = np.linalg.inv(basis.T @ basis)
    rhs = [sum(ref[k * T + t] for ref in rhs_refs) for k in range(4)]
    out = []
    for k in range(4):
        total = float(inverse[k, 0]) * rhs[0]
        for j in range(1, 4):
            total = total + float(inverse[k, j]) * rhs[j]
        out.append(total)
    return out


def curve(coeffs, x):
    return coeffs[0] + x * (coeffs[1] + x * (coeffs[2] + x * coeffs[3]))


def pick(index, parts):
    out = parts[0]
    for k in range(1, len(parts)):
        out = jnp.where(index == k, parts[k], out)
    return out


def setup_kernel(dims, cols, flux_hbm, flags_hbm, duals_hbm, g_ref, live_col_ref, live_half_ref,
                 live_own_ref, upright_ref, u_ref, rhs_ref, held_ref, slope_ref, samples_ref,
                 extra_ref, flux_ref, flags_ref, duals_ref, sems):
    F, T, _, O, R, C = dims
    W, rows, full = 2 * O, C * O, flags_ref.shape[2]
    row = lax.axis_index("row")
    col = lax.axis_index("col")
    copies = [
        pltpu.make_async_copy(flags_hbm, flags_ref, sems.at[0]),
        pltpu.make_async_copy(duals_hbm, duals_ref, sems.at[1]),
        pltpu.make_async_copy(flux_hbm, flux_ref, sems.at[2]),
    ]
    for copy in copies:
        copy.start()
    copies[0].wait()
    counts = jnp.zeros((T, full), jnp.float32)
    stacked = []
    for f in range(F):
        live = flags_ref[f].astype(jnp.float32)
        at = slice(f * T, (f + 1) * T)
        mine = pick(row, [live[:, r * rows : (r + 1) * rows] for r in range(R)])
        blocks = [mine[:, c * O : (c + 1) * O] for c in range(C)]
        live_col_ref[at, :] = pick(col, [live[:, c * cols : (c + 1) * cols] for c in range(C)])
        even = jnp.concatenate([blocks[0], blocks[2]], axis=1)
        odd = jnp.concatenate([blocks[1], blocks[3]], axis=1)
        live_half_ref[at, :] = pick(col % 2, [even, odd])
        own = pick(col, blocks)
        live_own_ref[at, :] = jnp.concatenate([own, own], axis=1)
        stacked.append(mine)
        count = jnp.sum(live, axis=1, keepdims=True)
        counts = counts + live * (count - 1.0)
    stacked = jnp.concatenate(stacked + [jnp.zeros((W - F * T, rows), jnp.float32)], axis=0)
    upright_ref[...] = jnp.transpose(stacked)
    samples = jnp.sum(counts, axis=0, keepdims=True)
    samples = jnp.sum(samples, axis=1, keepdims=True) / (R * C)
    copies[1].wait()
    copies[2].wait()
    for f in range(F):
        for t in range(T):
            u_ref[f * T + t] = jnp.concatenate([duals_ref[f, t, 0], duals_ref[f, t, 1]], axis=-1)
    fit_sums(dims, lambda f, t: u_ref[f * T + t] + g_ref[f * T + t], rhs_ref)
    own = own_terms(dims, flux_ref, live_own_ref, g_ref, held_ref, slope_ref)
    lanes = lax.broadcasted_iota(jnp.int32, own.shape, 1)
    samples = jnp.where(lanes == O, samples, 0.0)
    samples_ref[...] = samples
    extra_ref[...] = samples - jnp.where(low_lanes(own.shape), own, 0.0)


def again_kernel(dims, flux_ref, samples_ref, live_ref, u_ref, g_ref,
                 rhs_ref, held_ref, slope_ref, extra_ref):
    _, T, _, _, _, _ = dims
    fit_sums(dims, lambda f, t: u_ref[f * T + t] + g_ref[f * T + t], rhs_ref)
    own = own_terms(dims, flux_ref, live_ref, g_ref, held_ref, slope_ref)
    extra_ref[...] = samples_ref[...] - jnp.where(low_lanes(own.shape), own, 0.0)


def add_kernel(a_ref, b_ref, out_ref):
    out_ref[...] = a_ref[...] + b_ref[...]


def target_kernel(dims, first_pass, u_ref, g_ref, *refs):
    F, T, _, _, _, _ = dims
    rhs_refs, outs = refs[:2], refs[2:]
    for t in range(T):
        coeffs = solve(dims, rhs_refs, t)
        for f in range(F):
            ft = f * T + t
            smooth = curve(coeffs, place(dims, f))
            u = u_ref[ft]
            if not first_pass:
                u = u + g_ref[ft] - smooth
                outs[1][ft] = u
            outs[0][ft] = smooth - u


def block_mask(size):
    shape = (8 * size, 8 * size)
    a = lax.broadcasted_iota(jnp.int32, shape, 0) // size
    b = lax.broadcasted_iota(jnp.int32, shape, 1) // size
    return a == b


def sum_kernel(dims, flux_hbm, vis_hbm, live_ref, a_ref, b_ref, *refs):
    F, T, D, O, _, _ = dims
    upright_ref, refs = (refs[0], refs[1:]) if len(refs) == 8 else (None, refs)
    keep_ref, send_ref, refs = refs[0], refs[1], refs[2:]
    power_ref, refs = (refs[0], refs[1:]) if upright_ref is not None else (None, refs)
    vis_ref, distinct, flux_ref, sems = refs
    rows, cols = vis_ref.shape[3], vis_ref.shape[4]
    row = lax.axis_index("row")
    col = lax.axis_index("col")
    parity = col % 2

    def vis_copy(f):
        return pltpu.make_async_copy(vis_hbm.at[f], vis_ref.at[f], sems.at[f])

    flux_copy = pltpu.make_async_copy(flux_hbm, flux_ref, sems.at[F])
    flux_copy.start()
    ahead = 2 * CHUNK
    for f in range(ahead):
        vis_copy(f).start()
    p = lax.broadcasted_iota(jnp.int32, (rows, cols), 0) + row * rows
    q = lax.broadcasted_iota(jnp.int32, (rows, cols), 1) + col * cols
    distinct[...] = jnp.where(p == q, 0.0, 1.0).astype(jnp.bfloat16)
    group = 8 // T
    blocks = block_mask(2 * D)
    nt = (((1,), (1,)), ((), ()))

    def body(step, upright, start, power):
        highs, lows = [], []
        lives = live_ref[pl.ds(step * 8, 8), :]
        mask = distinct[...]
        for i in range(group):
            f = step * group + i
            scale = column(flux_ref, f, D, cols)
            for t in range(T):
                j = i * T + t
                ft = step * 8 + j
                a, b = a_ref[ft], b_ref[ft]
                first = jnp.where(row == 0, a, b)
                second = jnp.where(row == 0, b, a)
                weight = scale * lives[j : j + 1, :]
                re = join_low(first, second) * weight
                im = join_high(first, second) * weight
                x = jnp.concatenate(
                    [jnp.concatenate([re, -im], axis=1), jnp.concatenate([im, re], axis=1)], axis=0
                )
                high = x.astype(jnp.bfloat16)
                low = (x - high.astype(jnp.float32)).astype(jnp.bfloat16)
                highs.append(high)
                lows.append(low)
                both = jnp.concatenate([high, low], axis=0)
                seen = [vis_ref[f, t, part] * mask for part in range(2)]
                v = lax.dot_general(
                    both, jnp.concatenate(seen, axis=1), nt, preferred_element_type=jnp.float32
                )
                v = v[: 2 * D] + v[2 * D :]
                v0, v1 = v[:, : 2 * O], v[:, 2 * O :]
                even, odd = join_low(v0, v1), join_high(v0, v1)
                keep_ref[step * 9 + j] = jnp.where(parity == 0, even, odd)
                send_ref[step * 9 + j] = jnp.where(parity == 0, odd, even)
                if upright is not None:
                    square = [x.astype(jnp.float32) for x in seen]
                    square = square[0] * square[0] + square[1] * square[1]
                    at = start + j
                    square = square * jnp.broadcast_to(upright[:, at : at + 1], square.shape)
                    square = jnp.sum(square.reshape(rows // 8, 8, cols), axis=0)
                    power = power + square * lives[j : j + 1, :]
        high = jnp.concatenate(highs, axis=0)
        low = jnp.concatenate(lows, axis=0)
        gram = lax.dot_general(high, high, nt, preferred_element_type=jnp.float32)
        gram = gram + lax.dot_general(high, low, nt, preferred_element_type=jnp.float32)
        gram = gram + lax.dot_general(low, high, nt, preferred_element_type=jnp.float32)
        gram = jnp.where(blocks, gram, 0.0)
        folded = gram[: 2 * D]
        for i in range(1, 8):
            folded = folded + gram[i * 2 * D : (i + 1) * 2 * D]
        keep_ref[step * 9 + 8] = folded
        send_ref[step * 9 + 8] = folded
        return power

    def chunk(c, power):
        for i in range(CHUNK):
            vis_copy(c * CHUNK + i).wait()

        @pl.when(c * CHUNK + ahead < F)
        def _():
            for i in range(CHUNK):
                vis_copy(c * CHUNK + ahead + i).start()

        upright = None
        if upright_ref is not None:
            upright = pltpu.roll(upright_ref[...], (2 * O - c * CHUNK * T) % (2 * O), 1)
        for j in range(CHUNK // group):
            power = body(c * (CHUNK // group) + j, upright, j * 8, power)
        return power

    flux_copy.wait()
    power = lax.fori_loop(0, F // CHUNK, chunk, jnp.zeros((8, cols), jnp.float32))
    if power_ref is not None:
        power = jnp.sum(power, axis=0, keepdims=True)
        power_ref[...] = jnp.where(low_lanes(power.shape), power + swap(power), 0.0)


def residual_kernel(dims, live_ref, extra_ref, power_ref, kept_ref, other_ref, mine_ref, theirs_ref,
                    keep_ref, send_ref, scalar_ref):
    F, T, D, O, _, _ = dims
    W = 2 * O
    near = (lax.axis_index("col") // 2) == 0
    mask = block_mask(2 * D)
    eye = lax.broadcasted_iota(jnp.int32, (2 * D, W), 0) == (
        lax.broadcasted_iota(jnp.int32, (2 * D, W), 1) % (2 * D)
    )
    total = jnp.zeros((2 * D, W), jnp.float32)
    for group in range(F * T // 8):
        gram = kept_ref[group * 9 + 8] + other_ref[group * 9 + 8]
        diagonal = jnp.sum(jnp.where(eye, gram, 0.0), axis=0, keepdims=True)
        keep_ref[F * T, group : group + 1, :] = diagonal
        send_ref[F * T, group : group + 1, :] = diagonal
        spread = jnp.where(mask, jnp.concatenate([gram] * 8, axis=0), 0.0)
        station = []
        for i in range(8):
            a, b = mine_ref[group * 8 + i], theirs_ref[group * 8 + i]
            first = jnp.where(near, a, b)
            second = jnp.where(near, b, a)
            station += [join_low(first, second), join_high(first, second)]
        model = jnp.dot(
            spread, jnp.concatenate(station, axis=0), precision=HIGH,
            preferred_element_type=jnp.float32,
        )
        for i in range(8):
            ft = group * 8 + i
            live = live_ref[ft : ft + 1, :]
            v = kept_ref[group * 9 + i] + other_ref[group * 9 + i]
            num = (v - model[i * 2 * D : (i + 1) * 2 * D]) * live
            z = jnp.concatenate(station[2 * i : 2 * i + 2], axis=0)
            total = total + z * (v * live + num)
            low, high = join_low(num[:D], num[D:]), join_high(num[:D], num[D:])
            keep_ref[ft] = jnp.where(near, low, high)
            send_ref[ft] = jnp.where(near, high, low)
    squares = -jnp.sum(total, axis=0, keepdims=True)
    squares = squares + swap(squares)
    scalar = jnp.where(low_lanes(squares.shape), squares, 0.0) + extra_ref[...] + power_ref[...]
    scalar_ref[...] = jnp.broadcast_to(scalar, scalar_ref.shape)


def merge_kernel(dims, keep_ref, come_ref, live_ref, e_ref, g_ref, held_ref, slope_ref,
                 num_ref, den_ref):
    F, T, D, O, _, _ = dims
    W = 2 * O
    shape = (8 * D, W)
    a = lax.broadcasted_iota(jnp.int32, shape, 0)
    b = lax.broadcasted_iota(jnp.int32, shape, 1)
    eye = a // D * (2 * D) + a % D == b
    ones = jnp.ones((W, W), jnp.float32)
    for group in range(F * T // 8):
        diagonal = keep_ref[F * T, group : group + 1, :] + come_ref[F * T, group : group + 1, :]
        spread = jnp.dot(
            jnp.where(eye, diagonal, 0.0), ones, precision=HIGH, preferred_element_type=jnp.float32
        )
        for i in range(8):
            ft = group * 8 + i
            around = live_ref[ft : ft + 1, :] * spread[i * D : (i + 1) * D]
            num = counter_rotated(keep_ref[ft] + come_ref[ft], e_ref[ft])
            num_ref[ft] = num + held_ref[ft] + around * g_ref[ft]
            den_ref[ft] = around + slope_ref[ft]


def update_kernel(dims, last, full, *refs):
    F, T, D, O, _, _ = dims
    scalar_ref, num_ref, den_ref, target_ref, g_ref, other_ref = refs[:6]
    W = 2 * O
    sums = jnp.sum(scalar_ref[...], axis=0, keepdims=True)
    low = low_lanes(sums.shape)
    squares = jnp.sum(jnp.where(low, sums, 0.0), axis=1, keepdims=True)
    samples = jnp.sum(jnp.where(low, 0.0, sums), axis=1, keepdims=True)
    squares = jnp.maximum(squares, 0.0)
    rho = PENALTY * full * (squares / samples + 1e-06)
    rho = jnp.broadcast_to(rho, (D, W))
    for t in range(T):
        acc = [jnp.zeros((D, W), jnp.float32) for _ in range(4)]
        for f in range(F):
            ft = f * T + t
            fresh = (num_ref[ft] + rho * target_ref[ft]) / (den_ref[ft] + rho)
            g = 0.5 * (g_ref[ft] + fresh)
            if last:
                out_ref, total_ref, rhs_ref = refs[6:]
                out_ref[f, t, 0] = g[:, :O]
                out_ref[f, t, 1] = g[:, O:]
                total = other_ref[ft] + g
                total_ref[ft] = total
                x = place(dims, f)
                for k in range(4):
                    acc[k] = acc[k] + total
                    total = total * x if k < 3 else total
            else:
                g_out, p_out = refs[6:]
                g_out[ft] = g
                p_out[ft] = rotated(g, other_ref[ft])
        if last:
            for k in range(4):
                rhs_ref[k * T + t] = acc[k]


def final_kernel(dims, total_ref, *refs):
    F, T, _, O, _, _ = dims
    rhs_refs, out_ref = refs[:-1], refs[-1]
    for t in range(T):
        coeffs = solve(dims, rhs_refs, t)
        for f in range(F):
            dual = total_ref[f * T + t] - curve(coeffs, place(dims, f))
            out_ref[f, t, 0] = dual[:, :O]
            out_ref[f, t, 1] = dual[:, O:]


def shards(sizes, vis, flags, positions, lmn, flux, gains, duals):
    R, C, Z = sizes
    F, T, _, D, O = gains.shape
    rows, cols = vis.shape[3], vis.shape[4]
    full = flags.shape[2]
    FT, W = F * T, 2 * O
    dims = (F, T, D, O, R, C)
    f32 = jnp.float32
    smem = pl.BlockSpec(memory_space=pltpu.SMEM)
    vmem = pl.BlockSpec(memory_space=pltpu.VMEM)
    hbm = pl.BlockSpec(memory_space=pltpu.HBM)

    def array(*shape):
        return jax.ShapeDtypeStruct(shape, f32)

    def far(x):
        return pltpu.with_memory_space_constraint(x, pltpu.HBM)

    def call(kernel, outs, scalars, arrays, scratch=()):
        return pl.pallas_call(
            kernel,
            out_shape=outs,
            in_specs=[smem] * len(scalars) + [vmem] * len(arrays),
            out_specs=[vmem] * len(outs),
            scratch_shapes=list(scratch),
            compiler_params=LIMIT,
        )(*scalars, *arrays)

    def where(r, c, z):
        return (r * C + c) * Z + z

    def permute(x, move):
        pairs = [
            (where(r, c, z), where(*move(r, c, z)))
            for r in range(R) for c in range(C) for z in range(Z)
        ]
        return lax.ppermute(x, AXES, pairs)

    def gather(x, m):
        return permute(x, lambda r, c, z: (((r * C + c) % R + m) % R, (r * C + c) // R, z))

    def bands(x):
        return [x] + [permute(x, lambda r, c, z, k=k: (r, c, (z + k) % Z)) for k in range(1, Z)]

    whole, line, fit = array(FT, D, W), array(FT + 1, D, W), array(4 * T, D, W)
    pair, text = array(FT // 8 * 9, 2 * D, W), array(1, W)
    flux_t = flux.T
    rot, g, p = pl.pallas_call(
        functools.partial(start_kernel, dims),
        out_shape=[whole] * 3,
        in_specs=[hbm] * 3,
        out_specs=[vmem] * 3,
        scratch_shapes=[
            pltpu.VMEM((3, T, full), f32),
            pltpu.SMEM(lmn.shape, f32),
            pltpu.VMEM(gains.shape, f32),
            pltpu.SemaphoreType.DMA((3,)),
        ],
        compiler_params=LIMIT,
        name="start",
    )(far(positions.transpose(1, 0, 2)), far(lmn), far(gains))
    for step in range(ITERS):
        last = step == ITERS - 1
        got = [gather(p, m) for m in range(R)]
        if step == 0:
            (live_col, live_half, live_own, upright, u, rhs, held, slope, samples, extra) = (
                pl.pallas_call(
                    functools.partial(setup_kernel, dims, cols),
                    out_shape=[
                        array(FT, cols), array(FT, W), array(FT, W), array(rows, W), whole,
                        fit, whole, whole, text, text,
                    ],
                    in_specs=[hbm] * 3 + [vmem],
                    out_specs=[vmem] * 10,
                    scratch_shapes=[
                        pltpu.SMEM(flux_t.shape, f32),
                        pltpu.VMEM(flags.shape, flags.dtype),
                        pltpu.VMEM(duals.shape, f32),
                        pltpu.SemaphoreType.DMA((3,)),
                    ],
                    compiler_params=LIMIT,
                    name="setup",
                )(far(flux_t), far(flags), far(duals), g)
            )
        else:
            rhs, held, slope, extra = call(
                functools.partial(again_kernel, dims),
                [fit, whole, whole, text], [flux_t], [samples, live_own, u, g],
            )
        rhs_near = permute(rhs, lambda r, c, z: (r, c, z ^ 1))
        theirs = permute(p, lambda r, c, z: (r, c ^ 2, z))
        more = [] if step else [upright]
        keep, send, *found = pl.pallas_call(
            functools.partial(sum_kernel, dims),
            out_shape=[pair, pair] + ([] if step else [array(1, cols)]),
            in_specs=[hbm] * 2 + [vmem] * (3 + len(more)),
            out_specs=[vmem] * (2 + len(more)),
            scratch_shapes=[
                pltpu.VMEM(vis.shape, vis.dtype),
                pltpu.VMEM((rows, cols), vis.dtype),
                pltpu.SMEM(flux_t.shape, f32),
                pltpu.SemaphoreType.DMA((F + 1,)),
            ],
            compiler_params=LIMIT,
            name="sums",
        )(far(flux_t), far(vis), live_col, *got, *more)
        power = power if step else found[0]
        other = permute(send, lambda r, c, z: (r, c ^ 1, z))
        (rhs,) = call(add_kernel, [fit], [], [rhs, rhs_near])
        rhs_far = permute(rhs, lambda r, c, z: (r, c, z ^ 2))
        keep, send, scalar = call(
            functools.partial(residual_kernel, dims), [line, line, array(R * C * Z, W)],
            [], [live_half, extra, power, keep, other, p, theirs],
        )
        come = permute(send, lambda r, c, z: (r, c ^ 2, z))
        scalar = lax.all_to_all(scalar, AXES, 0, 0, tiled=True)
        target = call(
            functools.partial(target_kernel, dims, step == 0),
            [whole] * (1 if step == 0 else 2), [], [u, g, rhs, rhs_far],
        )
        num, den = call(
            functools.partial(merge_kernel, dims), [whole, whole], [],
            [keep, come, live_own, rot, g, held, slope],
        )
        update = functools.partial(update_kernel, dims, last, float(full))
        arrays = [scalar, num, den, target[0], g]
        if last:
            gain, total, rhs = call(
                update, [array(*gains.shape), whole, fit], [],
                arrays + [target[1]],
            )
        else:
            g, p = call(update, [whole, whole], [], arrays + [rot])
    (dual,) = call(
        functools.partial(final_kernel, dims), [array(*gains.shape)], [],
        [total, *bands(rhs)],
    )
    return (gain, dual)


def basis(count):
    grid = 2.0 * jnp.arange(count, dtype=jnp.float32) / (count - 1) - 1.0
    return jnp.stack([grid**power for power in range(4)], axis=1)


def rotate(positions, lmn, freq):
    geometry = jnp.einsum("tks,kd->tds", positions, lmn, precision=HIGH)
    angle = 2.0 * math.pi * freq[:, None, None, None] * geometry[None]
    return (jnp.cos(angle), -jnp.sin(angle))


def complex_mul(a_re, a_im, b_re, b_im):
    return (a_re * b_re - a_im * b_im, a_re * b_im + a_im * b_re)


def solve_fit(rhs, total_f):
    full = basis(total_f)
    gram = jnp.dot(full.T, full, precision=HIGH)
    factor = jnp.linalg.cholesky(gram)
    flat = rhs.reshape(rhs.shape[0], -1)
    return jax.scipy.linalg.cho_solve((factor, True), flat).reshape(rhs.shape)


def plain_shards(vis, flags, positions, lmn, flux, gains, duals):
    width = gains.shape[0]
    total_f = width * lax.axis_size("band")
    first = lax.axis_index("band") * width
    local_basis = lax.dynamic_slice_in_dim(basis(total_f), first, width, 0)
    freq = 1.0 + (first + jnp.arange(width, dtype=jnp.int32)).astype(jnp.float32) / total_f
    row_index = lax.axis_index("row")
    col_index = lax.axis_index("col")
    row_count = vis.shape[3]
    col_count = vis.shape[4]
    owned = gains.shape[4]
    own_start = (row_index * lax.axis_size("col") + col_index) * owned
    row_start = row_index * row_count
    col_start = col_index * col_count
    own_cos, own_sin = rotate(lax.dynamic_slice_in_dim(positions, own_start, owned, 2), lmn, freq)
    row_cos, row_sin = rotate(
        lax.dynamic_slice_in_dim(positions, row_start, row_count, 2), lmn, freq
    )
    col_cos, col_sin = rotate(
        lax.dynamic_slice_in_dim(positions, col_start, col_count, 2), lmn, freq
    )
    all_live = flags.astype(jnp.float32)
    row_live = lax.dynamic_slice_in_dim(all_live, row_start, row_count, 2)
    col_live = lax.dynamic_slice_in_dim(all_live, col_start, col_count, 2)
    own_live = lax.dynamic_slice_in_dim(all_live, own_start, owned, 2)
    row_ids = row_start + jnp.arange(row_count, dtype=jnp.int32)
    col_ids = col_start + jnp.arange(col_count, dtype=jnp.int32)
    distinct = (row_ids[:, None] != col_ids[None, :]).astype(jnp.float32)
    weight = row_live[:, :, :, None] * col_live[:, :, None, :] * distinct
    vis_re = vis[:, :, 0].astype(jnp.float32)
    vis_im = vis[:, :, 1].astype(jnp.float32)
    scale = flux[:, None, :, None]

    def fit(gain, dual):
        rhs = jnp.einsum("fk,ftcds->ktcds", local_basis, gain + dual, precision=HIGH)
        return solve_fit(lax.psum(rhs, "band"), total_f)

    gain, dual = (gains, duals)
    coeffs = fit(gain, dual)
    for _ in range(ITERS):
        target = jnp.einsum("fk,ktcds->ftcds", local_basis, coeffs, precision=HIGH) - dual
        every = lax.all_gather(gain, ("row", "col"), axis=4, tiled=True)
        row_gain = lax.dynamic_slice_in_dim(every, row_start, row_count, 4)
        col_gain = lax.dynamic_slice_in_dim(every, col_start, col_count, 4)
        row_re, row_im = complex_mul(row_gain[:, :, 0], row_gain[:, :, 1], row_cos, row_sin)
        col_re, col_im = complex_mul(col_gain[:, :, 0], col_gain[:, :, 1], col_cos, col_sin)
        col_re = scale * col_re
        col_im = scale * col_im
        model_re = jnp.einsum("ftdp,ftdq->ftpq", row_re, col_re, precision=HIGH) + jnp.einsum(
            "ftdp,ftdq->ftpq", row_im, col_im, precision=HIGH
        )
        model_im = jnp.einsum("ftdp,ftdq->ftpq", row_im, col_re, precision=HIGH) - jnp.einsum(
            "ftdp,ftdq->ftpq", row_re, col_im, precision=HIGH
        )
        resid_re = weight * (vis_re - model_re)
        resid_im = weight * (vis_im - model_im)
        squares, samples = lax.psum(
            (jnp.sum(resid_re * resid_re + resid_im * resid_im), jnp.sum(weight)),
            ("row", "col", "band"),
        )
        sum_re = jnp.einsum("ftpq,ftdq->ftdp", resid_re, col_re, precision=HIGH) - jnp.einsum(
            "ftpq,ftdq->ftdp", resid_im, col_im, precision=HIGH
        )
        sum_im = jnp.einsum("ftpq,ftdq->ftdp", resid_re, col_im, precision=HIGH) + jnp.einsum(
            "ftpq,ftdq->ftdp", resid_im, col_re, precision=HIGH
        )
        pairs = lax.psum_scatter(
            jnp.stack([sum_re, sum_im], axis=2), "col", scatter_dimension=4, tiled=True
        )
        every_mag = every[:, :, 0] * every[:, :, 0] + every[:, :, 1] * every[:, :, 1]
        total_mag = jnp.einsum("ftds,fts->ftd", every_mag, all_live, precision=HIGH)
        own_mag = gain[:, :, 0] * gain[:, :, 0] + gain[:, :, 1] * gain[:, :, 1]
        own_flag = own_live[:, :, None, :]
        own_denom = (scale * scale * own_flag * (total_mag[:, :, :, None] - own_flag * own_mag))[
            :, :, None
        ]
        num_re, num_im = complex_mul(own_cos, -own_sin, pairs[:, :, 0], pairs[:, :, 1])
        numer = jnp.stack([num_re, num_im], axis=2)
        rho = PENALTY * flags.shape[2] * (squares / samples + 1e-06)
        fresh = (numer + own_denom * gain + rho * target) / (own_denom + rho)
        gain = 0.5 * (gain + fresh)
        coeffs = fit(gain, dual)
        dual = dual + gain - jnp.einsum("fk,ktcds->ftcds", local_basis, coeffs, precision=HIGH)
    return (gain, dual)


def solution(mesh):
    sizes = tuple(mesh.shape[a] for a in AXES)

    fits = sizes == (2, 4, 4)

    def body(*args):
        gains = args[5]
        if fits and gains.shape[3:] == (8, 64) and 8 % gains.shape[1] == 0:
            return shards(sizes, *args)
        return plain_shards(*args)

    return jax.shard_map(
        body,
        mesh=mesh,
        in_specs=(
            P("band", None, None, "row", "col"),
            P("band", None, None),
            P(),
            P(),
            P("band", None),
            P("band", None, None, None, ("row", "col")),
            P("band", None, None, None, ("row", "col")),
        ),
        out_specs=(
            P("band", None, None, None, ("row", "col")),
            P("band", None, None, None, ("row", "col")),
        ),
        check_vma=False,
    )
```

```python
import functools
import math

import jax
import jax.numpy as jnp
import numpy as np
from jax import lax
from jax.experimental import pallas as pl
from jax.experimental.pallas import tpu as pltpu
from jax.sharding import PartitionSpec as P

ITERS = 2
PENALTY = 0.05
HIGH = lax.Precision.HIGHEST
AXES = ("row", "col", "band")
CHUNK = 4
LIMIT = pltpu.CompilerParams(vmem_limit_bytes=16 * 2**20)


def swap(x):
    half = x.shape[-1] // 2
    return pltpu.roll(x, half, x.ndim - 1)


def low_lanes(shape):
    return lax.broadcasted_iota(jnp.int32, shape, len(shape) - 1) < shape[-1] // 2


def join_low(a, b):
    return jnp.where(low_lanes(a.shape), a, swap(b))


def join_high(a, b):
    return jnp.where(low_lanes(a.shape), swap(a), b)


def column(ref, index, dirs, lanes):
    rows = lax.broadcasted_iota(jnp.int32, (dirs, lanes), 0)
    out = jnp.full((dirs, lanes), ref[0, index], jnp.float32)
    for d in range(1, dirs):
        out = jnp.where(rows == d, ref[d, index], out)
    return out


def cos_turns(r):
    t = 0.25 - jnp.abs(r)
    x = t * t
    coef = [(-1) ** n * (2.0 * math.pi) ** (2 * n + 1) / math.factorial(2 * n + 1) for n in range(7)]
    out = jnp.full_like(x, coef[-1])
    for c in coef[-2::-1]:
        out = out * x + c
    return out * t


def rotated(g, e):
    low = low_lanes(e.shape)
    turned = swap(e)
    cos2 = jnp.where(low, e, turned)
    sin2 = jnp.where(low, -turned, e)
    return g * cos2 + swap(g) * sin2


def counter_rotated(g, e):
    low = low_lanes(e.shape)
    turned = swap(e)
    cos2 = jnp.where(low, e, turned)
    sin2 = jnp.where(low, -turned, e)
    return g * cos2 - swap(g) * sin2


def start_kernel(dims, pos_hbm, lmn_hbm, gains_hbm, e_ref, g_ref, p_ref, pos_ref, lmn_ref, gains_ref, sems):
    F, T, D, O, R, C = dims
    W = 2 * O
    copies = [
        pltpu.make_async_copy(pos_hbm, pos_ref, sems.at[0]),
        pltpu.make_async_copy(lmn_hbm, lmn_ref, sems.at[1]),
        pltpu.make_async_copy(gains_hbm, gains_ref, sems.at[2]),
    ]
    for copy in copies:
        copy.start()
    own = lax.axis_index("row") * C + lax.axis_index("col")
    first = lax.axis_index("band") * F
    low = low_lanes((D, W))
    rows = lax.broadcasted_iota(jnp.int32, (D, W), 0)
    shift = jnp.where(low, 0.0, 0.25)
    copies[0].wait()
    copies[1].wait()
    pos = pos_ref[:, :, :O]
    for k in range(1, R * C):
        pos = jnp.where(own == k, pos_ref[:, :, k * O : (k + 1) * O], pos)
    pos = jnp.concatenate([pos, pos], axis=-1)
    geometry = []
    for t in range(T):
        total = jnp.zeros((D, W), jnp.float32)
        for k in range(3):
            lm = jnp.full((D, W), lmn_ref[k, 0], jnp.float32)
            for d in range(1, D):
                lm = jnp.where(rows == d, lmn_ref[k, d], lm)
            total = total + lm * pos[k, t : t + 1, :]
        geometry.append(total)
    total_f = F * lax.axis_size("band")
    for f in range(F):
        nu = 1.0 + (first + f).astype(jnp.float32) * (1.0 / total_f)
        for t in range(T):
            ft = f * T + t
            turns = nu * geometry[t]
            r = turns - jnp.round(turns) + shift
            e_ref[ft] = cos_turns(r - jnp.round(r))
    copies[2].wait()
    for f in range(F):
        for t in range(T):
            ft = f * T + t
            g = jnp.concatenate([gains_ref[f, t, 0], gains_ref[f, t, 1]], axis=-1)
            g_ref[ft] = g
            p_ref[ft] = rotated(g, e_ref[ft])


def own_terms(dims, flux_ref, live_ref, g_ref, held_ref, slope_ref):
    F, T, D, O, _, _ = dims
    total = jnp.zeros((1, 2 * O), jnp.float32)
    for f in range(F):
        flux = column(flux_ref, f, D, 2 * O)
        for t in range(T):
            ft = f * T + t
            live = live_ref[ft : ft + 1, :]
            g = g_ref[ft]
            power = g * g
            power = (power + swap(power)) * flux
            own = jnp.sum(power, axis=0, keepdims=True)
            total = total + live * own * own
            power = power * flux
            slope_ref[ft] = -live * power
            held_ref[ft] = live * (own * flux - power) * g
    return total


def place(dims, f):
    F = dims[0]
    full = F * lax.axis_size("band")
    at = (lax.axis_index("band") * F + f).astype(jnp.float32)
    return at * (2.0 / (full - 1)) - 1.0


def fit_sums(dims, value, rhs_ref):
    F, T, D, O, _, _ = dims
    for t in range(T):
        acc = [jnp.zeros((D, 2 * O), jnp.float32) for _ in range(4)]
        for f in range(F):
            total = value(f, t)
            x = place(dims, f)
            for k in range(4):
                acc[k] = acc[k] + total
                total = total * x if k < 3 else total
        for k in range(4):
            rhs_ref[k * T + t] = acc[k]


def solve(dims, rhs_refs, t):
    T = dims[1]
    full = dims[0] * lax.axis_size("band")
    grid = 2.0 * np.arange(full, dtype=np.float64) / (full - 1) - 1.0
    basis = np.stack([grid**k for k in range(4)], axis=1)
    inverse = np.linalg.inv(basis.T @ basis)
    rhs = [sum(ref[k * T + t] for ref in rhs_refs) for k in range(4)]
    out = []
    for k in range(4):
        total = float(inverse[k, 0]) * rhs[0]
        for j in range(1, 4):
            total = total + float(inverse[k, j]) * rhs[j]
        out.append(total)
    return out


def curve(coeffs, x):
    return coeffs[0] + x * (coeffs[1] + x * (coeffs[2] + x * coeffs[3]))


def pick(index, parts):
    out = parts[0]
    for k in range(1, len(parts)):
        out = jnp.where(index == k, parts[k], out)
    return out


def setup_kernel(dims, cols, flux_hbm, flags_hbm, duals_hbm, g_ref, live_col_ref, live_half_ref,
                 live_own_ref, upright_ref, u_ref, rhs_ref, held_ref, slope_ref, samples_ref,
                 extra_ref, flux_ref, flags_ref, duals_ref, sems):
    F, T, _, O, R, C = dims
    W, rows, full = 2 * O, C * O, flags_ref.shape[2]
    row = lax.axis_index("row")
    col = lax.axis_index("col")
    copies = [
        pltpu.make_async_copy(flags_hbm, flags_ref, sems.at[0]),
        pltpu.make_async_copy(duals_hbm, duals_ref, sems.at[1]),
        pltpu.make_async_copy(flux_hbm, flux_ref, sems.at[2]),
    ]
    for copy in copies:
        copy.start()
    copies[0].wait()
    counts = jnp.zeros((T, full), jnp.float32)
    stacked = []
    for f in range(F):
        live = flags_ref[f].astype(jnp.float32)
        at = slice(f * T, (f + 1) * T)
        mine = pick(row, [live[:, r * rows : (r + 1) * rows] for r in range(R)])
        blocks = [mine[:, c * O : (c + 1) * O] for c in range(C)]
        live_col_ref[at, :] = pick(col, [live[:, c * cols : (c + 1) * cols] for c in range(C)])
        even = jnp.concatenate([blocks[0], blocks[2]], axis=1)
        odd = jnp.concatenate([blocks[1], blocks[3]], axis=1)
        live_half_ref[at, :] = pick(col % 2, [even, odd])
        own = pick(col, blocks)
        live_own_ref[at, :] = jnp.concatenate([own, own], axis=1)
        stacked.append(mine)
        count = jnp.sum(live, axis=1, keepdims=True)
        counts = counts + live * (count - 1.0)
    stacked = jnp.concatenate(stacked + [jnp.zeros((W - F * T, rows), jnp.float32)], axis=0)
    upright_ref[...] = jnp.transpose(stacked)
    samples = jnp.sum(counts, axis=0, keepdims=True)
    samples = jnp.sum(samples, axis=1, keepdims=True) / (R * C)
    copies[1].wait()
    copies[2].wait()
    for f in range(F):
        for t in range(T):
            u_ref[f * T + t] = jnp.concatenate([duals_ref[f, t, 0], duals_ref[f, t, 1]], axis=-1)
    fit_sums(dims, lambda f, t: u_ref[f * T + t] + g_ref[f * T + t], rhs_ref)
    own = own_terms(dims, flux_ref, live_own_ref, g_ref, held_ref, slope_ref)
    lanes = lax.broadcasted_iota(jnp.int32, own.shape, 1)
    samples = jnp.where(lanes == O, samples, 0.0)
    samples_ref[...] = samples
    extra_ref[...] = samples - jnp.where(low_lanes(own.shape), own, 0.0)


def again_kernel(dims, flux_ref, samples_ref, live_ref, u_ref, g_ref,
                 rhs_ref, held_ref, slope_ref, extra_ref):
    _, T, _, _, _, _ = dims
    fit_sums(dims, lambda f, t: u_ref[f * T + t] + g_ref[f * T + t], rhs_ref)
    own = own_terms(dims, flux_ref, live_ref, g_ref, held_ref, slope_ref)
    extra_ref[...] = samples_ref[...] - jnp.where(low_lanes(own.shape), own, 0.0)


def add_kernel(a_ref, b_ref, out_ref):
    out_ref[...] = a_ref[...] + b_ref[...]


def target_kernel(dims, first_pass, u_ref, g_ref, *refs):
    F, T, _, _, _, _ = dims
    rhs_refs, outs = refs[:2], refs[2:]
    for t in range(T):
        coeffs = solve(dims, rhs_refs, t)
        for f in range(F):
            ft = f * T + t
            smooth = curve(coeffs, place(dims, f))
            u = u_ref[ft]
            if not first_pass:
                u = u + g_ref[ft] - smooth
                outs[1][ft] = u
            outs[0][ft] = smooth - u


def block_mask(size):
    shape = (8 * size, 8 * size)
    a = lax.broadcasted_iota(jnp.int32, shape, 0) // size
    b = lax.broadcasted_iota(jnp.int32, shape, 1) // size
    return a == b


def sum_kernel(dims, flux_hbm, vis_hbm, live_ref, a_ref, b_ref, *refs):
    F, T, D, O, _, _ = dims
    upright_ref, refs = (refs[0], refs[1:]) if len(refs) == 8 else (None, refs)
    keep_ref, send_ref, refs = refs[0], refs[1], refs[2:]
    power_ref, refs = (refs[0], refs[1:]) if upright_ref is not None else (None, refs)
    vis_ref, distinct, flux_ref, sems = refs
    rows, cols = vis_ref.shape[3], vis_ref.shape[4]
    row = lax.axis_index("row")
    col = lax.axis_index("col")
    parity = col % 2

    def vis_copy(f):
        return pltpu.make_async_copy(vis_hbm.at[f], vis_ref.at[f], sems.at[f])

    flux_copy = pltpu.make_async_copy(flux_hbm, flux_ref, sems.at[F])
    flux_copy.start()
    ahead = 2 * CHUNK
    for f in range(ahead):
        vis_copy(f).start()
    p = lax.broadcasted_iota(jnp.int32, (rows, cols), 0) + row * rows
    q = lax.broadcasted_iota(jnp.int32, (rows, cols), 1) + col * cols
    distinct[...] = jnp.where(p == q, 0.0, 1.0).astype(jnp.bfloat16)
    group = 8 // T
    blocks = block_mask(2 * D)
    nt = (((1,), (1,)), ((), ()))

    def body(step, upright, start, power):
        highs, lows = [], []
        lives = live_ref[pl.ds(step * 8, 8), :]
        mask = distinct[...]
        for i in range(group):
            f = step * group + i
            scale = column(flux_ref, f, D, cols)
            for t in range(T):
                j = i * T + t
                ft = step * 8 + j
                a, b = a_ref[ft], b_ref[ft]
                first = jnp.where(row == 0, a, b)
                second = jnp.where(row == 0, b, a)
                weight = scale * lives[j : j + 1, :]
                re = join_low(first, second) * weight
                im = join_high(first, second) * weight
                x = jnp.concatenate(
                    [jnp.concatenate([re, -im], axis=1), jnp.concatenate([im, re], axis=1)], axis=0
                )
                high = x.astype(jnp.bfloat16)
                low = (x - high.astype(jnp.float32)).astype(jnp.bfloat16)
                highs.append(high)
                lows.append(low)
                both = jnp.concatenate([high, low], axis=0)
                seen = [vis_ref[f, t, part] * mask for part in range(2)]
                v = lax.dot_general(
                    both, jnp.concatenate(seen, axis=1), nt, preferred_element_type=jnp.float32
                )
                v = v[: 2 * D] + v[2 * D :]
                v0, v1 = v[:, : 2 * O], v[:, 2 * O :]
                even, odd = join_low(v0, v1), join_high(v0, v1)
                keep_ref[step * 9 + j] = jnp.where(parity == 0, even, odd)
                send_ref[step * 9 + j] = jnp.where(parity == 0, odd, even)
                if upright is not None:
                    square = [x.astype(jnp.float32) for x in seen]
                    square = square[0] * square[0] + square[1] * square[1]
                    at = start + j
                    square = square * jnp.broadcast_to(upright[:, at : at + 1], square.shape)
                    square = jnp.sum(square.reshape(rows // 8, 8, cols), axis=0)
                    power = power + square * lives[j : j + 1, :]
        high = jnp.concatenate(highs, axis=0)
        low = jnp.concatenate(lows, axis=0)
        gram = lax.dot_general(high, high, nt, preferred_element_type=jnp.float32)
        gram = gram + lax.dot_general(high, low, nt, preferred_element_type=jnp.float32)
        gram = gram + lax.dot_general(low, high, nt, preferred_element_type=jnp.float32)
        gram = jnp.where(blocks, gram, 0.0)
        folded = gram[: 2 * D]
        for i in range(1, 8):
            folded = folded + gram[i * 2 * D : (i + 1) * 2 * D]
        keep_ref[step * 9 + 8] = folded
        send_ref[step * 9 + 8] = folded
        return power

    def chunk(c, power):
        for i in range(CHUNK):
            vis_copy(c * CHUNK + i).wait()

        @pl.when(c * CHUNK + ahead < F)
        def _():
            for i in range(CHUNK):
                vis_copy(c * CHUNK + ahead + i).start()

        upright = None
        if upright_ref is not None:
            upright = pltpu.roll(upright_ref[...], (2 * O - c * CHUNK * T) % (2 * O), 1)
        for j in range(CHUNK // group):
            power = body(c * (CHUNK // group) + j, upright, j * 8, power)
        return power

    flux_copy.wait()
    power = lax.fori_loop(0, F // CHUNK, chunk, jnp.zeros((8, cols), jnp.float32))
    if power_ref is not None:
        power = jnp.sum(power, axis=0, keepdims=True)
        power_ref[...] = jnp.where(low_lanes(power.shape), power + swap(power), 0.0)


def residual_kernel(dims, live_ref, extra_ref, power_ref, kept_ref, other_ref, mine_ref, theirs_ref,
                    passed_ref, got_ref,
                    keep_ref, send_ref, scalar_ref):
    F, T, D, O, _, _ = dims
    W = 2 * O
    row = lax.axis_index("row")
    col = lax.axis_index("col")
    near = col // 2 == 0
    away = col // 2 != row
    held = col % 2 != row
    mask = block_mask(2 * D)
    eye = lax.broadcasted_iota(jnp.int32, (2 * D, W), 0) == (
        lax.broadcasted_iota(jnp.int32, (2 * D, W), 1) % (2 * D)
    )
    total = jnp.zeros((2 * D, W), jnp.float32)
    for group in range(F * T // 8):
        gram = kept_ref[group * 9 + 8] + other_ref[group * 9 + 8]
        diagonal = jnp.sum(jnp.where(eye, gram, 0.0), axis=0, keepdims=True)
        keep_ref[F * T, group : group + 1, :] = diagonal
        send_ref[F * T, group : group + 1, :] = diagonal
        spread = jnp.where(mask, jnp.concatenate([gram] * 8, axis=0), 0.0)
        station = []
        for i in range(8):
            ft = group * 8 + i
            a = mine_ref[ft]
            b = jnp.where(away, theirs_ref[ft], jnp.where(held, got_ref[ft], passed_ref[ft]))
            first = jnp.where(near, a, b)
            second = jnp.where(near, b, a)
            station += [join_low(first, second), join_high(first, second)]
        model = jnp.dot(
            spread, jnp.concatenate(station, axis=0), precision=HIGH,
            preferred_element_type=jnp.float32,
        )
        for i in range(8):
            ft = group * 8 + i
            live = live_ref[ft : ft + 1, :]
            v = kept_ref[group * 9 + i] + other_ref[group * 9 + i]
            num = (v - model[i * 2 * D : (i + 1) * 2 * D]) * live
            z = jnp.concatenate(station[2 * i : 2 * i + 2], axis=0)
            total = total + z * (v * live + num)
            low, high = join_low(num[:D], num[D:]), join_high(num[:D], num[D:])
            keep_ref[ft] = jnp.where(near, low, high)
            send_ref[ft] = jnp.where(near, high, low)
    squares = -jnp.sum(total, axis=0, keepdims=True)
    squares = squares + swap(squares)
    scalar = jnp.where(low_lanes(squares.shape), squares, 0.0) + extra_ref[...] + power_ref[...]
    scalar_ref[...] = jnp.broadcast_to(scalar, scalar_ref.shape)


def merge_kernel(dims, keep_ref, come_ref, live_ref, e_ref, g_ref, held_ref, slope_ref,
                 num_ref, den_ref):
    F, T, D, O, _, _ = dims
    W = 2 * O
    shape = (8 * D, W)
    a = lax.broadcasted_iota(jnp.int32, shape, 0)
    b = lax.broadcasted_iota(jnp.int32, shape, 1)
    eye = a // D * (2 * D) + a % D == b
    ones = jnp.ones((W, W), jnp.float32)
    for group in range(F * T // 8):
        diagonal = keep_ref[F * T, group : group + 1, :] + come_ref[F * T, group : group + 1, :]
        spread = jnp.dot(
            jnp.where(eye, diagonal, 0.0), ones, precision=HIGH, preferred_element_type=jnp.float32
        )
        for i in range(8):
            ft = group * 8 + i
            around = live_ref[ft : ft + 1, :] * spread[i * D : (i + 1) * D]
            num = counter_rotated(keep_ref[ft] + come_ref[ft], e_ref[ft])
            num_ref[ft] = num + held_ref[ft] + around * g_ref[ft]
            den_ref[ft] = around + slope_ref[ft]


def update_kernel(dims, last, full, *refs):
    F, T, D, O, _, _ = dims
    scalar_ref, num_ref, den_ref, target_ref, g_ref, other_ref = refs[:6]
    W = 2 * O
    sums = jnp.sum(scalar_ref[...], axis=0, keepdims=True)
    low = low_lanes(sums.shape)
    squares = jnp.sum(jnp.where(low, sums, 0.0), axis=1, keepdims=True)
    samples = jnp.sum(jnp.where(low, 0.0, sums), axis=1, keepdims=True)
    squares = jnp.maximum(squares, 0.0)
    rho = PENALTY * full * (squares / samples + 1e-06)
    rho = jnp.broadcast_to(rho, (D, W))
    for t in range(T):
        acc = [jnp.zeros((D, W), jnp.float32) for _ in range(4)]
        for f in range(F):
            ft = f * T + t
            fresh = (num_ref[ft] + rho * target_ref[ft]) / (den_ref[ft] + rho)
            g = 0.5 * (g_ref[ft] + fresh)
            if last:
                out_ref, total_ref, rhs_ref = refs[6:]
                out_ref[f, t, 0] = g[:, :O]
                out_ref[f, t, 1] = g[:, O:]
                total = other_ref[ft] + g
                total_ref[ft] = total
                x = place(dims, f)
                for k in range(4):
                    acc[k] = acc[k] + total
                    total = total * x if k < 3 else total
            else:
                g_out, p_out = refs[6:]
                g_out[ft] = g
                p_out[ft] = rotated(g, other_ref[ft])
        if last:
            for k in range(4):
                rhs_ref[k * T + t] = acc[k]


def final_kernel(dims, total_ref, *refs):
    F, T, _, O, _, _ = dims
    rhs_refs, out_ref = refs[:-1], refs[-1]
    for t in range(T):
        coeffs = solve(dims, rhs_refs, t)
        for f in range(F):
            dual = total_ref[f * T + t] - curve(coeffs, place(dims, f))
            out_ref[f, t, 0] = dual[:, :O]
            out_ref[f, t, 1] = dual[:, O:]


def shards(sizes, vis, flags, positions, lmn, flux, gains, duals):
    R, C, Z = sizes
    F, T, _, D, O = gains.shape
    rows, cols = vis.shape[3], vis.shape[4]
    full = flags.shape[2]
    FT, W = F * T, 2 * O
    dims = (F, T, D, O, R, C)
    f32 = jnp.float32
    smem = pl.BlockSpec(memory_space=pltpu.SMEM)
    vmem = pl.BlockSpec(memory_space=pltpu.VMEM)
    hbm = pl.BlockSpec(memory_space=pltpu.HBM)

    def array(*shape):
        return jax.ShapeDtypeStruct(shape, f32)

    def far(x):
        return pltpu.with_memory_space_constraint(x, pltpu.HBM)

    def call(kernel, outs, scalars, arrays, scratch=()):
        return pl.pallas_call(
            kernel,
            out_shape=outs,
            in_specs=[smem] * len(scalars) + [vmem] * len(arrays),
            out_specs=[vmem] * len(outs),
            scratch_shapes=list(scratch),
            compiler_params=LIMIT,
        )(*scalars, *arrays)

    def where(r, c, z):
        return (r * C + c) * Z + z

    def permute(x, move, some=lambda r, c: True):
        pairs = [
            (where(r, c, z), where(*move(r, c, z)))
            for r in range(R) for c in range(C) for z in range(Z) if some(r, c)
        ]
        return lax.ppermute(x, AXES, pairs)

    def gather(x, m):
        return permute(x, lambda r, c, z: (((r * C + c) % R + m) % R, (r * C + c) // R, z))

    def bands(x):
        return [x] + [permute(x, lambda r, c, z, k=k: (r, c, (z + k) % Z)) for k in range(1, Z)]

    whole, line, fit = array(FT, D, W), array(FT + 1, D, W), array(4 * T, D, W)
    pair, text = array(FT // 8 * 9, 2 * D, W), array(1, W)
    flux_t = flux.T
    rot, g, p = pl.pallas_call(
        functools.partial(start_kernel, dims),
        out_shape=[whole] * 3,
        in_specs=[hbm] * 3,
        out_specs=[vmem] * 3,
        scratch_shapes=[
            pltpu.VMEM((3, T, full), f32),
            pltpu.SMEM(lmn.shape, f32),
            pltpu.VMEM(gains.shape, f32),
            pltpu.SemaphoreType.DMA((3,)),
        ],
        compiler_params=LIMIT,
        name="start",
    )(far(positions.transpose(1, 0, 2)), far(lmn), far(gains))
    for step in range(ITERS):
        last = step == ITERS - 1
        got = [gather(p, m) for m in range(R)]
        if step == 0:
            (live_col, live_half, live_own, upright, u, rhs, held, slope, samples, extra) = (
                pl.pallas_call(
                    functools.partial(setup_kernel, dims, cols),
                    out_shape=[
                        array(FT, cols), array(FT, W), array(FT, W), array(rows, W), whole,
                        fit, whole, whole, text, text,
                    ],
                    in_specs=[hbm] * 3 + [vmem],
                    out_specs=[vmem] * 10,
                    scratch_shapes=[
                        pltpu.SMEM(flux_t.shape, f32),
                        pltpu.VMEM(flags.shape, flags.dtype),
                        pltpu.VMEM(duals.shape, f32),
                        pltpu.SemaphoreType.DMA((3,)),
                    ],
                    compiler_params=LIMIT,
                    name="setup",
                )(far(flux_t), far(flags), far(duals), g)
            )
        else:
            rhs, held, slope, extra = call(
                functools.partial(again_kernel, dims),
                [fit, whole, whole, text], [flux_t], [samples, live_own, u, g],
            )
        rhs_near = permute(rhs, lambda r, c, z: (r, c, z ^ 1))
        theirs = permute(p, lambda r, c, z: (r, c ^ 2, z), lambda r, c: r == c // 2)
        more = [] if step else [upright]
        keep, send, *found = pl.pallas_call(
            functools.partial(sum_kernel, dims),
            out_shape=[pair, pair] + ([] if step else [array(1, cols)]),
            in_specs=[hbm] * 2 + [vmem] * (3 + len(more)),
            out_specs=[vmem] * (2 + len(more)),
            scratch_shapes=[
                pltpu.VMEM(vis.shape, vis.dtype),
                pltpu.VMEM((rows, cols), vis.dtype),
                pltpu.SMEM(flux_t.shape, f32),
                pltpu.SemaphoreType.DMA((F + 1,)),
            ],
            compiler_params=LIMIT,
            name="sums",
        )(far(flux_t), far(vis), live_col, *got, *more)
        power = power if step else found[0]
        passed = permute(
            got[0], lambda r, c, z: (r, c ^ 1, z), lambda r, c: c == 3 * r + (1 - 2 * r)
        )
        other = permute(send, lambda r, c, z: (r, c ^ 1, z))
        (rhs,) = call(add_kernel, [fit], [], [rhs, rhs_near])
        rhs_far = permute(rhs, lambda r, c, z: (r, c, z ^ 2))
        keep, send, scalar = call(
            functools.partial(residual_kernel, dims), [line, line, array(R * C * Z, W)],
            [], [live_half, extra, power, keep, other, p, theirs, passed, got[1]],
        )
        come = permute(send, lambda r, c, z: (r, c ^ 2, z))
        scalar = lax.all_to_all(scalar, AXES, 0, 0, tiled=True)
        target = call(
            functools.partial(target_kernel, dims, step == 0),
            [whole] * (1 if step == 0 else 2), [], [u, g, rhs, rhs_far],
        )
        num, den = call(
            functools.partial(merge_kernel, dims), [whole, whole], [],
            [keep, come, live_own, rot, g, held, slope],
        )
        update = functools.partial(update_kernel, dims, last, float(full))
        arrays = [scalar, num, den, target[0], g]
        if last:
            gain, total, rhs = call(
                update, [array(*gains.shape), whole, fit], [],
                arrays + [target[1]],
            )
        else:
            g, p = call(update, [whole, whole], [], arrays + [rot])
    (dual,) = call(
        functools.partial(final_kernel, dims), [array(*gains.shape)], [],
        [total, *bands(rhs)],
    )
    return (gain, dual)


def basis(count):
    grid = 2.0 * jnp.arange(count, dtype=jnp.float32) / (count - 1) - 1.0
    return jnp.stack([grid**power for power in range(4)], axis=1)


def rotate(positions, lmn, freq):
    geometry = jnp.einsum("tks,kd->tds", positions, lmn, precision=HIGH)
    angle = 2.0 * math.pi * freq[:, None, None, None] * geometry[None]
    return (jnp.cos(angle), -jnp.sin(angle))


def complex_mul(a_re, a_im, b_re, b_im):
    return (a_re * b_re - a_im * b_im, a_re * b_im + a_im * b_re)


def solve_fit(rhs, total_f):
    full = basis(total_f)
    gram = jnp.dot(full.T, full, precision=HIGH)
    factor = jnp.linalg.cholesky(gram)
    flat = rhs.reshape(rhs.shape[0], -1)
    return jax.scipy.linalg.cho_solve((factor, True), flat).reshape(rhs.shape)


def plain_shards(vis, flags, positions, lmn, flux, gains, duals):
    width = gains.shape[0]
    total_f = width * lax.axis_size("band")
    first = lax.axis_index("band") * width
    local_basis = lax.dynamic_slice_in_dim(basis(total_f), first, width, 0)
    freq = 1.0 + (first + jnp.arange(width, dtype=jnp.int32)).astype(jnp.float32) / total_f
    row_index = lax.axis_index("row")
    col_index = lax.axis_index("col")
    row_count = vis.shape[3]
    col_count = vis.shape[4]
    owned = gains.shape[4]
    own_start = (row_index * lax.axis_size("col") + col_index) * owned
    row_start = row_index * row_count
    col_start = col_index * col_count
    own_cos, own_sin = rotate(lax.dynamic_slice_in_dim(positions, own_start, owned, 2), lmn, freq)
    row_cos, row_sin = rotate(
        lax.dynamic_slice_in_dim(positions, row_start, row_count, 2), lmn, freq
    )
    col_cos, col_sin = rotate(
        lax.dynamic_slice_in_dim(positions, col_start, col_count, 2), lmn, freq
    )
    all_live = flags.astype(jnp.float32)
    row_live = lax.dynamic_slice_in_dim(all_live, row_start, row_count, 2)
    col_live = lax.dynamic_slice_in_dim(all_live, col_start, col_count, 2)
    own_live = lax.dynamic_slice_in_dim(all_live, own_start, owned, 2)
    row_ids = row_start + jnp.arange(row_count, dtype=jnp.int32)
    col_ids = col_start + jnp.arange(col_count, dtype=jnp.int32)
    distinct = (row_ids[:, None] != col_ids[None, :]).astype(jnp.float32)
    weight = row_live[:, :, :, None] * col_live[:, :, None, :] * distinct
    vis_re = vis[:, :, 0].astype(jnp.float32)
    vis_im = vis[:, :, 1].astype(jnp.float32)
    scale = flux[:, None, :, None]

    def fit(gain, dual):
        rhs = jnp.einsum("fk,ftcds->ktcds", local_basis, gain + dual, precision=HIGH)
        return solve_fit(lax.psum(rhs, "band"), total_f)

    gain, dual = (gains, duals)
    coeffs = fit(gain, dual)
    for _ in range(ITERS):
        target = jnp.einsum("fk,ktcds->ftcds", local_basis, coeffs, precision=HIGH) - dual
        every = lax.all_gather(gain, ("row", "col"), axis=4, tiled=True)
        row_gain = lax.dynamic_slice_in_dim(every, row_start, row_count, 4)
        col_gain = lax.dynamic_slice_in_dim(every, col_start, col_count, 4)
        row_re, row_im = complex_mul(row_gain[:, :, 0], row_gain[:, :, 1], row_cos, row_sin)
        col_re, col_im = complex_mul(col_gain[:, :, 0], col_gain[:, :, 1], col_cos, col_sin)
        col_re = scale * col_re
        col_im = scale * col_im
        model_re = jnp.einsum("ftdp,ftdq->ftpq", row_re, col_re, precision=HIGH) + jnp.einsum(
            "ftdp,ftdq->ftpq", row_im, col_im, precision=HIGH
        )
        model_im = jnp.einsum("ftdp,ftdq->ftpq", row_im, col_re, precision=HIGH) - jnp.einsum(
            "ftdp,ftdq->ftpq", row_re, col_im, precision=HIGH
        )
        resid_re = weight * (vis_re - model_re)
        resid_im = weight * (vis_im - model_im)
        squares, samples = lax.psum(
            (jnp.sum(resid_re * resid_re + resid_im * resid_im), jnp.sum(weight)),
            ("row", "col", "band"),
        )
        sum_re = jnp.einsum("ftpq,ftdq->ftdp", resid_re, col_re, precision=HIGH) - jnp.einsum(
            "ftpq,ftdq->ftdp", resid_im, col_im, precision=HIGH
        )
        sum_im = jnp.einsum("ftpq,ftdq->ftdp", resid_re, col_im, precision=HIGH) + jnp.einsum(
            "ftpq,ftdq->ftdp", resid_im, col_re, precision=HIGH
        )
        pairs = lax.psum_scatter(
            jnp.stack([sum_re, sum_im], axis=2), "col", scatter_dimension=4, tiled=True
        )
        every_mag = every[:, :, 0] * every[:, :, 0] + every[:, :, 1] * every[:, :, 1]
        total_mag = jnp.einsum("ftds,fts->ftd", every_mag, all_live, precision=HIGH)
        own_mag = gain[:, :, 0] * gain[:, :, 0] + gain[:, :, 1] * gain[:, :, 1]
        own_flag = own_live[:, :, None, :]
        own_denom = (scale * scale * own_flag * (total_mag[:, :, :, None] - own_flag * own_mag))[
            :, :, None
        ]
        num_re, num_im = complex_mul(own_cos, -own_sin, pairs[:, :, 0], pairs[:, :, 1])
        numer = jnp.stack([num_re, num_im], axis=2)
        rho = PENALTY * flags.shape[2] * (squares / samples + 1e-06)
        fresh = (numer + own_denom * gain + rho * target) / (own_denom + rho)
        gain = 0.5 * (gain + fresh)
        coeffs = fit(gain, dual)
        dual = dual + gain - jnp.einsum("fk,ktcds->ftcds", local_basis, coeffs, precision=HIGH)
    return (gain, dual)


def solution(mesh):
    sizes = tuple(mesh.shape[a] for a in AXES)

    fits = sizes == (2, 4, 4)

    def body(*args):
        gains = args[5]
        if fits and gains.shape[3:] == (8, 64) and 8 % gains.shape[1] == 0:
            return shards(sizes, *args)
        return plain_shards(*args)

    return jax.shard_map(
        body,
        mesh=mesh,
        in_specs=(
            P("band", None, None, "row", "col"),
            P("band", None, None),
            P(),
            P(),
            P("band", None),
            P("band", None, None, None, ("row", "col")),
            P("band", None, None, None, ("row", "col")),
        ),
        out_specs=(
            P("band", None, None, None, ("row", "col")),
            P("band", None, None, None, ("row", "col")),
        ),
        check_vma=False,
    )
```

```python
import functools
import math

import jax
import jax.numpy as jnp
import numpy as np
from jax import lax
from jax.experimental import pallas as pl
from jax.experimental.pallas import tpu as pltpu
from jax.sharding import PartitionSpec as P

ITERS = 2
PENALTY = 0.05
HIGH = lax.Precision.HIGHEST
AXES = ("row", "col", "band")
CHUNK = 4
LIMIT = pltpu.CompilerParams(vmem_limit_bytes=16 * 2**20)


def swap(x):
    half = x.shape[-1] // 2
    return pltpu.roll(x, half, x.ndim - 1)


def low_lanes(shape):
    return lax.broadcasted_iota(jnp.int32, shape, len(shape) - 1) < shape[-1] // 2


def join_low(a, b):
    return jnp.where(low_lanes(a.shape), a, swap(b))


def join_high(a, b):
    return jnp.where(low_lanes(a.shape), swap(a), b)


def column(ref, index, dirs, lanes):
    rows = lax.broadcasted_iota(jnp.int32, (dirs, lanes), 0)
    out = jnp.full((dirs, lanes), ref[0, index], jnp.float32)
    for d in range(1, dirs):
        out = jnp.where(rows == d, ref[d, index], out)
    return out


def cos_turns(r):
    t = 0.25 - jnp.abs(r)
    x = t * t
    coef = [(-1) ** n * (2.0 * math.pi) ** (2 * n + 1) / math.factorial(2 * n + 1) for n in range(7)]
    out = jnp.full_like(x, coef[-1])
    for c in coef[-2::-1]:
        out = out * x + c
    return out * t


def rotated(g, e):
    low = low_lanes(e.shape)
    turned = swap(e)
    cos2 = jnp.where(low, e, turned)
    sin2 = jnp.where(low, -turned, e)
    return g * cos2 + swap(g) * sin2


def counter_rotated(g, e):
    low = low_lanes(e.shape)
    turned = swap(e)
    cos2 = jnp.where(low, e, turned)
    sin2 = jnp.where(low, -turned, e)
    return g * cos2 - swap(g) * sin2


def start_kernel(dims, pos_hbm, lmn_hbm, gains_hbm, e_ref, g_ref, p_ref, pos_ref, lmn_ref, gains_ref, sems):
    F, T, D, O, R, C = dims
    W = 2 * O
    copies = [
        pltpu.make_async_copy(pos_hbm, pos_ref, sems.at[0]),
        pltpu.make_async_copy(lmn_hbm, lmn_ref, sems.at[1]),
        pltpu.make_async_copy(gains_hbm, gains_ref, sems.at[2]),
    ]
    for copy in copies:
        copy.start()
    own = lax.axis_index("row") * C + lax.axis_index("col")
    first = lax.axis_index("band") * F
    low = low_lanes((D, W))
    rows = lax.broadcasted_iota(jnp.int32, (D, W), 0)
    shift = jnp.where(low, 0.0, 0.25)
    copies[0].wait()
    copies[1].wait()
    pos = pos_ref[:, :, :O]
    for k in range(1, R * C):
        pos = jnp.where(own == k, pos_ref[:, :, k * O : (k + 1) * O], pos)
    pos = jnp.concatenate([pos, pos], axis=-1)
    geometry = []
    for t in range(T):
        total = jnp.zeros((D, W), jnp.float32)
        for k in range(3):
            lm = jnp.full((D, W), lmn_ref[k, 0], jnp.float32)
            for d in range(1, D):
                lm = jnp.where(rows == d, lmn_ref[k, d], lm)
            total = total + lm * pos[k, t : t + 1, :]
        geometry.append(total)
    total_f = F * lax.axis_size("band")
    for f in range(F):
        nu = 1.0 + (first + f).astype(jnp.float32) * (1.0 / total_f)
        for t in range(T):
            ft = f * T + t
            turns = nu * geometry[t]
            r = turns - jnp.round(turns) + shift
            e_ref[ft] = cos_turns(r - jnp.round(r))
    copies[2].wait()
    for f in range(F):
        for t in range(T):
            ft = f * T + t
            g = jnp.concatenate([gains_ref[f, t, 0], gains_ref[f, t, 1]], axis=-1)
            g_ref[ft] = g
            p_ref[ft] = rotated(g, e_ref[ft])


def own_terms(dims, flux_ref, live_ref, g_ref, held_ref, slope_ref):
    F, T, D, O, _, _ = dims
    total = jnp.zeros((1, 2 * O), jnp.float32)
    for f in range(F):
        flux = column(flux_ref, f, D, 2 * O)
        for t in range(T):
            ft = f * T + t
            live = live_ref[ft : ft + 1, :]
            g = g_ref[ft]
            power = g * g
            power = (power + swap(power)) * flux
            own = jnp.sum(power, axis=0, keepdims=True)
            total = total + live * own * own
            power = power * flux
            slope_ref[ft] = -live * power
            held_ref[ft] = live * (own * flux - power) * g
    return total


def place(dims, f):
    F = dims[0]
    full = F * lax.axis_size("band")
    at = (lax.axis_index("band") * F + f).astype(jnp.float32)
    return at * (2.0 / (full - 1)) - 1.0


def fit_sums(dims, value, rhs_ref):
    F, T, D, O, _, _ = dims
    for t in range(T):
        acc = [jnp.zeros((D, 2 * O), jnp.float32) for _ in range(4)]
        for f in range(F):
            total = value(f, t)
            x = place(dims, f)
            for k in range(4):
                acc[k] = acc[k] + total
                total = total * x if k < 3 else total
        for k in range(4):
            rhs_ref[k * T + t] = acc[k]


def solve(dims, rhs_refs, t):
    T = dims[1]
    full = dims[0] * lax.axis_size("band")
    grid = 2.0 * np.arange(full, dtype=np.float64) / (full - 1) - 1.0
    basis = np.stack([grid**k for k in range(4)], axis=1)
    inverse = np.linalg.inv(basis.T @ basis)
    rhs = [sum(ref[k * T + t] for ref in rhs_refs) for k in range(4)]
    out = []
    for k in range(4):
        total = float(inverse[k, 0]) * rhs[0]
        for j in range(1, 4):
            total = total + float(inverse[k, j]) * rhs[j]
        out.append(total)
    return out


def curve(coeffs, x):
    return coeffs[0] + x * (coeffs[1] + x * (coeffs[2] + x * coeffs[3]))


def pick(index, parts):
    out = parts[0]
    for k in range(1, len(parts)):
        out = jnp.where(index == k, parts[k], out)
    return out


def setup_kernel(dims, cols, flux_hbm, flags_hbm, duals_hbm, g_ref, live_col_ref, live_half_ref,
                 live_own_ref, upright_ref, u_ref, rhs_ref, held_ref, slope_ref, samples_ref,
                 extra_ref, flux_ref, flags_ref, duals_ref, sems):
    F, T, _, O, R, C = dims
    W, rows, full = 2 * O, C * O, flags_ref.shape[2]
    row = lax.axis_index("row")
    col = lax.axis_index("col")
    copies = [
        pltpu.make_async_copy(flags_hbm, flags_ref, sems.at[0]),
        pltpu.make_async_copy(duals_hbm, duals_ref, sems.at[1]),
        pltpu.make_async_copy(flux_hbm, flux_ref, sems.at[2]),
    ]
    for copy in copies:
        copy.start()
    copies[0].wait()
    counts = jnp.zeros((T, full), jnp.float32)
    stacked = []
    for f in range(F):
        live = flags_ref[f].astype(jnp.float32)
        at = slice(f * T, (f + 1) * T)
        mine = pick(row, [live[:, r * rows : (r + 1) * rows] for r in range(R)])
        blocks = [mine[:, c * O : (c + 1) * O] for c in range(C)]
        live_col_ref[at, :] = pick(col, [live[:, c * cols : (c + 1) * cols] for c in range(C)])
        even = jnp.concatenate([blocks[0], blocks[2]], axis=1)
        odd = jnp.concatenate([blocks[1], blocks[3]], axis=1)
        live_half_ref[at, :] = pick(col % 2, [even, odd])
        own = pick(col, blocks)
        live_own_ref[at, :] = jnp.concatenate([own, own], axis=1)
        stacked.append(mine)
        count = jnp.sum(live, axis=1, keepdims=True)
        counts = counts + live * (count - 1.0)
    stacked = jnp.concatenate(stacked + [jnp.zeros((W - F * T, rows), jnp.float32)], axis=0)
    upright_ref[...] = jnp.transpose(stacked)
    samples = jnp.sum(counts, axis=0, keepdims=True)
    samples = jnp.sum(samples, axis=1, keepdims=True) / (R * C)
    copies[1].wait()
    copies[2].wait()
    for f in range(F):
        for t in range(T):
            u_ref[f * T + t] = jnp.concatenate([duals_ref[f, t, 0], duals_ref[f, t, 1]], axis=-1)
    fit_sums(dims, lambda f, t: u_ref[f * T + t] + g_ref[f * T + t], rhs_ref)
    own = own_terms(dims, flux_ref, live_own_ref, g_ref, held_ref, slope_ref)
    lanes = lax.broadcasted_iota(jnp.int32, own.shape, 1)
    samples = jnp.where(lanes == O, samples, 0.0)
    samples_ref[...] = samples
    extra_ref[...] = samples - jnp.where(low_lanes(own.shape), own, 0.0)


def again_kernel(dims, flux_ref, samples_ref, live_ref, u_ref, g_ref,
                 rhs_ref, held_ref, slope_ref, extra_ref):
    _, T, _, _, _, _ = dims
    fit_sums(dims, lambda f, t: u_ref[f * T + t] + g_ref[f * T + t], rhs_ref)
    own = own_terms(dims, flux_ref, live_ref, g_ref, held_ref, slope_ref)
    extra_ref[...] = samples_ref[...] - jnp.where(low_lanes(own.shape), own, 0.0)


def add_kernel(a_ref, b_ref, out_ref):
    out_ref[...] = a_ref[...] + b_ref[...]


def target_kernel(dims, first_pass, u_ref, g_ref, *refs):
    F, T, _, _, _, _ = dims
    rhs_refs, outs = refs[:2], refs[2:]
    for t in range(T):
        coeffs = solve(dims, rhs_refs, t)
        for f in range(F):
            ft = f * T + t
            smooth = curve(coeffs, place(dims, f))
            u = u_ref[ft]
            if not first_pass:
                u = u + g_ref[ft] - smooth
                outs[1][ft] = u
            outs[0][ft] = smooth - u


def block_mask(size):
    shape = (8 * size, 8 * size)
    a = lax.broadcasted_iota(jnp.int32, shape, 0) // size
    b = lax.broadcasted_iota(jnp.int32, shape, 1) // size
    return a == b


def sum_kernel(dims, flux_hbm, vis_hbm, live_ref, a_ref, b_ref, *refs):
    F, T, D, O, _, _ = dims
    upright_ref, refs = (refs[0], refs[1:]) if len(refs) == 8 else (None, refs)
    keep_ref, send_ref, refs = refs[0], refs[1], refs[2:]
    power_ref, refs = (refs[0], refs[1:]) if upright_ref is not None else (None, refs)
    vis_ref, distinct, flux_ref, sems = refs
    rows, cols = vis_ref.shape[3], vis_ref.shape[4]
    row = lax.axis_index("row")
    col = lax.axis_index("col")
    parity = col % 2

    def vis_copy(f):
        return pltpu.make_async_copy(vis_hbm.at[f], vis_ref.at[f], sems.at[f])

    flux_copy = pltpu.make_async_copy(flux_hbm, flux_ref, sems.at[F])
    flux_copy.start()
    ahead = 2 * CHUNK
    for f in range(ahead):
        vis_copy(f).start()
    p = lax.broadcasted_iota(jnp.int32, (rows, cols), 0) + row * rows
    q = lax.broadcasted_iota(jnp.int32, (rows, cols), 1) + col * cols
    distinct[...] = jnp.where(p == q, 0.0, 1.0).astype(jnp.bfloat16)
    group = 8 // T
    blocks = block_mask(2 * D)
    nt = (((1,), (1,)), ((), ()))

    def body(step, upright, start, power):
        highs, lows = [], []
        lives = live_ref[pl.ds(step * 8, 8), :]
        mask = distinct[...]
        for i in range(group):
            f = step * group + i
            scale = column(flux_ref, f, D, cols)
            for t in range(T):
                j = i * T + t
                ft = step * 8 + j
                a, b = a_ref[ft], b_ref[ft]
                first = jnp.where(row == 0, a, b)
                second = jnp.where(row == 0, b, a)
                weight = scale * lives[j : j + 1, :]
                re = join_low(first, second) * weight
                im = join_high(first, second) * weight
                x = jnp.concatenate(
                    [jnp.concatenate([re, -im], axis=1), jnp.concatenate([im, re], axis=1)], axis=0
                )
                high = x.astype(jnp.bfloat16)
                low = (x - high.astype(jnp.float32)).astype(jnp.bfloat16)
                highs.append(high)
                lows.append(low)
                both = jnp.concatenate([high, low], axis=0)
                seen = [vis_ref[f, t, part] * mask for part in range(2)]
                v = lax.dot_general(
                    both, jnp.concatenate(seen, axis=1), nt, preferred_element_type=jnp.float32
                )
                v = v[: 2 * D] + v[2 * D :]
                v0, v1 = v[:, : 2 * O], v[:, 2 * O :]
                even, odd = join_low(v0, v1), join_high(v0, v1)
                keep_ref[step * 9 + j] = jnp.where(parity == 0, even, odd)
                send_ref[step * 9 + j] = jnp.where(parity == 0, odd, even)
                if upright is not None:
                    square = [x.astype(jnp.float32) for x in seen]
                    square = square[0] * square[0] + square[1] * square[1]
                    at = start + j
                    square = square * jnp.broadcast_to(upright[:, at : at + 1], square.shape)
                    square = jnp.sum(square.reshape(rows // 8, 8, cols), axis=0)
                    power = power + square * lives[j : j + 1, :]
        high = jnp.concatenate(highs, axis=0)
        low = jnp.concatenate(lows, axis=0)
        gram = lax.dot_general(high, high, nt, preferred_element_type=jnp.float32)
        gram = gram + lax.dot_general(high, low, nt, preferred_element_type=jnp.float32)
        gram = gram + lax.dot_general(low, high, nt, preferred_element_type=jnp.float32)
        gram = jnp.where(blocks, gram, 0.0)
        folded = gram[: 2 * D]
        for i in range(1, 8):
            folded = folded + gram[i * 2 * D : (i + 1) * 2 * D]
        keep_ref[step * 9 + 8] = folded
        send_ref[step * 9 + 8] = folded
        return power

    def chunk(c, power):
        first = isinstance(c, int)
        if not first:
            for i in range(CHUNK):
                vis_copy(c * CHUNK + i).wait()

        def more():
            for i in range(CHUNK):
                vis_copy(c * CHUNK + ahead + i).start()

        if not first:
            pl.when(c * CHUNK + ahead < F)(more)

        upright = None
        if upright_ref is not None:
            upright = pltpu.roll(upright_ref[...], (2 * O - c * CHUNK * T) % (2 * O), 1)
        for j in range(CHUNK // group):
            if first:
                for i in range(group):
                    vis_copy(j * group + i).wait()
            power = body(c * (CHUNK // group) + j, upright, j * 8, power)
        if first and ahead < F:
            more()
        return power

    flux_copy.wait()
    power = chunk(0, jnp.zeros((8, cols), jnp.float32))
    power = lax.fori_loop(1, F // CHUNK, chunk, power)
    if power_ref is not None:
        power = jnp.sum(power, axis=0, keepdims=True)
        power_ref[...] = jnp.where(low_lanes(power.shape), power + swap(power), 0.0)


def residual_kernel(dims, live_ref, extra_ref, power_ref, kept_ref, other_ref, mine_ref, theirs_ref,
                    passed_ref, got_ref,
                    keep_ref, send_ref, scalar_ref):
    F, T, D, O, _, _ = dims
    W = 2 * O
    row = lax.axis_index("row")
    col = lax.axis_index("col")
    near = col // 2 == 0
    away = col // 2 != row
    held = col % 2 != row
    mask = block_mask(2 * D)
    eye = lax.broadcasted_iota(jnp.int32, (2 * D, W), 0) == (
        lax.broadcasted_iota(jnp.int32, (2 * D, W), 1) % (2 * D)
    )
    total = jnp.zeros((2 * D, W), jnp.float32)
    for group in range(F * T // 8):
        gram = kept_ref[group * 9 + 8] + other_ref[group * 9 + 8]
        diagonal = jnp.sum(jnp.where(eye, gram, 0.0), axis=0, keepdims=True)
        keep_ref[F * T, group : group + 1, :] = diagonal
        send_ref[F * T, group : group + 1, :] = diagonal
        spread = jnp.where(mask, jnp.concatenate([gram] * 8, axis=0), 0.0)
        station = []
        for i in range(8):
            ft = group * 8 + i
            a = mine_ref[ft]
            b = jnp.where(away, theirs_ref[ft], jnp.where(held, got_ref[ft], passed_ref[ft]))
            first = jnp.where(near, a, b)
            second = jnp.where(near, b, a)
            station += [join_low(first, second), join_high(first, second)]
        model = jnp.dot(
            spread, jnp.concatenate(station, axis=0), precision=HIGH,
            preferred_element_type=jnp.float32,
        )
        for i in range(8):
            ft = group * 8 + i
            live = live_ref[ft : ft + 1, :]
            v = kept_ref[group * 9 + i] + other_ref[group * 9 + i]
            num = (v - model[i * 2 * D : (i + 1) * 2 * D]) * live
            z = jnp.concatenate(station[2 * i : 2 * i + 2], axis=0)
            total = total + z * (v * live + num)
            low, high = join_low(num[:D], num[D:]), join_high(num[:D], num[D:])
            keep_ref[ft] = jnp.where(near, low, high)
            send_ref[ft] = jnp.where(near, high, low)
    squares = -jnp.sum(total, axis=0, keepdims=True)
    squares = squares + swap(squares)
    scalar = jnp.where(low_lanes(squares.shape), squares, 0.0) + extra_ref[...] + power_ref[...]
    scalar_ref[...] = jnp.broadcast_to(scalar, scalar_ref.shape)


def merge_kernel(dims, keep_ref, come_ref, live_ref, e_ref, g_ref, held_ref, slope_ref,
                 num_ref, den_ref):
    F, T, D, O, _, _ = dims
    W = 2 * O
    shape = (8 * D, W)
    a = lax.broadcasted_iota(jnp.int32, shape, 0)
    b = lax.broadcasted_iota(jnp.int32, shape, 1)
    eye = a // D * (2 * D) + a % D == b
    ones = jnp.ones((W, W), jnp.float32)
    for group in range(F * T // 8):
        diagonal = keep_ref[F * T, group : group + 1, :] + come_ref[F * T, group : group + 1, :]
        spread = jnp.dot(
            jnp.where(eye, diagonal, 0.0), ones, precision=HIGH, preferred_element_type=jnp.float32
        )
        for i in range(8):
            ft = group * 8 + i
            around = live_ref[ft : ft + 1, :] * spread[i * D : (i + 1) * D]
            num = counter_rotated(keep_ref[ft] + come_ref[ft], e_ref[ft])
            num_ref[ft] = num + held_ref[ft] + around * g_ref[ft]
            den_ref[ft] = around + slope_ref[ft]


def update_kernel(dims, last, full, *refs):
    F, T, D, O, _, _ = dims
    scalar_ref, num_ref, den_ref, target_ref, g_ref, other_ref = refs[:6]
    W = 2 * O
    sums = jnp.sum(scalar_ref[...], axis=0, keepdims=True)
    low = low_lanes(sums.shape)
    squares = jnp.sum(jnp.where(low, sums, 0.0), axis=1, keepdims=True)
    samples = jnp.sum(jnp.where(low, 0.0, sums), axis=1, keepdims=True)
    squares = jnp.maximum(squares, 0.0)
    rho = PENALTY * full * (squares / samples + 1e-06)
    rho = jnp.broadcast_to(rho, (D, W))
    for t in range(T):
        acc = [jnp.zeros((D, W), jnp.float32) for _ in range(4)]
        for f in range(F):
            ft = f * T + t
            fresh = (num_ref[ft] + rho * target_ref[ft]) / (den_ref[ft] + rho)
            g = 0.5 * (g_ref[ft] + fresh)
            if last:
                out_ref, total_ref, rhs_ref = refs[6:]
                out_ref[ft] = g
                total = other_ref[ft] + g
                total_ref[ft] = total
                x = place(dims, f)
                for k in range(4):
                    acc[k] = acc[k] + total
                    total = total * x if k < 3 else total
            else:
                g_out, p_out = refs[6:]
                g_out[ft] = g
                p_out[ft] = rotated(g, other_ref[ft])
        if last:
            for k in range(4):
                rhs_ref[k * T + t] = acc[k]


def write_out(dims, value, out_hbm, out_ref, sems):
    F, T, _, O, _, _ = dims
    copies = []
    for part in range(F // CHUNK):
        for f in range(part * CHUNK, (part + 1) * CHUNK):
            for t in range(T):
                x = value(f, t)
                out_ref[f, t, 0] = x[:, :O]
                out_ref[f, t, 1] = x[:, O:]
        at = pl.ds(part * CHUNK, CHUNK)
        copies.append(pltpu.make_async_copy(out_ref.at[at], out_hbm.at[at], sems.at[part]))
        copies[-1].start()
    for copy in copies:
        copy.wait()


def emit_kernel(dims, g_ref, out_hbm, out_ref, sems):
    write_out(dims, lambda f, t: g_ref[f * dims[1] + t], out_hbm, out_ref, sems)


def final_kernel(dims, total_ref, *refs):
    T = dims[1]
    coeffs = [solve(dims, refs[:-3], t) for t in range(T)]
    write_out(
        dims, lambda f, t: total_ref[f * T + t] - curve(coeffs[t], place(dims, f)), *refs[-3:]
    )


def shards(sizes, vis, flags, positions, lmn, flux, gains, duals):
    R, C, Z = sizes
    F, T, _, D, O = gains.shape
    rows, cols = vis.shape[3], vis.shape[4]
    full = flags.shape[2]
    FT, W = F * T, 2 * O
    dims = (F, T, D, O, R, C)
    f32 = jnp.float32
    smem = pl.BlockSpec(memory_space=pltpu.SMEM)
    vmem = pl.BlockSpec(memory_space=pltpu.VMEM)
    hbm = pl.BlockSpec(memory_space=pltpu.HBM)

    def array(*shape):
        return jax.ShapeDtypeStruct(shape, f32)

    def far(x):
        return pltpu.with_memory_space_constraint(x, pltpu.HBM)

    def call(kernel, outs, scalars, arrays, scratch=()):
        return pl.pallas_call(
            kernel,
            out_shape=outs,
            in_specs=[smem] * len(scalars) + [vmem] * len(arrays),
            out_specs=[vmem] * len(outs),
            scratch_shapes=list(scratch),
            compiler_params=LIMIT,
        )(*scalars, *arrays)

    def where(r, c, z):
        return (r * C + c) * Z + z

    def permute(x, move, some=lambda r, c: True):
        pairs = [
            (where(r, c, z), where(*move(r, c, z)))
            for r in range(R) for c in range(C) for z in range(Z) if some(r, c)
        ]
        return lax.ppermute(x, AXES, pairs)

    def gather(x, m):
        return permute(x, lambda r, c, z: (((r * C + c) % R + m) % R, (r * C + c) // R, z))

    def bands(x):
        return [x] + [permute(x, lambda r, c, z, k=k: (r, c, (z + k) % Z)) for k in range(1, Z)]

    whole, line, fit = array(FT, D, W), array(FT + 1, D, W), array(4 * T, D, W)
    pair, text = array(FT // 8 * 9, 2 * D, W), array(1, W)
    flux_t = flux.T
    rot, g, p = pl.pallas_call(
        functools.partial(start_kernel, dims),
        out_shape=[whole] * 3,
        in_specs=[hbm] * 3,
        out_specs=[vmem] * 3,
        scratch_shapes=[
            pltpu.VMEM((3, T, full), f32),
            pltpu.SMEM(lmn.shape, f32),
            pltpu.VMEM(gains.shape, f32),
            pltpu.SemaphoreType.DMA((3,)),
        ],
        compiler_params=LIMIT,
        name="start",
    )(far(positions.transpose(1, 0, 2)), far(lmn), far(gains))
    for step in range(ITERS):
        last = step == ITERS - 1
        got = [gather(p, m) for m in range(R)]
        if step == 0:
            (live_col, live_half, live_own, upright, u, rhs, held, slope, samples, extra) = (
                pl.pallas_call(
                    functools.partial(setup_kernel, dims, cols),
                    out_shape=[
                        array(FT, cols), array(FT, W), array(FT, W), array(rows, W), whole,
                        fit, whole, whole, text, text,
                    ],
                    in_specs=[hbm] * 3 + [vmem],
                    out_specs=[vmem] * 10,
                    scratch_shapes=[
                        pltpu.SMEM(flux_t.shape, f32),
                        pltpu.VMEM(flags.shape, flags.dtype),
                        pltpu.VMEM(duals.shape, f32),
                        pltpu.SemaphoreType.DMA((3,)),
                    ],
                    compiler_params=LIMIT,
                    name="setup",
                )(far(flux_t), far(flags), far(duals), g)
            )
        else:
            rhs, held, slope, extra = call(
                functools.partial(again_kernel, dims),
                [fit, whole, whole, text], [flux_t], [samples, live_own, u, g],
            )
        rhs_near = permute(rhs, lambda r, c, z: (r, c, z ^ 1))
        theirs = permute(p, lambda r, c, z: (r, c ^ 2, z), lambda r, c: r == c // 2)
        more = [] if step else [upright]
        keep, send, *found = pl.pallas_call(
            functools.partial(sum_kernel, dims),
            out_shape=[pair, pair] + ([] if step else [array(1, cols)]),
            in_specs=[hbm] * 2 + [vmem] * (3 + len(more)),
            out_specs=[vmem] * (2 + len(more)),
            scratch_shapes=[
                pltpu.VMEM(vis.shape, vis.dtype),
                pltpu.VMEM((rows, cols), vis.dtype),
                pltpu.SMEM(flux_t.shape, f32),
                pltpu.SemaphoreType.DMA((F + 1,)),
            ],
            compiler_params=LIMIT,
            name="sums",
        )(far(flux_t), far(vis), live_col, *got, *more)
        power = power if step else found[0]
        passed = permute(
            got[0], lambda r, c, z: (r, c ^ 1, z), lambda r, c: c == 3 * r + (1 - 2 * r)
        )
        other = permute(send, lambda r, c, z: (r, c ^ 1, z))
        (rhs,) = call(add_kernel, [fit], [], [rhs, rhs_near])
        rhs_far = permute(rhs, lambda r, c, z: (r, c, z ^ 2))
        keep, send, scalar = call(
            functools.partial(residual_kernel, dims), [line, line, array(R * C * Z, W)],
            [], [live_half, extra, power, keep, other, p, theirs, passed, got[1]],
        )
        come = permute(send, lambda r, c, z: (r, c ^ 2, z))
        scalar = lax.all_to_all(scalar, AXES, 0, 0, tiled=True)
        target = call(
            functools.partial(target_kernel, dims, step == 0),
            [whole] * (1 if step == 0 else 2), [], [u, g, rhs, rhs_far],
        )
        num, den = call(
            functools.partial(merge_kernel, dims), [whole, whole], [],
            [keep, come, live_own, rot, g, held, slope],
        )
        update = functools.partial(update_kernel, dims, last, float(full))
        arrays = [scalar, num, den, target[0], g]
        if last:
            g, total, rhs = call(
                update, [whole, whole, fit], [],
                arrays + [target[1]],
            )
        else:
            g, p = call(update, [whole, whole], [], arrays + [rot])

    def write(kernel, arrays):
        return pl.pallas_call(
            functools.partial(kernel, dims),
            out_shape=array(*gains.shape),
            in_specs=[vmem] * len(arrays),
            out_specs=hbm,
            scratch_shapes=[pltpu.VMEM(gains.shape, f32), pltpu.SemaphoreType.DMA((F // CHUNK,))],
            compiler_params=LIMIT,
        )(*arrays)

    rhs_all = bands(rhs)
    gain = write(emit_kernel, [g])
    dual = write(final_kernel, [total, *rhs_all])
    return (gain, dual)


def basis(count):
    grid = 2.0 * jnp.arange(count, dtype=jnp.float32) / (count - 1) - 1.0
    return jnp.stack([grid**power for power in range(4)], axis=1)


def rotate(positions, lmn, freq):
    geometry = jnp.einsum("tks,kd->tds", positions, lmn, precision=HIGH)
    angle = 2.0 * math.pi * freq[:, None, None, None] * geometry[None]
    return (jnp.cos(angle), -jnp.sin(angle))


def complex_mul(a_re, a_im, b_re, b_im):
    return (a_re * b_re - a_im * b_im, a_re * b_im + a_im * b_re)


def solve_fit(rhs, total_f):
    full = basis(total_f)
    gram = jnp.dot(full.T, full, precision=HIGH)
    factor = jnp.linalg.cholesky(gram)
    flat = rhs.reshape(rhs.shape[0], -1)
    return jax.scipy.linalg.cho_solve((factor, True), flat).reshape(rhs.shape)


def plain_shards(vis, flags, positions, lmn, flux, gains, duals):
    width = gains.shape[0]
    total_f = width * lax.axis_size("band")
    first = lax.axis_index("band") * width
    local_basis = lax.dynamic_slice_in_dim(basis(total_f), first, width, 0)
    freq = 1.0 + (first + jnp.arange(width, dtype=jnp.int32)).astype(jnp.float32) / total_f
    row_index = lax.axis_index("row")
    col_index = lax.axis_index("col")
    row_count = vis.shape[3]
    col_count = vis.shape[4]
    owned = gains.shape[4]
    own_start = (row_index * lax.axis_size("col") + col_index) * owned
    row_start = row_index * row_count
    col_start = col_index * col_count
    own_cos, own_sin = rotate(lax.dynamic_slice_in_dim(positions, own_start, owned, 2), lmn, freq)
    row_cos, row_sin = rotate(
        lax.dynamic_slice_in_dim(positions, row_start, row_count, 2), lmn, freq
    )
    col_cos, col_sin = rotate(
        lax.dynamic_slice_in_dim(positions, col_start, col_count, 2), lmn, freq
    )
    all_live = flags.astype(jnp.float32)
    row_live = lax.dynamic_slice_in_dim(all_live, row_start, row_count, 2)
    col_live = lax.dynamic_slice_in_dim(all_live, col_start, col_count, 2)
    own_live = lax.dynamic_slice_in_dim(all_live, own_start, owned, 2)
    row_ids = row_start + jnp.arange(row_count, dtype=jnp.int32)
    col_ids = col_start + jnp.arange(col_count, dtype=jnp.int32)
    distinct = (row_ids[:, None] != col_ids[None, :]).astype(jnp.float32)
    weight = row_live[:, :, :, None] * col_live[:, :, None, :] * distinct
    vis_re = vis[:, :, 0].astype(jnp.float32)
    vis_im = vis[:, :, 1].astype(jnp.float32)
    scale = flux[:, None, :, None]

    def fit(gain, dual):
        rhs = jnp.einsum("fk,ftcds->ktcds", local_basis, gain + dual, precision=HIGH)
        return solve_fit(lax.psum(rhs, "band"), total_f)

    gain, dual = (gains, duals)
    coeffs = fit(gain, dual)
    for _ in range(ITERS):
        target = jnp.einsum("fk,ktcds->ftcds", local_basis, coeffs, precision=HIGH) - dual
        every = lax.all_gather(gain, ("row", "col"), axis=4, tiled=True)
        row_gain = lax.dynamic_slice_in_dim(every, row_start, row_count, 4)
        col_gain = lax.dynamic_slice_in_dim(every, col_start, col_count, 4)
        row_re, row_im = complex_mul(row_gain[:, :, 0], row_gain[:, :, 1], row_cos, row_sin)
        col_re, col_im = complex_mul(col_gain[:, :, 0], col_gain[:, :, 1], col_cos, col_sin)
        col_re = scale * col_re
        col_im = scale * col_im
        model_re = jnp.einsum("ftdp,ftdq->ftpq", row_re, col_re, precision=HIGH) + jnp.einsum(
            "ftdp,ftdq->ftpq", row_im, col_im, precision=HIGH
        )
        model_im = jnp.einsum("ftdp,ftdq->ftpq", row_im, col_re, precision=HIGH) - jnp.einsum(
            "ftdp,ftdq->ftpq", row_re, col_im, precision=HIGH
        )
        resid_re = weight * (vis_re - model_re)
        resid_im = weight * (vis_im - model_im)
        squares, samples = lax.psum(
            (jnp.sum(resid_re * resid_re + resid_im * resid_im), jnp.sum(weight)),
            ("row", "col", "band"),
        )
        sum_re = jnp.einsum("ftpq,ftdq->ftdp", resid_re, col_re, precision=HIGH) - jnp.einsum(
            "ftpq,ftdq->ftdp", resid_im, col_im, precision=HIGH
        )
        sum_im = jnp.einsum("ftpq,ftdq->ftdp", resid_re, col_im, precision=HIGH) + jnp.einsum(
            "ftpq,ftdq->ftdp", resid_im, col_re, precision=HIGH
        )
        pairs = lax.psum_scatter(
            jnp.stack([sum_re, sum_im], axis=2), "col", scatter_dimension=4, tiled=True
        )
        every_mag = every[:, :, 0] * every[:, :, 0] + every[:, :, 1] * every[:, :, 1]
        total_mag = jnp.einsum("ftds,fts->ftd", every_mag, all_live, precision=HIGH)
        own_mag = gain[:, :, 0] * gain[:, :, 0] + gain[:, :, 1] * gain[:, :, 1]
        own_flag = own_live[:, :, None, :]
        own_denom = (scale * scale * own_flag * (total_mag[:, :, :, None] - own_flag * own_mag))[
            :, :, None
        ]
        num_re, num_im = complex_mul(own_cos, -own_sin, pairs[:, :, 0], pairs[:, :, 1])
        numer = jnp.stack([num_re, num_im], axis=2)
        rho = PENALTY * flags.shape[2] * (squares / samples + 1e-06)
        fresh = (numer + own_denom * gain + rho * target) / (own_denom + rho)
        gain = 0.5 * (gain + fresh)
        coeffs = fit(gain, dual)
        dual = dual + gain - jnp.einsum("fk,ktcds->ftcds", local_basis, coeffs, precision=HIGH)
    return (gain, dual)


def solution(mesh):
    sizes = tuple(mesh.shape[a] for a in AXES)

    fits = sizes == (2, 4, 4)

    def body(*args):
        gains = args[5]
        if fits and gains.shape[3:] == (8, 64) and 8 % gains.shape[1] == 0:
            return shards(sizes, *args)
        return plain_shards(*args)

    return jax.shard_map(
        body,
        mesh=mesh,
        in_specs=(
            P("band", None, None, "row", "col"),
            P("band", None, None),
            P(),
            P(),
            P("band", None),
            P("band", None, None, None, ("row", "col")),
            P("band", None, None, None, ("row", "col")),
        ),
        out_specs=(
            P("band", None, None, None, ("row", "col")),
            P("band", None, None, None, ("row", "col")),
        ),
        check_vma=False,
    )
```

```python
import functools
import math

import jax
import jax.numpy as jnp
import numpy as np
from jax import lax
from jax.experimental import pallas as pl
from jax.experimental.pallas import tpu as pltpu
from jax.sharding import PartitionSpec as P

ITERS = 2
PENALTY = 0.05
HIGH = lax.Precision.HIGHEST
AXES = ("row", "col", "band")
CHUNK = 4
LIMIT = pltpu.CompilerParams(vmem_limit_bytes=16 * 2**20)


def swap(x):
    half = x.shape[-1] // 2
    return pltpu.roll(x, half, x.ndim - 1)


def low_lanes(shape):
    return lax.broadcasted_iota(jnp.int32, shape, len(shape) - 1) < shape[-1] // 2


def join_low(a, b):
    return jnp.where(low_lanes(a.shape), a, swap(b))


def join_high(a, b):
    return jnp.where(low_lanes(a.shape), swap(a), b)


def column(ref, index, dirs, lanes):
    rows = lax.broadcasted_iota(jnp.int32, (dirs, lanes), 0)
    out = jnp.full((dirs, lanes), ref[0, index], jnp.float32)
    for d in range(1, dirs):
        out = jnp.where(rows == d, ref[d, index], out)
    return out


def cos_turns(r):
    t = 0.25 - jnp.abs(r)
    x = t * t
    coef = [(-1) ** n * (2.0 * math.pi) ** (2 * n + 1) / math.factorial(2 * n + 1) for n in range(7)]
    out = jnp.full_like(x, coef[-1])
    for c in coef[-2::-1]:
        out = out * x + c
    return out * t


def rotated(g, e):
    low = low_lanes(e.shape)
    turned = swap(e)
    cos2 = jnp.where(low, e, turned)
    sin2 = jnp.where(low, -turned, e)
    return g * cos2 + swap(g) * sin2


def counter_rotated(g, e):
    low = low_lanes(e.shape)
    turned = swap(e)
    cos2 = jnp.where(low, e, turned)
    sin2 = jnp.where(low, -turned, e)
    return g * cos2 - swap(g) * sin2


def start_kernel(dims, pos_hbm, lmn_hbm, gains_hbm, e_ref, g_ref, p_ref, pos_ref, lmn_ref, gains_ref, sems):
    F, T, D, O, R, C = dims
    W = 2 * O
    copies = [
        pltpu.make_async_copy(pos_hbm, pos_ref, sems.at[0]),
        pltpu.make_async_copy(lmn_hbm, lmn_ref, sems.at[1]),
        pltpu.make_async_copy(gains_hbm, gains_ref, sems.at[2]),
    ]
    for copy in copies:
        copy.start()
    own = lax.axis_index("row") * C + lax.axis_index("col")
    first = lax.axis_index("band") * F
    low = low_lanes((D, W))
    rows = lax.broadcasted_iota(jnp.int32, (D, W), 0)
    shift = jnp.where(low, 0.0, 0.25)
    copies[0].wait()
    copies[1].wait()
    pos = pos_ref[:, :, :O]
    for k in range(1, R * C):
        pos = jnp.where(own == k, pos_ref[:, :, k * O : (k + 1) * O], pos)
    pos = jnp.concatenate([pos, pos], axis=-1)
    geometry = []
    for t in range(T):
        total = jnp.zeros((D, W), jnp.float32)
        for k in range(3):
            lm = jnp.full((D, W), lmn_ref[k, 0], jnp.float32)
            for d in range(1, D):
                lm = jnp.where(rows == d, lmn_ref[k, d], lm)
            total = total + lm * pos[k, t : t + 1, :]
        geometry.append(total)
    total_f = F * lax.axis_size("band")
    for f in range(F):
        nu = 1.0 + (first + f).astype(jnp.float32) * (1.0 / total_f)
        for t in range(T):
            ft = f * T + t
            turns = nu * geometry[t]
            r = turns - jnp.round(turns) + shift
            e_ref[ft] = cos_turns(r - jnp.round(r))
    copies[2].wait()
    for f in range(F):
        for t in range(T):
            ft = f * T + t
            g = jnp.concatenate([gains_ref[f, t, 0], gains_ref[f, t, 1]], axis=-1)
            g_ref[ft] = g
            p_ref[ft] = rotated(g, e_ref[ft])


def own_terms(dims, flux_ref, live_ref, g_ref, held_ref, slope_ref):
    F, T, D, O, _, _ = dims
    total = jnp.zeros((1, 2 * O), jnp.float32)
    for f in range(F):
        flux = column(flux_ref, f, D, 2 * O)
        for t in range(T):
            ft = f * T + t
            live = live_ref[ft : ft + 1, :]
            g = g_ref[ft]
            power = g * g
            power = (power + swap(power)) * flux
            own = jnp.sum(power, axis=0, keepdims=True)
            total = total + live * own * own
            power = power * flux
            slope_ref[ft] = -live * power
            held_ref[ft] = live * (own * flux - power) * g
    return total


def place(dims, f):
    F = dims[0]
    full = F * lax.axis_size("band")
    at = (lax.axis_index("band") * F + f).astype(jnp.float32)
    return at * (2.0 / (full - 1)) - 1.0


def fit_sums(dims, value, rhs_ref):
    F, T, D, O, _, _ = dims
    for t in range(T):
        acc = [jnp.zeros((D, 2 * O), jnp.float32) for _ in range(4)]
        for f in range(F):
            total = value(f, t)
            x = place(dims, f)
            for k in range(4):
                acc[k] = acc[k] + total
                total = total * x if k < 3 else total
        for k in range(4):
            rhs_ref[k * T + t] = acc[k]


def solve(dims, rhs_refs, t):
    T = dims[1]
    full = dims[0] * lax.axis_size("band")
    grid = 2.0 * np.arange(full, dtype=np.float64) / (full - 1) - 1.0
    basis = np.stack([grid**k for k in range(4)], axis=1)
    inverse = np.linalg.inv(basis.T @ basis)
    rhs = [sum(ref[k * T + t] for ref in rhs_refs) for k in range(4)]
    out = []
    for k in range(4):
        total = float(inverse[k, 0]) * rhs[0]
        for j in range(1, 4):
            total = total + float(inverse[k, j]) * rhs[j]
        out.append(total)
    return out


def curve(coeffs, x):
    return coeffs[0] + x * (coeffs[1] + x * (coeffs[2] + x * coeffs[3]))


def pick(index, parts):
    out = parts[0]
    for k in range(1, len(parts)):
        out = jnp.where(index == k, parts[k], out)
    return out


def setup_kernel(dims, cols, flux_hbm, flags_hbm, duals_hbm, g_ref, live_col_ref, live_half_ref,
                 live_own_ref, upright_ref, u_ref, rhs_ref, held_ref, slope_ref, samples_ref,
                 extra_ref, flux_ref, flags_ref, duals_ref, sems):
    F, T, _, O, R, C = dims
    W, rows, full = 2 * O, C * O, flags_ref.shape[2]
    row = lax.axis_index("row")
    col = lax.axis_index("col")
    copies = [
        pltpu.make_async_copy(flags_hbm, flags_ref, sems.at[0]),
        pltpu.make_async_copy(duals_hbm, duals_ref, sems.at[1]),
        pltpu.make_async_copy(flux_hbm, flux_ref, sems.at[2]),
    ]
    for copy in copies:
        copy.start()
    copies[0].wait()
    counts = jnp.zeros((T, full), jnp.float32)
    stacked = []
    for f in range(F):
        live = flags_ref[f].astype(jnp.float32)
        at = slice(f * T, (f + 1) * T)
        mine = pick(row, [live[:, r * rows : (r + 1) * rows] for r in range(R)])
        blocks = [mine[:, c * O : (c + 1) * O] for c in range(C)]
        live_col_ref[at, :] = pick(col, [live[:, c * cols : (c + 1) * cols] for c in range(C)])
        even = jnp.concatenate([blocks[0], blocks[2]], axis=1)
        odd = jnp.concatenate([blocks[1], blocks[3]], axis=1)
        live_half_ref[at, :] = pick(col % 2, [even, odd])
        own = pick(col, blocks)
        live_own_ref[at, :] = jnp.concatenate([own, own], axis=1)
        stacked.append(mine)
        count = jnp.sum(live, axis=1, keepdims=True)
        counts = counts + live * (count - 1.0)
    stacked = jnp.concatenate(stacked + [jnp.zeros((W - F * T, rows), jnp.float32)], axis=0)
    upright_ref[...] = jnp.transpose(stacked)
    samples = jnp.sum(counts, axis=0, keepdims=True)
    samples = jnp.sum(samples, axis=1, keepdims=True) / (R * C)
    copies[1].wait()
    copies[2].wait()
    for f in range(F):
        for t in range(T):
            u_ref[f * T + t] = jnp.concatenate([duals_ref[f, t, 0], duals_ref[f, t, 1]], axis=-1)
    fit_sums(dims, lambda f, t: u_ref[f * T + t] + g_ref[f * T + t], rhs_ref)
    own = own_terms(dims, flux_ref, live_own_ref, g_ref, held_ref, slope_ref)
    lanes = lax.broadcasted_iota(jnp.int32, own.shape, 1)
    samples = jnp.where(lanes == O, samples, 0.0)
    samples_ref[...] = samples
    extra_ref[...] = samples - jnp.where(low_lanes(own.shape), own, 0.0)


def again_kernel(dims, flux_ref, samples_ref, live_ref, u_ref, g_ref,
                 rhs_ref, held_ref, slope_ref, extra_ref):
    _, T, _, _, _, _ = dims
    fit_sums(dims, lambda f, t: u_ref[f * T + t] + g_ref[f * T + t], rhs_ref)
    own = own_terms(dims, flux_ref, live_ref, g_ref, held_ref, slope_ref)
    extra_ref[...] = samples_ref[...] - jnp.where(low_lanes(own.shape), own, 0.0)


def add_kernel(a_ref, b_ref, out_ref):
    out_ref[...] = a_ref[...] + b_ref[...]


def target_kernel(dims, first_pass, u_ref, g_ref, *refs):
    F, T, _, _, _, _ = dims
    rhs_refs, outs = refs[:2], refs[2:]
    for t in range(T):
        coeffs = solve(dims, rhs_refs, t)
        for f in range(F):
            ft = f * T + t
            smooth = curve(coeffs, place(dims, f))
            u = u_ref[ft]
            if not first_pass:
                u = u + g_ref[ft] - smooth
                outs[1][ft] = u
            outs[0][ft] = smooth - u


def block_mask(size):
    shape = (8 * size, 8 * size)
    a = lax.broadcasted_iota(jnp.int32, shape, 0) // size
    b = lax.broadcasted_iota(jnp.int32, shape, 1) // size
    return a == b


def sum_kernel(dims, flux_hbm, vis_hbm, live_ref, a_ref, b_ref, *refs):
    F, T, D, O, _, _ = dims
    upright_ref, refs = (refs[0], refs[1:]) if len(refs) == 8 else (None, refs)
    keep_ref, send_ref, refs = refs[0], refs[1], refs[2:]
    power_ref, refs = (refs[0], refs[1:]) if upright_ref is not None else (None, refs)
    vis_ref, distinct, flux_ref, sems = refs
    rows, cols = vis_ref.shape[3], vis_ref.shape[4]
    row = lax.axis_index("row")
    col = lax.axis_index("col")
    parity = col % 2

    def vis_copy(f):
        return pltpu.make_async_copy(vis_hbm.at[f], vis_ref.at[f], sems.at[f])

    flux_copy = pltpu.make_async_copy(flux_hbm, flux_ref, sems.at[F])
    flux_copy.start()
    ahead = 2 * CHUNK
    for f in range(ahead):
        vis_copy(f).start()
    p = lax.broadcasted_iota(jnp.int32, (rows, cols), 0) + row * rows
    q = lax.broadcasted_iota(jnp.int32, (rows, cols), 1) + col * cols
    distinct[...] = jnp.where(p == q, 0.0, 1.0).astype(jnp.bfloat16)
    group = 8 // T
    blocks = block_mask(2 * D)
    nt = (((1,), (1,)), ((), ()))

    def body(step, upright, start, power):
        highs, lows = [], []
        lives = live_ref[pl.ds(step * 8, 8), :]
        mask = distinct[...]
        for i in range(group):
            f = step * group + i
            scale = column(flux_ref, f, D, cols)
            for t in range(T):
                j = i * T + t
                ft = step * 8 + j
                a, b = a_ref[ft], b_ref[ft]
                first = jnp.where(row == 0, a, b)
                second = jnp.where(row == 0, b, a)
                weight = scale * lives[j : j + 1, :]
                re = join_low(first, second) * weight
                im = join_high(first, second) * weight
                x = jnp.concatenate(
                    [jnp.concatenate([re, -im], axis=1), jnp.concatenate([im, re], axis=1)], axis=0
                )
                high = x.astype(jnp.bfloat16)
                low = (x - high.astype(jnp.float32)).astype(jnp.bfloat16)
                highs.append(high)
                lows.append(low)
                both = jnp.concatenate([high, low], axis=0)
                seen = [vis_ref[f, t, part] * mask for part in range(2)]
                v = lax.dot_general(
                    both, jnp.concatenate(seen, axis=1), nt, preferred_element_type=jnp.float32
                )
                v = v[: 2 * D] + v[2 * D :]
                v0, v1 = v[:, : 2 * O], v[:, 2 * O :]
                even, odd = join_low(v0, v1), join_high(v0, v1)
                keep_ref[step * 9 + j] = jnp.where(parity == 0, even, odd)
                send_ref[step * 9 + j] = jnp.where(parity == 0, odd, even)
                if upright is not None:
                    square = [x.astype(jnp.float32) for x in seen]
                    square = square[0] * square[0] + square[1] * square[1]
                    at = start + j
                    square = square * jnp.broadcast_to(upright[:, at : at + 1], square.shape)
                    square = jnp.sum(square.reshape(rows // 8, 8, cols), axis=0)
                    power = power + square * lives[j : j + 1, :]
        high = jnp.concatenate(highs, axis=0)
        low = jnp.concatenate(lows, axis=0)
        gram = lax.dot_general(high, high, nt, preferred_element_type=jnp.float32)
        gram = gram + lax.dot_general(high, low, nt, preferred_element_type=jnp.float32)
        gram = gram + lax.dot_general(low, high, nt, preferred_element_type=jnp.float32)
        gram = jnp.where(blocks, gram, 0.0)
        folded = gram[: 2 * D]
        for i in range(1, 8):
            folded = folded + gram[i * 2 * D : (i + 1) * 2 * D]
        keep_ref[step * 9 + 8] = folded
        send_ref[step * 9 + 8] = folded
        return power

    def chunk(c, power):
        first = isinstance(c, int)
        if not first:
            for i in range(CHUNK):
                vis_copy(c * CHUNK + i).wait()

        def more():
            for i in range(CHUNK):
                vis_copy(c * CHUNK + ahead + i).start()

        if not first:
            pl.when(c * CHUNK + ahead < F)(more)

        upright = None
        if upright_ref is not None:
            upright = pltpu.roll(upright_ref[...], (2 * O - c * CHUNK * T) % (2 * O), 1)
        for j in range(CHUNK // group):
            if first:
                for i in range(group):
                    vis_copy(j * group + i).wait()
            power = body(c * (CHUNK // group) + j, upright, j * 8, power)
        if first and ahead < F:
            more()
        return power

    flux_copy.wait()
    power = jnp.zeros((8, cols), jnp.float32)
    peeled = 1 if power_ref is not None else 0
    if peeled:
        power = chunk(0, power)
    power = lax.fori_loop(peeled, F // CHUNK, chunk, power)
    if power_ref is not None:
        power = jnp.sum(power, axis=0, keepdims=True)
        power_ref[...] = jnp.where(low_lanes(power.shape), power + swap(power), 0.0)


def residual_kernel(dims, live_ref, extra_ref, power_ref, kept_ref, other_ref, mine_ref, theirs_ref,
                    passed_ref, got_ref,
                    keep_ref, send_ref, scalar_ref):
    F, T, D, O, _, _ = dims
    W = 2 * O
    row = lax.axis_index("row")
    col = lax.axis_index("col")
    near = col // 2 == 0
    away = col // 2 != row
    held = col % 2 != row
    mask = block_mask(2 * D)
    eye = lax.broadcasted_iota(jnp.int32, (2 * D, W), 0) == (
        lax.broadcasted_iota(jnp.int32, (2 * D, W), 1) % (2 * D)
    )
    total = jnp.zeros((2 * D, W), jnp.float32)
    for group in range(F * T // 8):
        gram = kept_ref[group * 9 + 8] + other_ref[group * 9 + 8]
        diagonal = jnp.sum(jnp.where(eye, gram, 0.0), axis=0, keepdims=True)
        keep_ref[F * T, group : group + 1, :] = diagonal
        send_ref[F * T, group : group + 1, :] = diagonal
        spread = jnp.where(mask, jnp.concatenate([gram] * 8, axis=0), 0.0)
        station = []
        for i in range(8):
            ft = group * 8 + i
            a = mine_ref[ft]
            b = jnp.where(away, theirs_ref[ft], jnp.where(held, got_ref[ft], passed_ref[ft]))
            first = jnp.where(near, a, b)
            second = jnp.where(near, b, a)
            station += [join_low(first, second), join_high(first, second)]
        model = jnp.dot(
            spread, jnp.concatenate(station, axis=0), precision=HIGH,
            preferred_element_type=jnp.float32,
        )
        for i in range(8):
            ft = group * 8 + i
            live = live_ref[ft : ft + 1, :]
            v = kept_ref[group * 9 + i] + other_ref[group * 9 + i]
            num = (v - model[i * 2 * D : (i + 1) * 2 * D]) * live
            z = jnp.concatenate(station[2 * i : 2 * i + 2], axis=0)
            total = total + z * (v * live + num)
            low, high = join_low(num[:D], num[D:]), join_high(num[:D], num[D:])
            keep_ref[ft] = jnp.where(near, low, high)
            send_ref[ft] = jnp.where(near, high, low)
    squares = -jnp.sum(total, axis=0, keepdims=True)
    squares = squares + swap(squares)
    scalar = jnp.where(low_lanes(squares.shape), squares, 0.0) + extra_ref[...] + power_ref[...]
    scalar_ref[...] = jnp.broadcast_to(scalar, scalar_ref.shape)


def merge_kernel(dims, keep_ref, come_ref, live_ref, e_ref, g_ref, held_ref, slope_ref,
                 num_ref, den_ref):
    F, T, D, O, _, _ = dims
    W = 2 * O
    shape = (8 * D, W)
    a = lax.broadcasted_iota(jnp.int32, shape, 0)
    b = lax.broadcasted_iota(jnp.int32, shape, 1)
    eye = a // D * (2 * D) + a % D == b
    ones = jnp.ones((W, W), jnp.float32)
    for group in range(F * T // 8):
        diagonal = keep_ref[F * T, group : group + 1, :] + come_ref[F * T, group : group + 1, :]
        spread = jnp.dot(
            jnp.where(eye, diagonal, 0.0), ones, precision=HIGH, preferred_element_type=jnp.float32
        )
        for i in range(8):
            ft = group * 8 + i
            around = live_ref[ft : ft + 1, :] * spread[i * D : (i + 1) * D]
            num = counter_rotated(keep_ref[ft] + come_ref[ft], e_ref[ft])
            num_ref[ft] = num + held_ref[ft] + around * g_ref[ft]
            den_ref[ft] = around + slope_ref[ft]


def update_kernel(dims, last, full, *refs):
    F, T, D, O, _, _ = dims
    scalar_ref, num_ref, den_ref, target_ref, g_ref, other_ref = refs[:6]
    W = 2 * O
    sums = jnp.sum(scalar_ref[...], axis=0, keepdims=True)
    low = low_lanes(sums.shape)
    squares = jnp.sum(jnp.where(low, sums, 0.0), axis=1, keepdims=True)
    samples = jnp.sum(jnp.where(low, 0.0, sums), axis=1, keepdims=True)
    squares = jnp.maximum(squares, 0.0)
    rho = PENALTY * full * (squares / samples + 1e-06)
    rho = jnp.broadcast_to(rho, (D, W))
    for t in range(T):
        acc = [jnp.zeros((D, W), jnp.float32) for _ in range(4)]
        for f in range(F):
            ft = f * T + t
            fresh = (num_ref[ft] + rho * target_ref[ft]) / (den_ref[ft] + rho)
            g = 0.5 * (g_ref[ft] + fresh)
            if last:
                out_ref, total_ref, rhs_ref = refs[6:]
                out_ref[ft] = g
                total = other_ref[ft] + g
                total_ref[ft] = total
                x = place(dims, f)
                for k in range(4):
                    acc[k] = acc[k] + total
                    total = total * x if k < 3 else total
            else:
                g_out, p_out = refs[6:]
                g_out[ft] = g
                p_out[ft] = rotated(g, other_ref[ft])
        if last:
            for k in range(4):
                rhs_ref[k * T + t] = acc[k]


def write_out(dims, value, out_hbm, out_ref, sems):
    F, T, _, O, _, _ = dims
    copies = []
    for part in range(F // CHUNK):
        for f in range(part * CHUNK, (part + 1) * CHUNK):
            for t in range(T):
                x = value(f, t)
                out_ref[f, t, 0] = x[:, :O]
                out_ref[f, t, 1] = x[:, O:]
        at = pl.ds(part * CHUNK, CHUNK)
        copies.append(pltpu.make_async_copy(out_ref.at[at], out_hbm.at[at], sems.at[part]))
        copies[-1].start()
    for copy in copies:
        copy.wait()


def emit_kernel(dims, g_ref, out_hbm, out_ref, sems):
    write_out(dims, lambda f, t: g_ref[f * dims[1] + t], out_hbm, out_ref, sems)


def final_kernel(dims, total_ref, *refs):
    T = dims[1]
    coeffs = [solve(dims, refs[:-3], t) for t in range(T)]
    write_out(
        dims, lambda f, t: total_ref[f * T + t] - curve(coeffs[t], place(dims, f)), *refs[-3:]
    )


def shards(sizes, vis, flags, positions, lmn, flux, gains, duals):
    R, C, Z = sizes
    F, T, _, D, O = gains.shape
    rows, cols = vis.shape[3], vis.shape[4]
    full = flags.shape[2]
    FT, W = F * T, 2 * O
    dims = (F, T, D, O, R, C)
    f32 = jnp.float32
    smem = pl.BlockSpec(memory_space=pltpu.SMEM)
    vmem = pl.BlockSpec(memory_space=pltpu.VMEM)
    hbm = pl.BlockSpec(memory_space=pltpu.HBM)

    def array(*shape):
        return jax.ShapeDtypeStruct(shape, f32)

    def far(x):
        return pltpu.with_memory_space_constraint(x, pltpu.HBM)

    def call(kernel, outs, scalars, arrays, scratch=()):
        return pl.pallas_call(
            kernel,
            out_shape=outs,
            in_specs=[smem] * len(scalars) + [vmem] * len(arrays),
            out_specs=[vmem] * len(outs),
            scratch_shapes=list(scratch),
            compiler_params=LIMIT,
        )(*scalars, *arrays)

    def where(r, c, z):
        return (r * C + c) * Z + z

    def permute(x, move, some=lambda r, c: True):
        pairs = [
            (where(r, c, z), where(*move(r, c, z)))
            for r in range(R) for c in range(C) for z in range(Z) if some(r, c)
        ]
        return lax.ppermute(x, AXES, pairs)

    def gather(x, m):
        return permute(x, lambda r, c, z: (((r * C + c) % R + m) % R, (r * C + c) // R, z))

    def bands(x):
        return [x] + [permute(x, lambda r, c, z, k=k: (r, c, z ^ k)) for k in range(1, Z)]

    whole, line, fit = array(FT, D, W), array(FT + 1, D, W), array(4 * T, D, W)
    pair, text = array(FT // 8 * 9, 2 * D, W), array(1, W)
    flux_t = flux.T
    rot, g, p = pl.pallas_call(
        functools.partial(start_kernel, dims),
        out_shape=[whole] * 3,
        in_specs=[hbm] * 3,
        out_specs=[vmem] * 3,
        scratch_shapes=[
            pltpu.VMEM((3, T, full), f32),
            pltpu.SMEM(lmn.shape, f32),
            pltpu.VMEM(gains.shape, f32),
            pltpu.SemaphoreType.DMA((3,)),
        ],
        compiler_params=LIMIT,
        name="start",
    )(far(positions.transpose(1, 0, 2)), far(lmn), far(gains))
    for step in range(ITERS):
        last = step == ITERS - 1
        got = [gather(p, m) for m in range(R)]
        if step == 0:
            (live_col, live_half, live_own, upright, u, rhs, held, slope, samples, extra) = (
                pl.pallas_call(
                    functools.partial(setup_kernel, dims, cols),
                    out_shape=[
                        array(FT, cols), array(FT, W), array(FT, W), array(rows, W), whole,
                        fit, whole, whole, text, text,
                    ],
                    in_specs=[hbm] * 3 + [vmem],
                    out_specs=[vmem] * 10,
                    scratch_shapes=[
                        pltpu.SMEM(flux_t.shape, f32),
                        pltpu.VMEM(flags.shape, flags.dtype),
                        pltpu.VMEM(duals.shape, f32),
                        pltpu.SemaphoreType.DMA((3,)),
                    ],
                    compiler_params=LIMIT,
                    name="setup",
                )(far(flux_t), far(flags), far(duals), g)
            )
        else:
            rhs, held, slope, extra = call(
                functools.partial(again_kernel, dims),
                [fit, whole, whole, text], [flux_t], [samples, live_own, u, g],
            )
        rhs_near = permute(rhs, lambda r, c, z: (r, c, z ^ 1))
        theirs = permute(p, lambda r, c, z: (r, c ^ 2, z), lambda r, c: r == c // 2)
        more = [] if step else [upright]
        keep, send, *found = pl.pallas_call(
            functools.partial(sum_kernel, dims),
            out_shape=[pair, pair] + ([] if step else [array(1, cols)]),
            in_specs=[hbm] * 2 + [vmem] * (3 + len(more)),
            out_specs=[vmem] * (2 + len(more)),
            scratch_shapes=[
                pltpu.VMEM(vis.shape, vis.dtype),
                pltpu.VMEM((rows, cols), vis.dtype),
                pltpu.SMEM(flux_t.shape, f32),
                pltpu.SemaphoreType.DMA((F + 1,)),
            ],
            compiler_params=LIMIT,
            name="sums",
        )(far(flux_t), far(vis), live_col, *got, *more)
        power = power if step else found[0]
        passed = permute(
            got[0], lambda r, c, z: (r, c ^ 1, z), lambda r, c: c == 3 * r + (1 - 2 * r)
        )
        other = permute(send, lambda r, c, z: (r, c ^ 1, z))
        (rhs,) = call(add_kernel, [fit], [], [rhs, rhs_near])
        rhs_far = permute(rhs, lambda r, c, z: (r, c, z ^ 2))
        keep, send, scalar = call(
            functools.partial(residual_kernel, dims), [line, line, array(R * C * Z, W)],
            [], [live_half, extra, power, keep, other, p, theirs, passed, got[1]],
        )
        come = permute(send, lambda r, c, z: (r, c ^ 2, z))
        scalar = lax.all_to_all(scalar, AXES, 0, 0, tiled=True)
        target = call(
            functools.partial(target_kernel, dims, step == 0),
            [whole] * (1 if step == 0 else 2), [], [u, g, rhs, rhs_far],
        )
        num, den = call(
            functools.partial(merge_kernel, dims), [whole, whole], [],
            [keep, come, live_own, rot, g, held, slope],
        )
        update = functools.partial(update_kernel, dims, last, float(full))
        arrays = [scalar, num, den, target[0], g]
        if last:
            g, total, rhs = call(
                update, [whole, whole, fit], [],
                arrays + [target[1]],
            )
        else:
            g, p = call(update, [whole, whole], [], arrays + [rot])

    def write(kernel, arrays):
        return pl.pallas_call(
            functools.partial(kernel, dims),
            out_shape=array(*gains.shape),
            in_specs=[vmem] * len(arrays),
            out_specs=hbm,
            scratch_shapes=[pltpu.VMEM(gains.shape, f32), pltpu.SemaphoreType.DMA((F // CHUNK,))],
            compiler_params=LIMIT,
        )(*arrays)

    rhs_all = bands(rhs)
    gain = write(emit_kernel, [g])
    dual = write(final_kernel, [total, *rhs_all])
    return (gain, dual)


def basis(count):
    grid = 2.0 * jnp.arange(count, dtype=jnp.float32) / (count - 1) - 1.0
    return jnp.stack([grid**power for power in range(4)], axis=1)


def rotate(positions, lmn, freq):
    geometry = jnp.einsum("tks,kd->tds", positions, lmn, precision=HIGH)
    angle = 2.0 * math.pi * freq[:, None, None, None] * geometry[None]
    return (jnp.cos(angle), -jnp.sin(angle))


def complex_mul(a_re, a_im, b_re, b_im):
    return (a_re * b_re - a_im * b_im, a_re * b_im + a_im * b_re)


def solve_fit(rhs, total_f):
    full = basis(total_f)
    gram = jnp.dot(full.T, full, precision=HIGH)
    factor = jnp.linalg.cholesky(gram)
    flat = rhs.reshape(rhs.shape[0], -1)
    return jax.scipy.linalg.cho_solve((factor, True), flat).reshape(rhs.shape)


def plain_shards(vis, flags, positions, lmn, flux, gains, duals):
    width = gains.shape[0]
    total_f = width * lax.axis_size("band")
    first = lax.axis_index("band") * width
    local_basis = lax.dynamic_slice_in_dim(basis(total_f), first, width, 0)
    freq = 1.0 + (first + jnp.arange(width, dtype=jnp.int32)).astype(jnp.float32) / total_f
    row_index = lax.axis_index("row")
    col_index = lax.axis_index("col")
    row_count = vis.shape[3]
    col_count = vis.shape[4]
    owned = gains.shape[4]
    own_start = (row_index * lax.axis_size("col") + col_index) * owned
    row_start = row_index * row_count
    col_start = col_index * col_count
    own_cos, own_sin = rotate(lax.dynamic_slice_in_dim(positions, own_start, owned, 2), lmn, freq)
    row_cos, row_sin = rotate(
        lax.dynamic_slice_in_dim(positions, row_start, row_count, 2), lmn, freq
    )
    col_cos, col_sin = rotate(
        lax.dynamic_slice_in_dim(positions, col_start, col_count, 2), lmn, freq
    )
    all_live = flags.astype(jnp.float32)
    row_live = lax.dynamic_slice_in_dim(all_live, row_start, row_count, 2)
    col_live = lax.dynamic_slice_in_dim(all_live, col_start, col_count, 2)
    own_live = lax.dynamic_slice_in_dim(all_live, own_start, owned, 2)
    row_ids = row_start + jnp.arange(row_count, dtype=jnp.int32)
    col_ids = col_start + jnp.arange(col_count, dtype=jnp.int32)
    distinct = (row_ids[:, None] != col_ids[None, :]).astype(jnp.float32)
    weight = row_live[:, :, :, None] * col_live[:, :, None, :] * distinct
    vis_re = vis[:, :, 0].astype(jnp.float32)
    vis_im = vis[:, :, 1].astype(jnp.float32)
    scale = flux[:, None, :, None]

    def fit(gain, dual):
        rhs = jnp.einsum("fk,ftcds->ktcds", local_basis, gain + dual, precision=HIGH)
        return solve_fit(lax.psum(rhs, "band"), total_f)

    gain, dual = (gains, duals)
    coeffs = fit(gain, dual)
    for _ in range(ITERS):
        target = jnp.einsum("fk,ktcds->ftcds", local_basis, coeffs, precision=HIGH) - dual
        every = lax.all_gather(gain, ("row", "col"), axis=4, tiled=True)
        row_gain = lax.dynamic_slice_in_dim(every, row_start, row_count, 4)
        col_gain = lax.dynamic_slice_in_dim(every, col_start, col_count, 4)
        row_re, row_im = complex_mul(row_gain[:, :, 0], row_gain[:, :, 1], row_cos, row_sin)
        col_re, col_im = complex_mul(col_gain[:, :, 0], col_gain[:, :, 1], col_cos, col_sin)
        col_re = scale * col_re
        col_im = scale * col_im
        model_re = jnp.einsum("ftdp,ftdq->ftpq", row_re, col_re, precision=HIGH) + jnp.einsum(
            "ftdp,ftdq->ftpq", row_im, col_im, precision=HIGH
        )
        model_im = jnp.einsum("ftdp,ftdq->ftpq", row_im, col_re, precision=HIGH) - jnp.einsum(
            "ftdp,ftdq->ftpq", row_re, col_im, precision=HIGH
        )
        resid_re = weight * (vis_re - model_re)
        resid_im = weight * (vis_im - model_im)
        squares, samples = lax.psum(
            (jnp.sum(resid_re * resid_re + resid_im * resid_im), jnp.sum(weight)),
            ("row", "col", "band"),
        )
        sum_re = jnp.einsum("ftpq,ftdq->ftdp", resid_re, col_re, precision=HIGH) - jnp.einsum(
            "ftpq,ftdq->ftdp", resid_im, col_im, precision=HIGH
        )
        sum_im = jnp.einsum("ftpq,ftdq->ftdp", resid_re, col_im, precision=HIGH) + jnp.einsum(
            "ftpq,ftdq->ftdp", resid_im, col_re, precision=HIGH
        )
        pairs = lax.psum_scatter(
            jnp.stack([sum_re, sum_im], axis=2), "col", scatter_dimension=4, tiled=True
        )
        every_mag = every[:, :, 0] * every[:, :, 0] + every[:, :, 1] * every[:, :, 1]
        total_mag = jnp.einsum("ftds,fts->ftd", every_mag, all_live, precision=HIGH)
        own_mag = gain[:, :, 0] * gain[:, :, 0] + gain[:, :, 1] * gain[:, :, 1]
        own_flag = own_live[:, :, None, :]
        own_denom = (scale * scale * own_flag * (total_mag[:, :, :, None] - own_flag * own_mag))[
            :, :, None
        ]
        num_re, num_im = complex_mul(own_cos, -own_sin, pairs[:, :, 0], pairs[:, :, 1])
        numer = jnp.stack([num_re, num_im], axis=2)
        rho = PENALTY * flags.shape[2] * (squares / samples + 1e-06)
        fresh = (numer + own_denom * gain + rho * target) / (own_denom + rho)
        gain = 0.5 * (gain + fresh)
        coeffs = fit(gain, dual)
        dual = dual + gain - jnp.einsum("fk,ktcds->ftcds", local_basis, coeffs, precision=HIGH)
    return (gain, dual)


def solution(mesh):
    sizes = tuple(mesh.shape[a] for a in AXES)

    fits = sizes == (2, 4, 4)

    def body(*args):
        gains = args[5]
        if fits and gains.shape[3:] == (8, 64) and 8 % gains.shape[1] == 0:
            return shards(sizes, *args)
        return plain_shards(*args)

    return jax.shard_map(
        body,
        mesh=mesh,
        in_specs=(
            P("band", None, None, "row", "col"),
            P("band", None, None),
            P(),
            P(),
            P("band", None),
            P("band", None, None, None, ("row", "col")),
            P("band", None, None, None, ("row", "col")),
        ),
        out_specs=(
            P("band", None, None, None, ("row", "col")),
            P("band", None, None, None, ("row", "col")),
        ),
        check_vma=False,
    )
```

```python
import functools
import math

import jax
import jax.numpy as jnp
import numpy as np
from jax import lax
from jax.experimental import pallas as pl
from jax.experimental.pallas import tpu as pltpu
from jax.sharding import PartitionSpec as P

ITERS = 2
PENALTY = 0.05
HIGH = lax.Precision.HIGHEST
AXES = ("row", "col", "band")
CHUNK = 4
HEAD = 2
LIMIT = pltpu.CompilerParams(vmem_limit_bytes=16 * 2**20)


def swap(x):
    half = x.shape[-1] // 2
    return pltpu.roll(x, half, x.ndim - 1)


def low_lanes(shape):
    return lax.broadcasted_iota(jnp.int32, shape, len(shape) - 1) < shape[-1] // 2


def join_low(a, b):
    return jnp.where(low_lanes(a.shape), a, swap(b))


def join_high(a, b):
    return jnp.where(low_lanes(a.shape), swap(a), b)


def column(ref, index, dirs, lanes):
    rows = lax.broadcasted_iota(jnp.int32, (dirs, lanes), 0)
    out = jnp.full((dirs, lanes), ref[0, index], jnp.float32)
    for d in range(1, dirs):
        out = jnp.where(rows == d, ref[d, index], out)
    return out


def cos_turns(r):
    t = 0.25 - jnp.abs(r)
    x = t * t
    coef = [(-1) ** n * (2.0 * math.pi) ** (2 * n + 1) / math.factorial(2 * n + 1) for n in range(7)]
    out = jnp.full_like(x, coef[-1])
    for c in coef[-2::-1]:
        out = out * x + c
    return out * t


def rotated(g, e):
    low = low_lanes(e.shape)
    turned = swap(e)
    cos2 = jnp.where(low, e, turned)
    sin2 = jnp.where(low, -turned, e)
    return g * cos2 + swap(g) * sin2


def counter_rotated(g, e):
    low = low_lanes(e.shape)
    turned = swap(e)
    cos2 = jnp.where(low, e, turned)
    sin2 = jnp.where(low, -turned, e)
    return g * cos2 - swap(g) * sin2


def start_kernel(dims, pos_hbm, lmn_hbm, gains_hbm, e_ref, g_ref, p_ref, pos_ref, lmn_ref, gains_ref, sems):
    F, T, D, O, R, C = dims
    W = 2 * O
    copies = [
        pltpu.make_async_copy(pos_hbm, pos_ref, sems.at[0]),
        pltpu.make_async_copy(lmn_hbm, lmn_ref, sems.at[1]),
        pltpu.make_async_copy(gains_hbm, gains_ref, sems.at[2]),
    ]
    for copy in copies:
        copy.start()
    own = lax.axis_index("row") * C + lax.axis_index("col")
    first = lax.axis_index("band") * F
    low = low_lanes((D, W))
    rows = lax.broadcasted_iota(jnp.int32, (D, W), 0)
    shift = jnp.where(low, 0.0, 0.25)
    copies[0].wait()
    copies[1].wait()
    pos = pos_ref[:, :, :O]
    for k in range(1, R * C):
        pos = jnp.where(own == k, pos_ref[:, :, k * O : (k + 1) * O], pos)
    pos = jnp.concatenate([pos, pos], axis=-1)
    geometry = []
    for t in range(T):
        total = jnp.zeros((D, W), jnp.float32)
        for k in range(3):
            lm = jnp.full((D, W), lmn_ref[k, 0], jnp.float32)
            for d in range(1, D):
                lm = jnp.where(rows == d, lmn_ref[k, d], lm)
            total = total + lm * pos[k, t : t + 1, :]
        geometry.append(total)
    total_f = F * lax.axis_size("band")
    for f in range(F):
        nu = 1.0 + (first + f).astype(jnp.float32) * (1.0 / total_f)
        for t in range(T):
            ft = f * T + t
            turns = nu * geometry[t]
            r = turns - jnp.round(turns) + shift
            e_ref[ft] = cos_turns(r - jnp.round(r))
    copies[2].wait()
    for f in range(F):
        for t in range(T):
            ft = f * T + t
            g = jnp.concatenate([gains_ref[f, t, 0], gains_ref[f, t, 1]], axis=-1)
            g_ref[ft] = g
            p_ref[ft] = rotated(g, e_ref[ft])


def own_terms(dims, flux_ref, live_ref, g_ref, held_ref, slope_ref):
    F, T, D, O, _, _ = dims
    total = jnp.zeros((1, 2 * O), jnp.float32)
    for f in range(F):
        flux = column(flux_ref, f, D, 2 * O)
        for t in range(T):
            ft = f * T + t
            live = live_ref[ft : ft + 1, :]
            g = g_ref[ft]
            power = g * g
            power = (power + swap(power)) * flux
            own = jnp.sum(power, axis=0, keepdims=True)
            total = total + live * own * own
            power = power * flux
            slope_ref[ft] = -live * power
            held_ref[ft] = live * (own * flux - power) * g
    return total


def place(dims, f):
    F = dims[0]
    full = F * lax.axis_size("band")
    at = (lax.axis_index("band") * F + f).astype(jnp.float32)
    return at * (2.0 / (full - 1)) - 1.0


def fit_sums(dims, value, rhs_ref):
    F, T, D, O, _, _ = dims
    for t in range(T):
        acc = [jnp.zeros((D, 2 * O), jnp.float32) for _ in range(4)]
        for f in range(F):
            total = value(f, t)
            x = place(dims, f)
            for k in range(4):
                acc[k] = acc[k] + total
                total = total * x if k < 3 else total
        for k in range(4):
            rhs_ref[k * T + t] = acc[k]


def solve(dims, rhs_refs, t):
    T = dims[1]
    full = dims[0] * lax.axis_size("band")
    grid = 2.0 * np.arange(full, dtype=np.float64) / (full - 1) - 1.0
    basis = np.stack([grid**k for k in range(4)], axis=1)
    inverse = np.linalg.inv(basis.T @ basis)
    rhs = [sum(ref[k * T + t] for ref in rhs_refs) for k in range(4)]
    out = []
    for k in range(4):
        total = float(inverse[k, 0]) * rhs[0]
        for j in range(1, 4):
            total = total + float(inverse[k, j]) * rhs[j]
        out.append(total)
    return out


def curve(coeffs, x):
    return coeffs[0] + x * (coeffs[1] + x * (coeffs[2] + x * coeffs[3]))


def pick(index, parts):
    out = parts[0]
    for k in range(1, len(parts)):
        out = jnp.where(index == k, parts[k], out)
    return out


def setup_kernel(dims, cols, flux_hbm, flags_hbm, duals_hbm, vis_hbm, g_ref, live_col_ref, live_half_ref,
                 live_own_ref, upright_ref, u_ref, rhs_ref, held_ref, slope_ref, samples_ref,
                 extra_ref, head_ref, flux_ref, flags_ref, duals_ref, sems):
    F, T, _, O, R, C = dims
    W, rows, full = 2 * O, C * O, flags_ref.shape[2]
    row = lax.axis_index("row")
    col = lax.axis_index("col")
    copies = [
        pltpu.make_async_copy(flags_hbm, flags_ref, sems.at[0]),
        pltpu.make_async_copy(duals_hbm, duals_ref, sems.at[1]),
        pltpu.make_async_copy(flux_hbm, flux_ref, sems.at[2]),
        pltpu.make_async_copy(vis_hbm.at[pl.ds(0, HEAD)], head_ref, sems.at[3]),
    ]
    for copy in copies:
        copy.start()
    copies[0].wait()
    counts = jnp.zeros((T, full), jnp.float32)
    stacked = []
    for f in range(F):
        live = flags_ref[f].astype(jnp.float32)
        at = slice(f * T, (f + 1) * T)
        mine = pick(row, [live[:, r * rows : (r + 1) * rows] for r in range(R)])
        blocks = [mine[:, c * O : (c + 1) * O] for c in range(C)]
        live_col_ref[at, :] = pick(col, [live[:, c * cols : (c + 1) * cols] for c in range(C)])
        even = jnp.concatenate([blocks[0], blocks[2]], axis=1)
        odd = jnp.concatenate([blocks[1], blocks[3]], axis=1)
        live_half_ref[at, :] = pick(col % 2, [even, odd])
        own = pick(col, blocks)
        live_own_ref[at, :] = jnp.concatenate([own, own], axis=1)
        stacked.append(mine)
        count = jnp.sum(live, axis=1, keepdims=True)
        counts = counts + live * (count - 1.0)
    stacked = jnp.concatenate(stacked + [jnp.zeros((W - F * T, rows), jnp.float32)], axis=0)
    upright_ref[...] = jnp.transpose(stacked)
    samples = jnp.sum(counts, axis=0, keepdims=True)
    samples = jnp.sum(samples, axis=1, keepdims=True) / (R * C)
    copies[1].wait()
    copies[2].wait()
    for f in range(F):
        for t in range(T):
            u_ref[f * T + t] = jnp.concatenate([duals_ref[f, t, 0], duals_ref[f, t, 1]], axis=-1)
    fit_sums(dims, lambda f, t: u_ref[f * T + t] + g_ref[f * T + t], rhs_ref)
    own = own_terms(dims, flux_ref, live_own_ref, g_ref, held_ref, slope_ref)
    lanes = lax.broadcasted_iota(jnp.int32, own.shape, 1)
    samples = jnp.where(lanes == O, samples, 0.0)
    samples_ref[...] = samples
    extra_ref[...] = samples - jnp.where(low_lanes(own.shape), own, 0.0)
    copies[3].wait()


def again_kernel(dims, flux_ref, vis_hbm, samples_ref, live_ref, u_ref, g_ref,
                 rhs_ref, held_ref, slope_ref, extra_ref, head_ref, sem):
    _, T, _, _, _, _ = dims
    copy = pltpu.make_async_copy(vis_hbm.at[pl.ds(0, HEAD)], head_ref, sem.at[0])
    copy.start()
    fit_sums(dims, lambda f, t: u_ref[f * T + t] + g_ref[f * T + t], rhs_ref)
    own = own_terms(dims, flux_ref, live_ref, g_ref, held_ref, slope_ref)
    extra_ref[...] = samples_ref[...] - jnp.where(low_lanes(own.shape), own, 0.0)
    copy.wait()


def add_kernel(a_ref, b_ref, out_ref):
    out_ref[...] = a_ref[...] + b_ref[...]


def target_kernel(dims, first_pass, u_ref, g_ref, *refs):
    F, T, _, _, _, _ = dims
    rhs_refs, outs = refs[:2], refs[2:]
    for t in range(T):
        coeffs = solve(dims, rhs_refs, t)
        for f in range(F):
            ft = f * T + t
            smooth = curve(coeffs, place(dims, f))
            u = u_ref[ft]
            if not first_pass:
                u = u + g_ref[ft] - smooth
                outs[1][ft] = u
            outs[0][ft] = smooth - u


def block_mask(size):
    shape = (8 * size, 8 * size)
    a = lax.broadcasted_iota(jnp.int32, shape, 0) // size
    b = lax.broadcasted_iota(jnp.int32, shape, 1) // size
    return a == b


def sum_kernel(dims, flux_hbm, vis_hbm, live_ref, a_ref, b_ref, head_ref, *refs):
    F, T, D, O, _, _ = dims
    upright_ref, refs = (refs[0], refs[1:]) if len(refs) == 9 else (None, refs)
    keep_ref, send_ref, refs = refs[0], refs[1], refs[2:]
    power_ref, refs = (refs[0], refs[1:]) if upright_ref is not None else (None, refs)
    vis_ref, distinct, flux_ref, sems = refs[:4]
    rows, cols = vis_ref.shape[3], vis_ref.shape[4]
    row = lax.axis_index("row")
    col = lax.axis_index("col")
    parity = col % 2

    def vis_copy(f):
        return pltpu.make_async_copy(vis_hbm.at[f], vis_ref.at[f], sems.at[f])

    flux_copy = pltpu.make_async_copy(flux_hbm, flux_ref, sems.at[F])
    flux_copy.start()
    ahead = 2 * CHUNK
    for f in range(HEAD, ahead):
        vis_copy(f).start()
    p = lax.broadcasted_iota(jnp.int32, (rows, cols), 0) + row * rows
    q = lax.broadcasted_iota(jnp.int32, (rows, cols), 1) + col * cols
    distinct[...] = jnp.where(p == q, 0.0, 1.0).astype(jnp.bfloat16)
    group = 8 // T
    blocks = block_mask(2 * D)
    nt = (((1,), (1,)), ((), ()))

    def body(step, upright, start, power, source):
        highs, lows = [], []
        lives = live_ref[pl.ds(step * 8, 8), :]
        mask = distinct[...]
        for i in range(group):
            f = step * group + i
            scale = column(flux_ref, f, D, cols)
            for t in range(T):
                j = i * T + t
                ft = step * 8 + j
                a, b = a_ref[ft], b_ref[ft]
                first = jnp.where(row == 0, a, b)
                second = jnp.where(row == 0, b, a)
                weight = scale * lives[j : j + 1, :]
                re = join_low(first, second) * weight
                im = join_high(first, second) * weight
                x = jnp.concatenate(
                    [jnp.concatenate([re, -im], axis=1), jnp.concatenate([im, re], axis=1)], axis=0
                )
                high = x.astype(jnp.bfloat16)
                low = (x - high.astype(jnp.float32)).astype(jnp.bfloat16)
                highs.append(high)
                lows.append(low)
                both = jnp.concatenate([high, low], axis=0)
                seen = [source[f, t, part] * mask for part in range(2)]
                v = lax.dot_general(
                    both, jnp.concatenate(seen, axis=1), nt, preferred_element_type=jnp.float32
                )
                v = v[: 2 * D] + v[2 * D :]
                v0, v1 = v[:, : 2 * O], v[:, 2 * O :]
                even, odd = join_low(v0, v1), join_high(v0, v1)
                keep_ref[step * 9 + j] = jnp.where(parity == 0, even, odd)
                send_ref[step * 9 + j] = jnp.where(parity == 0, odd, even)
                if upright is not None:
                    square = [x.astype(jnp.float32) for x in seen]
                    square = square[0] * square[0] + square[1] * square[1]
                    at = start + j
                    square = square * jnp.broadcast_to(upright[:, at : at + 1], square.shape)
                    square = jnp.sum(square.reshape(rows // 8, 8, cols), axis=0)
                    power = power + square * lives[j : j + 1, :]
        high = jnp.concatenate(highs, axis=0)
        low = jnp.concatenate(lows, axis=0)
        gram = lax.dot_general(high, high, nt, preferred_element_type=jnp.float32)
        gram = gram + lax.dot_general(high, low, nt, preferred_element_type=jnp.float32)
        gram = gram + lax.dot_general(low, high, nt, preferred_element_type=jnp.float32)
        gram = jnp.where(blocks, gram, 0.0)
        folded = gram[: 2 * D]
        for i in range(1, 8):
            folded = folded + gram[i * 2 * D : (i + 1) * 2 * D]
        keep_ref[step * 9 + 8] = folded
        send_ref[step * 9 + 8] = folded
        return power

    def roll_to(c):
        if upright_ref is None:
            return None
        upright = refs[4]
        upright[...] = pltpu.roll(upright_ref[...], (2 * O - c * CHUNK * T) % (2 * O), 1)
        return upright

    def chunk(c, power):
        for i in range(CHUNK):
            vis_copy(c * CHUNK + i).wait()

        @pl.when(c * CHUNK + ahead < F)
        def _():
            for i in range(CHUNK):
                vis_copy(c * CHUNK + ahead + i).start()

        upright = roll_to(c)
        for j in range(CHUNK // group):
            power = body(c * (CHUNK // group) + j, upright, j * 8, power, vis_ref)
        return power

    flux_copy.wait()
    power = jnp.zeros((8, cols), jnp.float32)
    upright = roll_to(0)
    for j in range(CHUNK // group):
        inside = (j + 1) * group <= HEAD
        if not inside:
            for i in range(group):
                vis_copy(j * group + i).wait()
        power = body(j, upright, j * 8, power, head_ref if inside else vis_ref)
    for i in range(CHUNK):
        vis_copy(ahead + i).start()
    power = lax.fori_loop(1, F // CHUNK, chunk, power)
    if power_ref is not None:
        power = jnp.sum(power, axis=0, keepdims=True)
        power_ref[...] = jnp.where(low_lanes(power.shape), power + swap(power), 0.0)


def residual_kernel(dims, live_ref, extra_ref, power_ref, kept_ref, other_ref, mine_ref, theirs_ref,
                    passed_ref, got_ref, keep_ref, send_ref, scalar_hbm, num_ref, scalar_ref, sem):
    F, T, D, O, _, _ = dims
    W = 2 * O
    row = lax.axis_index("row")
    col = lax.axis_index("col")
    near = col // 2 == 0
    away = col // 2 != row
    held = col % 2 != row
    mask = block_mask(2 * D)
    eye = lax.broadcasted_iota(jnp.int32, (2 * D, W), 0) == (
        lax.broadcasted_iota(jnp.int32, (2 * D, W), 1) % (2 * D)
    )

    def body(group, total):
        gram = kept_ref[group * 9 + 8] + other_ref[group * 9 + 8]
        diagonal = jnp.sum(jnp.where(eye, gram, 0.0), axis=0, keepdims=True)
        keep_ref[F * T, pl.ds(group, 1), :] = diagonal
        send_ref[F * T, pl.ds(group, 1), :] = diagonal
        spread = jnp.where(mask, jnp.concatenate([gram] * 8, axis=0), 0.0)
        station = []
        for i in range(8):
            ft = group * 8 + i
            a = mine_ref[ft]
            b = jnp.where(away, theirs_ref[ft], jnp.where(held, got_ref[ft], passed_ref[ft]))
            first = jnp.where(near, a, b)
            second = jnp.where(near, b, a)
            station += [join_low(first, second), join_high(first, second)]
        model = jnp.dot(
            spread, jnp.concatenate(station, axis=0), precision=HIGH,
            preferred_element_type=jnp.float32,
        )
        lives = live_ref[pl.ds(group * 8, 8), :]
        for i in range(8):
            ft = group * 8 + i
            live = lives[i : i + 1, :]
            v = kept_ref[group * 9 + i] + other_ref[group * 9 + i]
            num = (v - model[i * 2 * D : (i + 1) * 2 * D]) * live
            z = jnp.concatenate(station[2 * i : 2 * i + 2], axis=0)
            total = total + z * (v * live + num)
            num_ref[ft] = num
        return total

    total = jnp.zeros((2 * D, W), jnp.float32)
    for group in range(F * T // 8):
        total = body(group, total)
    squares = -jnp.sum(total, axis=0, keepdims=True)
    squares = squares + swap(squares)
    scalar = jnp.where(low_lanes(squares.shape), squares, 0.0) + extra_ref[...] + power_ref[...]
    scalar_ref[...] = jnp.broadcast_to(scalar, scalar_ref.shape)
    copy = pltpu.make_async_copy(scalar_ref, scalar_hbm, sem.at[0])
    copy.start()
    for ft in range(F * T):
        num = num_ref[ft]
        low, high = join_low(num[:D], num[D:]), join_high(num[:D], num[D:])
        keep_ref[ft] = jnp.where(near, low, high)
        send_ref[ft] = jnp.where(near, high, low)
    copy.wait()


def merge_kernel(dims, keep_ref, come_ref, live_ref, e_ref, g_ref, held_ref, slope_ref,
                 num_ref, den_ref):
    F, T, D, O, _, _ = dims
    W = 2 * O
    shape = (8 * D, W)
    a = lax.broadcasted_iota(jnp.int32, shape, 0)
    b = lax.broadcasted_iota(jnp.int32, shape, 1)
    eye = a // D * (2 * D) + a % D == b
    ones = jnp.ones((W, W), jnp.float32)
    for group in range(F * T // 8):
        diagonal = keep_ref[F * T, group : group + 1, :] + come_ref[F * T, group : group + 1, :]
        spread = jnp.dot(
            jnp.where(eye, diagonal, 0.0), ones, precision=HIGH, preferred_element_type=jnp.float32
        )
        for i in range(8):
            ft = group * 8 + i
            around = live_ref[ft : ft + 1, :] * spread[i * D : (i + 1) * D]
            num = counter_rotated(keep_ref[ft] + come_ref[ft], e_ref[ft])
            num_ref[ft] = num + held_ref[ft] + around * g_ref[ft]
            den_ref[ft] = around + slope_ref[ft]


def update_kernel(dims, last, full, *refs):
    F, T, D, O, _, _ = dims
    scalar_ref, num_ref, den_ref, target_ref, g_ref, other_ref = refs[:6]
    W = 2 * O
    sums = jnp.sum(scalar_ref[...], axis=0, keepdims=True)
    low = low_lanes(sums.shape)
    squares = jnp.sum(jnp.where(low, sums, 0.0), axis=1, keepdims=True)
    samples = jnp.sum(jnp.where(low, 0.0, sums), axis=1, keepdims=True)
    squares = jnp.maximum(squares, 0.0)
    rho = PENALTY * full * (squares / samples + 1e-06)
    rho = jnp.broadcast_to(rho, (D, W))
    for t in range(T):
        acc = [jnp.zeros((D, W), jnp.float32) for _ in range(4)]
        for f in range(F):
            ft = f * T + t
            fresh = (num_ref[ft] + rho * target_ref[ft]) / (den_ref[ft] + rho)
            g = 0.5 * (g_ref[ft] + fresh)
            if last:
                out_ref, total_ref, rhs_ref = refs[6:]
                out_ref[ft] = g
                total = other_ref[ft] + g
                total_ref[ft] = total
                x = place(dims, f)
                for k in range(4):
                    acc[k] = acc[k] + total
                    total = total * x if k < 3 else total
            else:
                g_out, p_out = refs[6:]
                g_out[ft] = g
                p_out[ft] = rotated(g, other_ref[ft])
        if last:
            for k in range(4):
                rhs_ref[k * T + t] = acc[k]


def write_out(dims, value, out_hbm, out_ref, sems):
    F, T, _, O, _, _ = dims
    copies = []
    for part in range(F // CHUNK):
        for f in range(part * CHUNK, (part + 1) * CHUNK):
            for t in range(T):
                x = value(f, t)
                out_ref[f, t, 0] = x[:, :O]
                out_ref[f, t, 1] = x[:, O:]
        at = pl.ds(part * CHUNK, CHUNK)
        copies.append(pltpu.make_async_copy(out_ref.at[at], out_hbm.at[at], sems.at[part]))
        copies[-1].start()
    for copy in copies:
        copy.wait()


def emit_kernel(dims, g_ref, out_hbm, out_ref, sems):
    write_out(dims, lambda f, t: g_ref[f * dims[1] + t], out_hbm, out_ref, sems)


def final_kernel(dims, total_ref, *refs):
    T = dims[1]
    coeffs = [solve(dims, refs[:-3], t) for t in range(T)]
    write_out(
        dims, lambda f, t: total_ref[f * T + t] - curve(coeffs[t], place(dims, f)), *refs[-3:]
    )


def shards(sizes, vis, flags, positions, lmn, flux, gains, duals):
    R, C, Z = sizes
    F, T, _, D, O = gains.shape
    rows, cols = vis.shape[3], vis.shape[4]
    full = flags.shape[2]
    FT, W = F * T, 2 * O
    dims = (F, T, D, O, R, C)
    f32 = jnp.float32
    smem = pl.BlockSpec(memory_space=pltpu.SMEM)
    vmem = pl.BlockSpec(memory_space=pltpu.VMEM)
    hbm = pl.BlockSpec(memory_space=pltpu.HBM)

    def array(*shape):
        return jax.ShapeDtypeStruct(shape, f32)

    def far(x):
        return pltpu.with_memory_space_constraint(x, pltpu.HBM)

    def call(kernel, outs, scalars, arrays, scratch=()):
        return pl.pallas_call(
            kernel,
            out_shape=outs,
            in_specs=[smem] * len(scalars) + [vmem] * len(arrays),
            out_specs=[vmem] * len(outs),
            scratch_shapes=list(scratch),
            compiler_params=LIMIT,
        )(*scalars, *arrays)

    def where(r, c, z):
        return (r * C + c) * Z + z

    def permute(x, move, some=lambda r, c: True):
        pairs = [
            (where(r, c, z), where(*move(r, c, z)))
            for r in range(R) for c in range(C) for z in range(Z) if some(r, c)
        ]
        return lax.ppermute(x, AXES, pairs)

    def gather(x, m):
        return permute(x, lambda r, c, z: (((r * C + c) % R + m) % R, (r * C + c) // R, z))

    def bands(x):
        return [x] + [permute(x, lambda r, c, z, k=k: (r, c, z ^ k)) for k in range(1, Z)]

    whole, line, fit = array(FT, D, W), array(FT + 1, D, W), array(4 * T, D, W)
    pair, text = array(FT // 8 * 9, 2 * D, W), array(1, W)
    flux_t = flux.T
    start = jax.ShapeDtypeStruct((HEAD,) + vis.shape[1:], vis.dtype)
    rot, g, p = pl.pallas_call(
        functools.partial(start_kernel, dims),
        out_shape=[whole] * 3,
        in_specs=[hbm] * 3,
        out_specs=[vmem] * 3,
        scratch_shapes=[
            pltpu.VMEM((3, T, full), f32),
            pltpu.SMEM(lmn.shape, f32),
            pltpu.VMEM(gains.shape, f32),
            pltpu.SemaphoreType.DMA((3,)),
        ],
        compiler_params=LIMIT,
        name="start",
    )(far(positions.transpose(1, 0, 2)), far(lmn), far(gains))
    for step in range(ITERS):
        last = step == ITERS - 1
        got = [gather(p, m) for m in range(R)]
        if step == 0:
            (live_col, live_half, live_own, upright, u, rhs, held, slope, samples, extra, head) = (
                pl.pallas_call(
                    functools.partial(setup_kernel, dims, cols),
                    out_shape=[
                        array(FT, cols), array(FT, W), array(FT, W), array(rows, W), whole,
                        fit, whole, whole, text, text, start,
                    ],
                    in_specs=[hbm] * 4 + [vmem],
                    out_specs=[vmem] * 11,
                    scratch_shapes=[
                        pltpu.SMEM(flux_t.shape, f32),
                        pltpu.VMEM(flags.shape, flags.dtype),
                        pltpu.VMEM(duals.shape, f32),
                        pltpu.SemaphoreType.DMA((4,)),
                    ],
                    compiler_params=LIMIT,
                    name="setup",
                )(far(flux_t), far(flags), far(duals), far(vis), g)
            )
        else:
            rhs, held, slope, extra, head = pl.pallas_call(
                functools.partial(again_kernel, dims),
                out_shape=[fit, whole, whole, text, start],
                in_specs=[smem, hbm] + [vmem] * 4,
                out_specs=[vmem] * 5,
                scratch_shapes=[pltpu.SemaphoreType.DMA((1,))],
                compiler_params=LIMIT,
                name="again",
            )(flux_t, far(vis), samples, live_own, u, g)
        rhs_near = permute(rhs, lambda r, c, z: (r, c, z ^ 1))
        theirs = permute(p, lambda r, c, z: (r, c ^ 2, z), lambda r, c: r == c // 2)
        more = [] if step else [upright]
        keep, send, *found = pl.pallas_call(
            functools.partial(sum_kernel, dims),
            out_shape=[pair, pair] + ([] if step else [array(1, cols)]),
            in_specs=[hbm] * 2 + [vmem] * (4 + len(more)),
            out_specs=[vmem] * (2 + len(more)),
            scratch_shapes=[
                pltpu.VMEM(vis.shape, vis.dtype),
                pltpu.VMEM((rows, cols), vis.dtype),
                pltpu.SMEM(flux_t.shape, f32),
                pltpu.SemaphoreType.DMA((F + 1,)),
            ] + [pltpu.VMEM((rows, W), f32)] * len(more),
            compiler_params=LIMIT,
            name="sums",
        )(far(flux_t), far(vis), live_col, *got, head, *more)
        power = power if step else found[0]
        passed = permute(
            got[0], lambda r, c, z: (r, c ^ 1, z), lambda r, c: c == 3 * r + (1 - 2 * r)
        )
        other = permute(send, lambda r, c, z: (r, c ^ 1, z))
        (rhs,) = call(add_kernel, [fit], [], [rhs, rhs_near])
        rhs_far = permute(rhs, lambda r, c, z: (r, c, z ^ 2))
        everyone = array(R * C * Z, W)
        keep, send, scalar = pl.pallas_call(
            functools.partial(residual_kernel, dims),
            out_shape=[line, line, everyone],
            in_specs=[vmem] * 9,
            out_specs=[vmem, vmem, hbm],
            scratch_shapes=[
                pltpu.VMEM((FT, 2 * D, W), f32), pltpu.VMEM(everyone.shape, f32),
                pltpu.SemaphoreType.DMA((1,)),
            ],
            compiler_params=LIMIT,
            name="residual",
        )(live_half, extra, power, keep, other, p, theirs, passed, got[1])
        come = permute(send, lambda r, c, z: (r, c ^ 2, z))
        scalar = lax.all_to_all(scalar, AXES, 0, 0, tiled=True)
        target = call(
            functools.partial(target_kernel, dims, step == 0),
            [whole] * (1 if step == 0 else 2), [], [u, g, rhs, rhs_far],
        )
        num, den = call(
            functools.partial(merge_kernel, dims), [whole, whole], [],
            [keep, come, live_own, rot, g, held, slope],
        )
        update = functools.partial(update_kernel, dims, last, float(full))
        arrays = [scalar, num, den, target[0], g]
        if last:
            g, total, rhs = call(
                update, [whole, whole, fit], [],
                arrays + [target[1]],
            )
        else:
            g, p = call(update, [whole, whole], [], arrays + [rot])

    def write(kernel, arrays):
        return pl.pallas_call(
            functools.partial(kernel, dims),
            out_shape=array(*gains.shape),
            in_specs=[vmem] * len(arrays),
            out_specs=hbm,
            scratch_shapes=[pltpu.VMEM(gains.shape, f32), pltpu.SemaphoreType.DMA((F // CHUNK,))],
            compiler_params=LIMIT,
        )(*arrays)

    rhs_all = bands(rhs)
    gain = write(emit_kernel, [g])
    dual = write(final_kernel, [total, *rhs_all])
    return (gain, dual)


def basis(count):
    grid = 2.0 * jnp.arange(count, dtype=jnp.float32) / (count - 1) - 1.0
    return jnp.stack([grid**power for power in range(4)], axis=1)


def rotate(positions, lmn, freq):
    geometry = jnp.einsum("tks,kd->tds", positions, lmn, precision=HIGH)
    angle = 2.0 * math.pi * freq[:, None, None, None] * geometry[None]
    return (jnp.cos(angle), -jnp.sin(angle))


def complex_mul(a_re, a_im, b_re, b_im):
    return (a_re * b_re - a_im * b_im, a_re * b_im + a_im * b_re)


def solve_fit(rhs, total_f):
    full = basis(total_f)
    gram = jnp.dot(full.T, full, precision=HIGH)
    factor = jnp.linalg.cholesky(gram)
    flat = rhs.reshape(rhs.shape[0], -1)
    return jax.scipy.linalg.cho_solve((factor, True), flat).reshape(rhs.shape)


def plain_shards(vis, flags, positions, lmn, flux, gains, duals):
    width = gains.shape[0]
    total_f = width * lax.axis_size("band")
    first = lax.axis_index("band") * width
    local_basis = lax.dynamic_slice_in_dim(basis(total_f), first, width, 0)
    freq = 1.0 + (first + jnp.arange(width, dtype=jnp.int32)).astype(jnp.float32) / total_f
    row_index = lax.axis_index("row")
    col_index = lax.axis_index("col")
    row_count = vis.shape[3]
    col_count = vis.shape[4]
    owned = gains.shape[4]
    own_start = (row_index * lax.axis_size("col") + col_index) * owned
    row_start = row_index * row_count
    col_start = col_index * col_count
    own_cos, own_sin = rotate(lax.dynamic_slice_in_dim(positions, own_start, owned, 2), lmn, freq)
    row_cos, row_sin = rotate(
        lax.dynamic_slice_in_dim(positions, row_start, row_count, 2), lmn, freq
    )
    col_cos, col_sin = rotate(
        lax.dynamic_slice_in_dim(positions, col_start, col_count, 2), lmn, freq
    )
    all_live = flags.astype(jnp.float32)
    row_live = lax.dynamic_slice_in_dim(all_live, row_start, row_count, 2)
    col_live = lax.dynamic_slice_in_dim(all_live, col_start, col_count, 2)
    own_live = lax.dynamic_slice_in_dim(all_live, own_start, owned, 2)
    row_ids = row_start + jnp.arange(row_count, dtype=jnp.int32)
    col_ids = col_start + jnp.arange(col_count, dtype=jnp.int32)
    distinct = (row_ids[:, None] != col_ids[None, :]).astype(jnp.float32)
    weight = row_live[:, :, :, None] * col_live[:, :, None, :] * distinct
    vis_re = vis[:, :, 0].astype(jnp.float32)
    vis_im = vis[:, :, 1].astype(jnp.float32)
    scale = flux[:, None, :, None]

    def fit(gain, dual):
        rhs = jnp.einsum("fk,ftcds->ktcds", local_basis, gain + dual, precision=HIGH)
        return solve_fit(lax.psum(rhs, "band"), total_f)

    gain, dual = (gains, duals)
    coeffs = fit(gain, dual)
    for _ in range(ITERS):
        target = jnp.einsum("fk,ktcds->ftcds", local_basis, coeffs, precision=HIGH) - dual
        every = lax.all_gather(gain, ("row", "col"), axis=4, tiled=True)
        row_gain = lax.dynamic_slice_in_dim(every, row_start, row_count, 4)
        col_gain = lax.dynamic_slice_in_dim(every, col_start, col_count, 4)
        row_re, row_im = complex_mul(row_gain[:, :, 0], row_gain[:, :, 1], row_cos, row_sin)
        col_re, col_im = complex_mul(col_gain[:, :, 0], col_gain[:, :, 1], col_cos, col_sin)
        col_re = scale * col_re
        col_im = scale * col_im
        model_re = jnp.einsum("ftdp,ftdq->ftpq", row_re, col_re, precision=HIGH) + jnp.einsum(
            "ftdp,ftdq->ftpq", row_im, col_im, precision=HIGH
        )
        model_im = jnp.einsum("ftdp,ftdq->ftpq", row_im, col_re, precision=HIGH) - jnp.einsum(
            "ftdp,ftdq->ftpq", row_re, col_im, precision=HIGH
        )
        resid_re = weight * (vis_re - model_re)
        resid_im = weight * (vis_im - model_im)
        squares, samples = lax.psum(
            (jnp.sum(resid_re * resid_re + resid_im * resid_im), jnp.sum(weight)),
            ("row", "col", "band"),
        )
        sum_re = jnp.einsum("ftpq,ftdq->ftdp", resid_re, col_re, precision=HIGH) - jnp.einsum(
            "ftpq,ftdq->ftdp", resid_im, col_im, precision=HIGH
        )
        sum_im = jnp.einsum("ftpq,ftdq->ftdp", resid_re, col_im, precision=HIGH) + jnp.einsum(
            "ftpq,ftdq->ftdp", resid_im, col_re, precision=HIGH
        )
        pairs = lax.psum_scatter(
            jnp.stack([sum_re, sum_im], axis=2), "col", scatter_dimension=4, tiled=True
        )
        every_mag = every[:, :, 0] * every[:, :, 0] + every[:, :, 1] * every[:, :, 1]
        total_mag = jnp.einsum("ftds,fts->ftd", every_mag, all_live, precision=HIGH)
        own_mag = gain[:, :, 0] * gain[:, :, 0] + gain[:, :, 1] * gain[:, :, 1]
        own_flag = own_live[:, :, None, :]
        own_denom = (scale * scale * own_flag * (total_mag[:, :, :, None] - own_flag * own_mag))[
            :, :, None
        ]
        num_re, num_im = complex_mul(own_cos, -own_sin, pairs[:, :, 0], pairs[:, :, 1])
        numer = jnp.stack([num_re, num_im], axis=2)
        rho = PENALTY * flags.shape[2] * (squares / samples + 1e-06)
        fresh = (numer + own_denom * gain + rho * target) / (own_denom + rho)
        gain = 0.5 * (gain + fresh)
        coeffs = fit(gain, dual)
        dual = dual + gain - jnp.einsum("fk,ktcds->ftcds", local_basis, coeffs, precision=HIGH)
    return (gain, dual)


def solution(mesh):
    sizes = tuple(mesh.shape[a] for a in AXES)

    fits = sizes == (2, 4, 4)

    def body(*args):
        gains = args[5]
        if fits and gains.shape[3:] == (8, 64) and 8 % gains.shape[1] == 0:
            return shards(sizes, *args)
        return plain_shards(*args)

    return jax.shard_map(
        body,
        mesh=mesh,
        in_specs=(
            P("band", None, None, "row", "col"),
            P("band", None, None),
            P(),
            P(),
            P("band", None),
            P("band", None, None, None, ("row", "col")),
            P("band", None, None, None, ("row", "col")),
        ),
        out_specs=(
            P("band", None, None, None, ("row", "col")),
            P("band", None, None, None, ("row", "col")),
        ),
        check_vma=False,
    )
```

```python
import functools
import math

import jax
import jax.numpy as jnp
import numpy as np
from jax import lax
from jax.experimental import pallas as pl
from jax.experimental.pallas import tpu as pltpu
from jax.sharding import PartitionSpec as P

ITERS = 2
PENALTY = 0.05
HIGH = lax.Precision.HIGHEST
AXES = ("row", "col", "band")
CHUNK = 4
PARTS = 4
HEAD = 2
LIMIT = pltpu.CompilerParams(vmem_limit_bytes=16 * 2**20)


def swap(x):
    half = x.shape[-1] // 2
    return pltpu.roll(x, half, x.ndim - 1)


def low_lanes(shape):
    return lax.broadcasted_iota(jnp.int32, shape, len(shape) - 1) < shape[-1] // 2


def join_low(a, b):
    return jnp.where(low_lanes(a.shape), a, swap(b))


def join_high(a, b):
    return jnp.where(low_lanes(a.shape), swap(a), b)


def column(ref, index, dirs, lanes):
    rows = lax.broadcasted_iota(jnp.int32, (dirs, lanes), 0)
    out = jnp.full((dirs, lanes), ref[0, index], jnp.float32)
    for d in range(1, dirs):
        out = jnp.where(rows == d, ref[d, index], out)
    return out


def cos_turns(r):
    t = 0.25 - jnp.abs(r)
    x = t * t
    coef = [(-1) ** n * (2.0 * math.pi) ** (2 * n + 1) / math.factorial(2 * n + 1) for n in range(7)]
    out = jnp.full_like(x, coef[-1])
    for c in coef[-2::-1]:
        out = out * x + c
    return out * t


def rotated(g, e):
    low = low_lanes(e.shape)
    turned = swap(e)
    cos2 = jnp.where(low, e, turned)
    sin2 = jnp.where(low, -turned, e)
    return g * cos2 + swap(g) * sin2


def counter_rotated(g, e):
    low = low_lanes(e.shape)
    turned = swap(e)
    cos2 = jnp.where(low, e, turned)
    sin2 = jnp.where(low, -turned, e)
    return g * cos2 - swap(g) * sin2


def start_kernel(dims, pos_hbm, lmn_hbm, gains_hbm, e_ref, g_ref, p_ref, pos_ref, lmn_ref, gains_ref, sems):
    F, T, D, O, R, C = dims
    W = 2 * O
    copies = [
        pltpu.make_async_copy(pos_hbm, pos_ref, sems.at[0]),
        pltpu.make_async_copy(lmn_hbm, lmn_ref, sems.at[1]),
    ]
    part = F // PARTS
    for i in range(PARTS):
        at = pl.ds(i * part, part)
        copies.append(pltpu.make_async_copy(gains_hbm.at[at], gains_ref.at[at], sems.at[2 + i]))
    for copy in copies:
        copy.start()
    own = lax.axis_index("row") * C + lax.axis_index("col")
    first = lax.axis_index("band") * F
    low = low_lanes((D, W))
    rows = lax.broadcasted_iota(jnp.int32, (D, W), 0)
    shift = jnp.where(low, 0.0, 0.25)
    copies[0].wait()
    copies[1].wait()
    pos = pos_ref[:, :, :O]
    for k in range(1, R * C):
        pos = jnp.where(own == k, pos_ref[:, :, k * O : (k + 1) * O], pos)
    pos = jnp.concatenate([pos, pos], axis=-1)
    geometry = []
    for t in range(T):
        total = jnp.zeros((D, W), jnp.float32)
        for k in range(3):
            lm = jnp.full((D, W), lmn_ref[k, 0], jnp.float32)
            for d in range(1, D):
                lm = jnp.where(rows == d, lmn_ref[k, d], lm)
            total = total + lm * pos[k, t : t + 1, :]
        geometry.append(total)
    total_f = F * lax.axis_size("band")
    for f in range(F):
        nu = 1.0 + (first + f).astype(jnp.float32) * (1.0 / total_f)
        for t in range(T):
            ft = f * T + t
            turns = nu * geometry[t]
            r = turns - jnp.round(turns) + shift
            e_ref[ft] = cos_turns(r - jnp.round(r))
    for f in range(F):
        if f % part == 0:
            copies[2 + f // part].wait()
        for t in range(T):
            ft = f * T + t
            g = jnp.concatenate([gains_ref[f, t, 0], gains_ref[f, t, 1]], axis=-1)
            g_ref[ft] = g
            p_ref[ft] = rotated(g, e_ref[ft])


def own_terms(dims, flux_ref, live_ref, g_ref, held_ref, slope_ref):
    F, T, D, O, _, _ = dims
    total = jnp.zeros((1, 2 * O), jnp.float32)
    for f in range(F):
        flux = column(flux_ref, f, D, 2 * O)
        for t in range(T):
            ft = f * T + t
            live = live_ref[ft : ft + 1, :]
            g = g_ref[ft]
            power = g * g
            power = (power + swap(power)) * flux
            own = jnp.sum(power, axis=0, keepdims=True)
            total = total + live * own * own
            power = power * flux
            slope_ref[ft] = -live * power
            held_ref[ft] = live * (own * flux - power) * g
    return total


def place(dims, f):
    F = dims[0]
    full = F * lax.axis_size("band")
    at = (lax.axis_index("band") * F + f).astype(jnp.float32)
    return at * (2.0 / (full - 1)) - 1.0


def fit_sums(dims, value, rhs_ref):
    F, T, D, O, _, _ = dims
    for t in range(T):
        acc = [jnp.zeros((D, 2 * O), jnp.float32) for _ in range(4)]
        for f in range(F):
            total = value(f, t)
            x = place(dims, f)
            for k in range(4):
                acc[k] = acc[k] + total
                total = total * x if k < 3 else total
        for k in range(4):
            rhs_ref[k * T + t] = acc[k]


def solve(dims, rhs_refs, t):
    T = dims[1]
    full = dims[0] * lax.axis_size("band")
    grid = 2.0 * np.arange(full, dtype=np.float64) / (full - 1) - 1.0
    basis = np.stack([grid**k for k in range(4)], axis=1)
    inverse = np.linalg.inv(basis.T @ basis)
    rhs = [sum(ref[k * T + t] for ref in rhs_refs) for k in range(4)]
    out = []
    for k in range(4):
        total = float(inverse[k, 0]) * rhs[0]
        for j in range(1, 4):
            total = total + float(inverse[k, j]) * rhs[j]
        out.append(total)
    return out


def curve(coeffs, x):
    return coeffs[0] + x * (coeffs[1] + x * (coeffs[2] + x * coeffs[3]))


def pick(index, parts):
    out = parts[0]
    for k in range(1, len(parts)):
        out = jnp.where(index == k, parts[k], out)
    return out


def setup_kernel(dims, cols, flux_hbm, flags_hbm, duals_hbm, vis_hbm, g_ref, live_col_ref, live_half_ref,
                 live_own_ref, upright_ref, u_ref, rhs_ref, held_ref, slope_ref, samples_ref,
                 extra_ref, head_ref, flux_ref, flags_ref, duals_ref, sems):
    F, T, _, O, R, C = dims
    W, rows, full = 2 * O, C * O, flags_ref.shape[2]
    row = lax.axis_index("row")
    col = lax.axis_index("col")
    copies = [
        pltpu.make_async_copy(flags_hbm, flags_ref, sems.at[0]),
        pltpu.make_async_copy(duals_hbm, duals_ref, sems.at[1]),
        pltpu.make_async_copy(flux_hbm, flux_ref, sems.at[2]),
        pltpu.make_async_copy(vis_hbm.at[pl.ds(0, HEAD)], head_ref, sems.at[3]),
    ]
    for copy in copies:
        copy.start()
    copies[0].wait()
    counts = jnp.zeros((T, full), jnp.float32)
    stacked = []
    for f in range(F):
        live = flags_ref[f].astype(jnp.float32)
        at = slice(f * T, (f + 1) * T)
        mine = pick(row, [live[:, r * rows : (r + 1) * rows] for r in range(R)])
        blocks = [mine[:, c * O : (c + 1) * O] for c in range(C)]
        live_col_ref[at, :] = pick(col, [live[:, c * cols : (c + 1) * cols] for c in range(C)])
        even = jnp.concatenate([blocks[0], blocks[2]], axis=1)
        odd = jnp.concatenate([blocks[1], blocks[3]], axis=1)
        live_half_ref[at, :] = pick(col % 2, [even, odd])
        own = pick(col, blocks)
        live_own_ref[at, :] = jnp.concatenate([own, own], axis=1)
        stacked.append(mine)
        count = jnp.sum(live, axis=1, keepdims=True)
        counts = counts + live * (count - 1.0)
    stacked = jnp.concatenate(stacked + [jnp.zeros((W - F * T, rows), jnp.float32)], axis=0)
    upright_ref[...] = jnp.transpose(stacked)
    samples = jnp.sum(counts, axis=0, keepdims=True)
    samples = jnp.sum(samples, axis=1, keepdims=True) / (R * C)
    copies[1].wait()
    copies[2].wait()
    for f in range(F):
        for t in range(T):
            u_ref[f * T + t] = jnp.concatenate([duals_ref[f, t, 0], duals_ref[f, t, 1]], axis=-1)
    fit_sums(dims, lambda f, t: u_ref[f * T + t] + g_ref[f * T + t], rhs_ref)
    own = own_terms(dims, flux_ref, live_own_ref, g_ref, held_ref, slope_ref)
    lanes = lax.broadcasted_iota(jnp.int32, own.shape, 1)
    samples = jnp.where(lanes == O, samples, 0.0)
    samples_ref[...] = samples
    extra_ref[...] = samples - jnp.where(low_lanes(own.shape), own, 0.0)
    copies[3].wait()


def again_kernel(dims, flux_ref, vis_hbm, samples_ref, live_ref, u_ref, g_ref,
                 rhs_ref, held_ref, slope_ref, extra_ref, head_ref, sem):
    _, T, _, _, _, _ = dims
    copy = pltpu.make_async_copy(vis_hbm.at[pl.ds(0, HEAD)], head_ref, sem.at[0])
    copy.start()
    fit_sums(dims, lambda f, t: u_ref[f * T + t] + g_ref[f * T + t], rhs_ref)
    own = own_terms(dims, flux_ref, live_ref, g_ref, held_ref, slope_ref)
    extra_ref[...] = samples_ref[...] - jnp.where(low_lanes(own.shape), own, 0.0)
    copy.wait()


def add_kernel(a_ref, b_ref, out_ref):
    out_ref[...] = a_ref[...] + b_ref[...]


def target_kernel(dims, first_pass, u_ref, g_ref, *refs):
    F, T, _, _, _, _ = dims
    rhs_refs, outs = refs[:2], refs[2:]
    for t in range(T):
        coeffs = solve(dims, rhs_refs, t)
        for f in range(F):
            ft = f * T + t
            smooth = curve(coeffs, place(dims, f))
            u = u_ref[ft]
            if not first_pass:
                u = u + g_ref[ft] - smooth
                outs[1][ft] = u
            outs[0][ft] = smooth - u


def halves(x):
    high = x.astype(jnp.bfloat16)
    return high, (x - high.astype(jnp.float32)).astype(jnp.bfloat16)


def product(a, b):
    (a0, a1), (b0, b1) = halves(a), halves(b)
    out = jnp.dot(a0, b1, preferred_element_type=jnp.float32)
    out = out + jnp.dot(a1, b0, preferred_element_type=jnp.float32)
    return out + jnp.dot(a0, b0, preferred_element_type=jnp.float32)


def block_mask(size):
    shape = (8 * size, 8 * size)
    a = lax.broadcasted_iota(jnp.int32, shape, 0) // size
    b = lax.broadcasted_iota(jnp.int32, shape, 1) // size
    return a == b


def sum_kernel(dims, flux_hbm, vis_hbm, live_ref, a_ref, b_ref, head_ref, *refs):
    F, T, D, O, _, _ = dims
    upright_ref, refs = (refs[0], refs[1:]) if len(refs) == 9 else (None, refs)
    keep_ref, send_ref, refs = refs[0], refs[1], refs[2:]
    power_ref, refs = (refs[0], refs[1:]) if upright_ref is not None else (None, refs)
    vis_ref, distinct, flux_ref, sems = refs[:4]
    rows, cols = vis_ref.shape[3], vis_ref.shape[4]
    row = lax.axis_index("row")
    col = lax.axis_index("col")
    parity = col % 2

    def vis_copy(f):
        return pltpu.make_async_copy(vis_hbm.at[f], vis_ref.at[f], sems.at[f])

    flux_copy = pltpu.make_async_copy(flux_hbm, flux_ref, sems.at[F])
    flux_copy.start()
    for f in range(HEAD, F):
        vis_copy(f).start()
    p = lax.broadcasted_iota(jnp.int32, (rows, cols), 0) + row * rows
    q = lax.broadcasted_iota(jnp.int32, (rows, cols), 1) + col * cols
    distinct[...] = jnp.where(p == q, 0.0, 1.0).astype(jnp.bfloat16)
    group = 8 // T
    blocks = block_mask(2 * D)
    nt = (((1,), (1,)), ((), ()))

    def body(step, upright, start, power, source):
        highs, lows = [], []
        lives = live_ref[pl.ds(step * 8, 8), :]
        mask = distinct[...]
        for i in range(group):
            f = step * group + i
            scale = column(flux_ref, f, D, cols)
            for t in range(T):
                j = i * T + t
                ft = step * 8 + j
                a, b = a_ref[ft], b_ref[ft]
                first = jnp.where(row == 0, a, b)
                second = jnp.where(row == 0, b, a)
                weight = scale * lives[j : j + 1, :]
                re = join_low(first, second) * weight
                im = join_high(first, second) * weight
                x = jnp.concatenate(
                    [jnp.concatenate([re, -im], axis=1), jnp.concatenate([im, re], axis=1)], axis=0
                )
                high = x.astype(jnp.bfloat16)
                low = (x - high.astype(jnp.float32)).astype(jnp.bfloat16)
                highs.append(high)
                lows.append(low)
                both = jnp.concatenate([high, low], axis=0)
                seen = [source[f, t, part] * mask for part in range(2)]
                v = lax.dot_general(
                    both, jnp.concatenate(seen, axis=1), nt, preferred_element_type=jnp.float32
                )
                v = v[: 2 * D] + v[2 * D :]
                v0, v1 = v[:, : 2 * O], v[:, 2 * O :]
                even, odd = join_low(v0, v1), join_high(v0, v1)
                keep_ref[step * 9 + j] = jnp.where(parity == 0, even, odd)
                send_ref[step * 9 + j] = jnp.where(parity == 0, odd, even)
                if upright is not None:
                    square = [x.astype(jnp.float32) for x in seen]
                    square = square[0] * square[0] + square[1] * square[1]
                    at = start + j
                    square = square * jnp.broadcast_to(upright[:, at : at + 1], square.shape)
                    square = jnp.sum(square.reshape(rows // 8, 8, cols), axis=0)
                    power = power + square * lives[j : j + 1, :]
        high = jnp.concatenate(highs, axis=0)
        low = jnp.concatenate(lows, axis=0)
        gram = lax.dot_general(high, high, nt, preferred_element_type=jnp.float32)
        gram = gram + lax.dot_general(high, low, nt, preferred_element_type=jnp.float32)
        gram = gram + lax.dot_general(low, high, nt, preferred_element_type=jnp.float32)
        gram = jnp.where(blocks, gram, 0.0)
        folded = gram[: 2 * D]
        for i in range(1, 8):
            folded = folded + gram[i * 2 * D : (i + 1) * 2 * D]
        keep_ref[step * 9 + 8] = folded
        send_ref[step * 9 + 8] = folded
        return power

    def roll_to(c):
        if upright_ref is None:
            return None
        upright = refs[4]
        upright[...] = pltpu.roll(upright_ref[...], (2 * O - c * CHUNK * T) % (2 * O), 1)
        return upright

    def chunk(c, power):
        for i in range(CHUNK):
            vis_copy(c * CHUNK + i).wait()

        upright = roll_to(c)
        for j in range(CHUNK // group):
            power = body(c * (CHUNK // group) + j, upright, j * 8, power, vis_ref)
        return power

    flux_copy.wait()
    power = jnp.zeros((8, cols), jnp.float32)
    upright = roll_to(0)
    for j in range(CHUNK // group):
        inside = (j + 1) * group <= HEAD
        if not inside:
            for i in range(group):
                vis_copy(j * group + i).wait()
        power = body(j, upright, j * 8, power, head_ref if inside else vis_ref)
    power = lax.fori_loop(1, F // CHUNK, chunk, power)
    if power_ref is not None:
        power = jnp.sum(power, axis=0, keepdims=True)
        power_ref[...] = jnp.where(low_lanes(power.shape), power + swap(power), 0.0)


def residual_kernel(dims, live_ref, extra_ref, power_ref, kept_ref, other_ref, mine_ref, theirs_ref,
                    passed_ref, got_ref, keep_ref, send_ref, scalar_hbm, num_ref, scalar_ref, sem):
    F, T, D, O, _, _ = dims
    W = 2 * O
    row = lax.axis_index("row")
    col = lax.axis_index("col")
    near = col // 2 == 0
    away = col // 2 != row
    held = col % 2 != row
    mask = block_mask(2 * D)
    eye = lax.broadcasted_iota(jnp.int32, (2 * D, W), 0) == (
        lax.broadcasted_iota(jnp.int32, (2 * D, W), 1) % (2 * D)
    )

    def body(group, total):
        gram = kept_ref[group * 9 + 8] + other_ref[group * 9 + 8]
        diagonal = jnp.sum(jnp.where(eye, gram, 0.0), axis=0, keepdims=True)
        keep_ref[F * T, pl.ds(group, 1), :] = diagonal
        send_ref[F * T, pl.ds(group, 1), :] = diagonal
        spread = jnp.where(mask, jnp.concatenate([gram] * 8, axis=0), 0.0)
        station = []
        for i in range(8):
            ft = group * 8 + i
            a = mine_ref[ft]
            b = jnp.where(away, theirs_ref[ft], jnp.where(held, got_ref[ft], passed_ref[ft]))
            first = jnp.where(near, a, b)
            second = jnp.where(near, b, a)
            station += [join_low(first, second), join_high(first, second)]
        model = product(spread, jnp.concatenate(station, axis=0))
        lives = live_ref[pl.ds(group * 8, 8), :]
        for i in range(8):
            ft = group * 8 + i
            live = lives[i : i + 1, :]
            v = kept_ref[group * 9 + i] + other_ref[group * 9 + i]
            num = (v - model[i * 2 * D : (i + 1) * 2 * D]) * live
            z = jnp.concatenate(station[2 * i : 2 * i + 2], axis=0)
            total = total + z * (v * live + num)
            num_ref[ft] = num
        return total

    total = jnp.zeros((2 * D, W), jnp.float32)
    for group in range(F * T // 8):
        total = body(group, total)
    squares = -jnp.sum(total, axis=0, keepdims=True)
    squares = squares + swap(squares)
    scalar = jnp.where(low_lanes(squares.shape), squares, 0.0) + extra_ref[...] + power_ref[...]
    scalar_ref[...] = jnp.broadcast_to(scalar, scalar_ref.shape)
    copy = pltpu.make_async_copy(scalar_ref, scalar_hbm, sem.at[0])
    copy.start()
    for ft in range(F * T):
        num = num_ref[ft]
        low, high = join_low(num[:D], num[D:]), join_high(num[:D], num[D:])
        keep_ref[ft] = jnp.where(near, low, high)
        send_ref[ft] = jnp.where(near, high, low)
    copy.wait()


def merge_kernel(dims, keep_ref, come_ref, live_ref, e_ref, g_ref, held_ref, slope_ref,
                 num_ref, den_ref):
    F, T, D, O, _, _ = dims
    W = 2 * O
    shape = (8 * D, W)
    a = lax.broadcasted_iota(jnp.int32, shape, 0)
    b = lax.broadcasted_iota(jnp.int32, shape, 1)
    eye = a // D * (2 * D) + a % D == b
    ones = jnp.ones((W, W), jnp.bfloat16)
    for group in range(F * T // 8):
        diagonal = keep_ref[F * T, group : group + 1, :] + come_ref[F * T, group : group + 1, :]
        rest, spread = jnp.where(eye, diagonal, 0.0), 0.0
        for _ in range(3):
            high = rest.astype(jnp.bfloat16)
            rest = rest - high.astype(jnp.float32)
            spread = spread + jnp.dot(high, ones, preferred_element_type=jnp.float32)
        for i in range(8):
            ft = group * 8 + i
            around = live_ref[ft : ft + 1, :] * spread[i * D : (i + 1) * D]
            num = counter_rotated(keep_ref[ft] + come_ref[ft], e_ref[ft])
            num_ref[ft] = num + held_ref[ft] + around * g_ref[ft]
            den_ref[ft] = around + slope_ref[ft]


def update_kernel(dims, last, full, *refs):
    F, T, D, O, _, _ = dims
    scalar_ref, num_ref, den_ref, target_ref, g_ref, other_ref = refs[:6]
    W = 2 * O
    sums = jnp.sum(scalar_ref[...], axis=0, keepdims=True)
    low = low_lanes(sums.shape)
    squares = jnp.sum(jnp.where(low, sums, 0.0), axis=1, keepdims=True)
    samples = jnp.sum(jnp.where(low, 0.0, sums), axis=1, keepdims=True)
    squares = jnp.maximum(squares, 0.0)
    rho = PENALTY * full * (squares / samples + 1e-06)
    rho = jnp.broadcast_to(rho, (D, W))
    for t in range(T):
        acc = [jnp.zeros((D, W), jnp.float32) for _ in range(4)]
        for f in range(F):
            ft = f * T + t
            fresh = (num_ref[ft] + rho * target_ref[ft]) / (den_ref[ft] + rho)
            g = 0.5 * (g_ref[ft] + fresh)
            if last:
                out_ref, total_ref, rhs_ref = refs[6:]
                out_ref[ft] = g
                total = other_ref[ft] + g
                total_ref[ft] = total
                x = place(dims, f)
                for k in range(4):
                    acc[k] = acc[k] + total
                    total = total * x if k < 3 else total
            else:
                g_out, p_out = refs[6:]
                g_out[ft] = g
                p_out[ft] = rotated(g, other_ref[ft])
        if last:
            for k in range(4):
                rhs_ref[k * T + t] = acc[k]


def write_out(dims, value, out_hbm, out_ref, sems):
    F, T, _, O, _, _ = dims
    copies = []
    for part in range(F // CHUNK):
        for f in range(part * CHUNK, (part + 1) * CHUNK):
            for t in range(T):
                x = value(f, t)
                out_ref[f, t, 0] = x[:, :O]
                out_ref[f, t, 1] = x[:, O:]
        at = pl.ds(part * CHUNK, CHUNK)
        copies.append(pltpu.make_async_copy(out_ref.at[at], out_hbm.at[at], sems.at[part]))
        copies[-1].start()
    for copy in copies:
        copy.wait()


def emit_kernel(dims, g_ref, out_hbm, out_ref, sems):
    write_out(dims, lambda f, t: g_ref[f * dims[1] + t], out_hbm, out_ref, sems)


def final_kernel(dims, total_ref, *refs):
    T = dims[1]
    coeffs = [solve(dims, refs[:-3], t) for t in range(T)]
    write_out(
        dims, lambda f, t: total_ref[f * T + t] - curve(coeffs[t], place(dims, f)), *refs[-3:]
    )


def shards(sizes, vis, flags, positions, lmn, flux, gains, duals):
    R, C, Z = sizes
    F, T, _, D, O = gains.shape
    rows, cols = vis.shape[3], vis.shape[4]
    full = flags.shape[2]
    FT, W = F * T, 2 * O
    dims = (F, T, D, O, R, C)
    f32 = jnp.float32
    smem = pl.BlockSpec(memory_space=pltpu.SMEM)
    vmem = pl.BlockSpec(memory_space=pltpu.VMEM)
    hbm = pl.BlockSpec(memory_space=pltpu.HBM)

    def array(*shape):
        return jax.ShapeDtypeStruct(shape, f32)

    def far(x):
        return pltpu.with_memory_space_constraint(x, pltpu.HBM)

    def call(kernel, outs, scalars, arrays, scratch=()):
        return pl.pallas_call(
            kernel,
            out_shape=outs,
            in_specs=[smem] * len(scalars) + [vmem] * len(arrays),
            out_specs=[vmem] * len(outs),
            scratch_shapes=list(scratch),
            compiler_params=LIMIT,
        )(*scalars, *arrays)

    def where(r, c, z):
        return (r * C + c) * Z + z

    def permute(x, move, some=lambda r, c: True):
        pairs = [
            (where(r, c, z), where(*move(r, c, z)))
            for r in range(R) for c in range(C) for z in range(Z) if some(r, c)
        ]
        return lax.ppermute(x, AXES, pairs)

    def gather(x, m):
        return permute(x, lambda r, c, z: (((r * C + c) % R + m) % R, (r * C + c) // R, z))

    def bands(x):
        return [x] + [permute(x, lambda r, c, z, k=k: (r, c, z ^ k)) for k in range(1, Z)]

    whole, line, fit = array(FT, D, W), array(FT + 1, D, W), array(4 * T, D, W)
    pair, text = array(FT // 8 * 9, 2 * D, W), array(1, W)
    flux_t = flux.T
    start = jax.ShapeDtypeStruct((HEAD,) + vis.shape[1:], vis.dtype)
    rot, g, p = pl.pallas_call(
        functools.partial(start_kernel, dims),
        out_shape=[whole] * 3,
        in_specs=[hbm] * 3,
        out_specs=[vmem] * 3,
        scratch_shapes=[
            pltpu.VMEM((3, T, full), f32),
            pltpu.SMEM(lmn.shape, f32),
            pltpu.VMEM(gains.shape, f32),
            pltpu.SemaphoreType.DMA((2 + PARTS,)),
        ],
        compiler_params=LIMIT,
        name="start",
    )(far(positions.transpose(1, 0, 2)), far(lmn), far(gains))
    for step in range(ITERS):
        last = step == ITERS - 1
        got = [gather(p, m) for m in range(R)]
        if step == 0:
            (live_col, live_half, live_own, upright, u, rhs, held, slope, samples, extra, head) = (
                pl.pallas_call(
                    functools.partial(setup_kernel, dims, cols),
                    out_shape=[
                        array(FT, cols), array(FT, W), array(FT, W), array(rows, W), whole,
                        fit, whole, whole, text, text, start,
                    ],
                    in_specs=[hbm] * 4 + [vmem],
                    out_specs=[vmem] * 11,
                    scratch_shapes=[
                        pltpu.SMEM(flux_t.shape, f32),
                        pltpu.VMEM(flags.shape, flags.dtype),
                        pltpu.VMEM(duals.shape, f32),
                        pltpu.SemaphoreType.DMA((4,)),
                    ],
                    compiler_params=LIMIT,
                    name="setup",
                )(far(flux_t), far(flags), far(duals), far(vis), g)
            )
        else:
            rhs, held, slope, extra, head = pl.pallas_call(
                functools.partial(again_kernel, dims),
                out_shape=[fit, whole, whole, text, start],
                in_specs=[smem, hbm] + [vmem] * 4,
                out_specs=[vmem] * 5,
                scratch_shapes=[pltpu.SemaphoreType.DMA((1,))],
                compiler_params=LIMIT,
                name="again",
            )(flux_t, far(vis), samples, live_own, u, g)
        rhs_near = permute(rhs, lambda r, c, z: (r, c, z ^ 1))
        theirs = permute(p, lambda r, c, z: (r, c ^ 2, z), lambda r, c: r == c // 2)
        more = [] if step else [upright]
        keep, send, *found = pl.pallas_call(
            functools.partial(sum_kernel, dims),
            out_shape=[pair, pair] + ([] if step else [array(1, cols)]),
            in_specs=[hbm] * 2 + [vmem] * (4 + len(more)),
            out_specs=[vmem] * (2 + len(more)),
            scratch_shapes=[
                pltpu.VMEM(vis.shape, vis.dtype),
                pltpu.VMEM((rows, cols), vis.dtype),
                pltpu.SMEM(flux_t.shape, f32),
                pltpu.SemaphoreType.DMA((F + 1,)),
            ] + [pltpu.VMEM((rows, W), f32)] * len(more),
            compiler_params=LIMIT,
            name="sums",
        )(far(flux_t), far(vis), live_col, *got, head, *more)
        power = power if step else found[0]
        passed = permute(
            got[0], lambda r, c, z: (r, c ^ 1, z), lambda r, c: c == 3 * r + (1 - 2 * r)
        )
        other = permute(send, lambda r, c, z: (r, c ^ 1, z))
        (rhs,) = call(add_kernel, [fit], [], [rhs, rhs_near])
        rhs_far = permute(rhs, lambda r, c, z: (r, c, z ^ 2))
        everyone = array(R * C * Z, W)
        keep, send, scalar = pl.pallas_call(
            functools.partial(residual_kernel, dims),
            out_shape=[line, line, everyone],
            in_specs=[vmem] * 9,
            out_specs=[vmem, vmem, hbm],
            scratch_shapes=[
                pltpu.VMEM((FT, 2 * D, W), f32), pltpu.VMEM(everyone.shape, f32),
                pltpu.SemaphoreType.DMA((1,)),
            ],
            compiler_params=LIMIT,
            name="residual",
        )(live_half, extra, power, keep, other, p, theirs, passed, got[1])
        come = permute(send, lambda r, c, z: (r, c ^ 2, z))
        scalar = lax.all_to_all(scalar, AXES, 0, 0, tiled=True)
        target = call(
            functools.partial(target_kernel, dims, step == 0),
            [whole] * (1 if step == 0 else 2), [], [u, g, rhs, rhs_far],
        )
        num, den = call(
            functools.partial(merge_kernel, dims), [whole, whole], [],
            [keep, come, live_own, rot, g, held, slope],
        )
        update = functools.partial(update_kernel, dims, last, float(full))
        arrays = [scalar, num, den, target[0], g]
        if last:
            g, total, rhs = call(
                update, [whole, whole, fit], [],
                arrays + [target[1]],
            )
        else:
            g, p = call(update, [whole, whole], [], arrays + [rot])

    def write(kernel, arrays):
        return pl.pallas_call(
            functools.partial(kernel, dims),
            out_shape=array(*gains.shape),
            in_specs=[vmem] * len(arrays),
            out_specs=hbm,
            scratch_shapes=[pltpu.VMEM(gains.shape, f32), pltpu.SemaphoreType.DMA((F // CHUNK,))],
            compiler_params=LIMIT,
        )(*arrays)

    rhs_all = bands(rhs)
    gain = write(emit_kernel, [g])
    dual = write(final_kernel, [total, *rhs_all])
    return (gain, dual)


def basis(count):
    grid = 2.0 * jnp.arange(count, dtype=jnp.float32) / (count - 1) - 1.0
    return jnp.stack([grid**power for power in range(4)], axis=1)


def rotate(positions, lmn, freq):
    geometry = jnp.einsum("tks,kd->tds", positions, lmn, precision=HIGH)
    angle = 2.0 * math.pi * freq[:, None, None, None] * geometry[None]
    return (jnp.cos(angle), -jnp.sin(angle))


def complex_mul(a_re, a_im, b_re, b_im):
    return (a_re * b_re - a_im * b_im, a_re * b_im + a_im * b_re)


def solve_fit(rhs, total_f):
    full = basis(total_f)
    gram = jnp.dot(full.T, full, precision=HIGH)
    factor = jnp.linalg.cholesky(gram)
    flat = rhs.reshape(rhs.shape[0], -1)
    return jax.scipy.linalg.cho_solve((factor, True), flat).reshape(rhs.shape)


def plain_shards(vis, flags, positions, lmn, flux, gains, duals):
    width = gains.shape[0]
    total_f = width * lax.axis_size("band")
    first = lax.axis_index("band") * width
    local_basis = lax.dynamic_slice_in_dim(basis(total_f), first, width, 0)
    freq = 1.0 + (first + jnp.arange(width, dtype=jnp.int32)).astype(jnp.float32) / total_f
    row_index = lax.axis_index("row")
    col_index = lax.axis_index("col")
    row_count = vis.shape[3]
    col_count = vis.shape[4]
    owned = gains.shape[4]
    own_start = (row_index * lax.axis_size("col") + col_index) * owned
    row_start = row_index * row_count
    col_start = col_index * col_count
    own_cos, own_sin = rotate(lax.dynamic_slice_in_dim(positions, own_start, owned, 2), lmn, freq)
    row_cos, row_sin = rotate(
        lax.dynamic_slice_in_dim(positions, row_start, row_count, 2), lmn, freq
    )
    col_cos, col_sin = rotate(
        lax.dynamic_slice_in_dim(positions, col_start, col_count, 2), lmn, freq
    )
    all_live = flags.astype(jnp.float32)
    row_live = lax.dynamic_slice_in_dim(all_live, row_start, row_count, 2)
    col_live = lax.dynamic_slice_in_dim(all_live, col_start, col_count, 2)
    own_live = lax.dynamic_slice_in_dim(all_live, own_start, owned, 2)
    row_ids = row_start + jnp.arange(row_count, dtype=jnp.int32)
    col_ids = col_start + jnp.arange(col_count, dtype=jnp.int32)
    distinct = (row_ids[:, None] != col_ids[None, :]).astype(jnp.float32)
    weight = row_live[:, :, :, None] * col_live[:, :, None, :] * distinct
    vis_re = vis[:, :, 0].astype(jnp.float32)
    vis_im = vis[:, :, 1].astype(jnp.float32)
    scale = flux[:, None, :, None]

    def fit(gain, dual):
        rhs = jnp.einsum("fk,ftcds->ktcds", local_basis, gain + dual, precision=HIGH)
        return solve_fit(lax.psum(rhs, "band"), total_f)

    gain, dual = (gains, duals)
    coeffs = fit(gain, dual)
    for _ in range(ITERS):
        target = jnp.einsum("fk,ktcds->ftcds", local_basis, coeffs, precision=HIGH) - dual
        every = lax.all_gather(gain, ("row", "col"), axis=4, tiled=True)
        row_gain = lax.dynamic_slice_in_dim(every, row_start, row_count, 4)
        col_gain = lax.dynamic_slice_in_dim(every, col_start, col_count, 4)
        row_re, row_im = complex_mul(row_gain[:, :, 0], row_gain[:, :, 1], row_cos, row_sin)
        col_re, col_im = complex_mul(col_gain[:, :, 0], col_gain[:, :, 1], col_cos, col_sin)
        col_re = scale * col_re
        col_im = scale * col_im
        model_re = jnp.einsum("ftdp,ftdq->ftpq", row_re, col_re, precision=HIGH) + jnp.einsum(
            "ftdp,ftdq->ftpq", row_im, col_im, precision=HIGH
        )
        model_im = jnp.einsum("ftdp,ftdq->ftpq", row_im, col_re, precision=HIGH) - jnp.einsum(
            "ftdp,ftdq->ftpq", row_re, col_im, precision=HIGH
        )
        resid_re = weight * (vis_re - model_re)
        resid_im = weight * (vis_im - model_im)
        squares, samples = lax.psum(
            (jnp.sum(resid_re * resid_re + resid_im * resid_im), jnp.sum(weight)),
            ("row", "col", "band"),
        )
        sum_re = jnp.einsum("ftpq,ftdq->ftdp", resid_re, col_re, precision=HIGH) - jnp.einsum(
            "ftpq,ftdq->ftdp", resid_im, col_im, precision=HIGH
        )
        sum_im = jnp.einsum("ftpq,ftdq->ftdp", resid_re, col_im, precision=HIGH) + jnp.einsum(
            "ftpq,ftdq->ftdp", resid_im, col_re, precision=HIGH
        )
        pairs = lax.psum_scatter(
            jnp.stack([sum_re, sum_im], axis=2), "col", scatter_dimension=4, tiled=True
        )
        every_mag = every[:, :, 0] * every[:, :, 0] + every[:, :, 1] * every[:, :, 1]
        total_mag = jnp.einsum("ftds,fts->ftd", every_mag, all_live, precision=HIGH)
        own_mag = gain[:, :, 0] * gain[:, :, 0] + gain[:, :, 1] * gain[:, :, 1]
        own_flag = own_live[:, :, None, :]
        own_denom = (scale * scale * own_flag * (total_mag[:, :, :, None] - own_flag * own_mag))[
            :, :, None
        ]
        num_re, num_im = complex_mul(own_cos, -own_sin, pairs[:, :, 0], pairs[:, :, 1])
        numer = jnp.stack([num_re, num_im], axis=2)
        rho = PENALTY * flags.shape[2] * (squares / samples + 1e-06)
        fresh = (numer + own_denom * gain + rho * target) / (own_denom + rho)
        gain = 0.5 * (gain + fresh)
        coeffs = fit(gain, dual)
        dual = dual + gain - jnp.einsum("fk,ktcds->ftcds", local_basis, coeffs, precision=HIGH)
    return (gain, dual)


def solution(mesh):
    sizes = tuple(mesh.shape[a] for a in AXES)

    fits = sizes == (2, 4, 4)

    def body(*args):
        gains = args[5]
        if fits and gains.shape[3:] == (8, 64) and 8 % gains.shape[1] == 0:
            return shards(sizes, *args)
        return plain_shards(*args)

    return jax.shard_map(
        body,
        mesh=mesh,
        in_specs=(
            P("band", None, None, "row", "col"),
            P("band", None, None),
            P(),
            P(),
            P("band", None),
            P("band", None, None, None, ("row", "col")),
            P("band", None, None, None, ("row", "col")),
        ),
        out_specs=(
            P("band", None, None, None, ("row", "col")),
            P("band", None, None, None, ("row", "col")),
        ),
        check_vma=False,
    )
```

```python
import functools
import math

import jax
import jax.numpy as jnp
import numpy as np
from jax import lax
from jax.experimental import pallas as pl
from jax.experimental.pallas import tpu as pltpu
from jax.sharding import PartitionSpec as P

ITERS = 2
PENALTY = 0.05
HIGH = lax.Precision.HIGHEST
AXES = ("row", "col", "band")
CHUNK = 4
PARTS = 4
HEAD = 2
LIMIT = pltpu.CompilerParams(vmem_limit_bytes=16 * 2**20)


def swap(x):
    half = x.shape[-1] // 2
    return pltpu.roll(x, half, x.ndim - 1)


def low_lanes(shape):
    return lax.broadcasted_iota(jnp.int32, shape, len(shape) - 1) < shape[-1] // 2


def join_low(a, b):
    return jnp.where(low_lanes(a.shape), a, swap(b))


def join_high(a, b):
    return jnp.where(low_lanes(a.shape), swap(a), b)


def column(ref, index, dirs, lanes):
    rows = lax.broadcasted_iota(jnp.int32, (dirs, lanes), 0)
    out = jnp.full((dirs, lanes), ref[0, index], jnp.float32)
    for d in range(1, dirs):
        out = jnp.where(rows == d, ref[d, index], out)
    return out


def cos_turns(r):
    t = 0.25 - jnp.abs(r)
    x = t * t
    coef = [(-1) ** n * (2.0 * math.pi) ** (2 * n + 1) / math.factorial(2 * n + 1) for n in range(7)]
    out = jnp.full_like(x, coef[-1])
    for c in coef[-2::-1]:
        out = out * x + c
    return out * t


def rotated(g, e):
    low = low_lanes(e.shape)
    turned = swap(e)
    cos2 = jnp.where(low, e, turned)
    sin2 = jnp.where(low, -turned, e)
    return g * cos2 + swap(g) * sin2


def counter_rotated(g, e):
    low = low_lanes(e.shape)
    turned = swap(e)
    cos2 = jnp.where(low, e, turned)
    sin2 = jnp.where(low, -turned, e)
    return g * cos2 - swap(g) * sin2


def store_parts(ft, value, whole, part0, part1):
    half = part0.shape[0]
    whole[ft] = value
    (part0 if ft < half else part1)[ft % half] = value


def start_kernel(dims, pos_hbm, lmn_hbm, gains_hbm, e_ref, g_ref, p_ref, p0_ref, p1_ref, pos_ref, lmn_ref, gains_ref, sems):
    F, T, D, O, R, C = dims
    W = 2 * O
    copies = [
        pltpu.make_async_copy(pos_hbm, pos_ref, sems.at[0]),
        pltpu.make_async_copy(lmn_hbm, lmn_ref, sems.at[1]),
    ]
    part = F // PARTS
    for i in range(PARTS):
        at = pl.ds(i * part, part)
        copies.append(pltpu.make_async_copy(gains_hbm.at[at], gains_ref.at[at], sems.at[2 + i]))
    for copy in copies:
        copy.start()
    own = lax.axis_index("row") * C + lax.axis_index("col")
    first = lax.axis_index("band") * F
    low = low_lanes((D, W))
    rows = lax.broadcasted_iota(jnp.int32, (D, W), 0)
    shift = jnp.where(low, 0.0, 0.25)
    copies[0].wait()
    copies[1].wait()
    pos = pos_ref[:, :, :O]
    for k in range(1, R * C):
        pos = jnp.where(own == k, pos_ref[:, :, k * O : (k + 1) * O], pos)
    pos = jnp.concatenate([pos, pos], axis=-1)
    geometry = []
    for t in range(T):
        total = jnp.zeros((D, W), jnp.float32)
        for k in range(3):
            lm = jnp.full((D, W), lmn_ref[k, 0], jnp.float32)
            for d in range(1, D):
                lm = jnp.where(rows == d, lmn_ref[k, d], lm)
            total = total + lm * pos[k, t : t + 1, :]
        geometry.append(total)
    total_f = F * lax.axis_size("band")
    for f in range(F):
        nu = 1.0 + (first + f).astype(jnp.float32) * (1.0 / total_f)
        for t in range(T):
            ft = f * T + t
            turns = nu * geometry[t]
            r = turns - jnp.round(turns) + shift
            e_ref[ft] = cos_turns(r - jnp.round(r))
    for f in range(F):
        if f % part == 0:
            copies[2 + f // part].wait()
        for t in range(T):
            ft = f * T + t
            g = jnp.concatenate([gains_ref[f, t, 0], gains_ref[f, t, 1]], axis=-1)
            g_ref[ft] = g
            store_parts(ft, rotated(g, e_ref[ft]), p_ref, p0_ref, p1_ref)


def own_terms(dims, flux_ref, live_ref, g_ref, held_ref, slope_ref):
    F, T, D, O, _, _ = dims
    total = jnp.zeros((1, 2 * O), jnp.float32)
    for f in range(F):
        flux = column(flux_ref, f, D, 2 * O)
        for t in range(T):
            ft = f * T + t
            live = live_ref[ft : ft + 1, :]
            g = g_ref[ft]
            power = g * g
            power = (power + swap(power)) * flux
            own = jnp.sum(power, axis=0, keepdims=True)
            total = total + live * own * own
            power = power * flux
            slope_ref[ft] = -live * power
            held_ref[ft] = live * (own * flux - power) * g
    return total


def place(dims, f):
    F = dims[0]
    full = F * lax.axis_size("band")
    at = (lax.axis_index("band") * F + f).astype(jnp.float32)
    return at * (2.0 / (full - 1)) - 1.0


def fit_sums(dims, value, rhs_ref):
    F, T, D, O, _, _ = dims
    for t in range(T):
        acc = [jnp.zeros((D, 2 * O), jnp.float32) for _ in range(4)]
        for f in range(F):
            total = value(f, t)
            x = place(dims, f)
            for k in range(4):
                acc[k] = acc[k] + total
                total = total * x if k < 3 else total
        for k in range(4):
            rhs_ref[k * T + t] = acc[k]


def solve(dims, rhs_refs, t):
    T = dims[1]
    full = dims[0] * lax.axis_size("band")
    grid = 2.0 * np.arange(full, dtype=np.float64) / (full - 1) - 1.0
    basis = np.stack([grid**k for k in range(4)], axis=1)
    inverse = np.linalg.inv(basis.T @ basis)
    rhs = [sum(ref[k * T + t] for ref in rhs_refs) for k in range(4)]
    out = []
    for k in range(4):
        total = float(inverse[k, 0]) * rhs[0]
        for j in range(1, 4):
            total = total + float(inverse[k, j]) * rhs[j]
        out.append(total)
    return out


def curve(coeffs, x):
    return coeffs[0] + x * (coeffs[1] + x * (coeffs[2] + x * coeffs[3]))


def pick(index, parts):
    out = parts[0]
    for k in range(1, len(parts)):
        out = jnp.where(index == k, parts[k], out)
    return out


def setup_kernel(dims, cols, flux_hbm, flags_hbm, duals_hbm, vis_hbm, g_ref, live_col_ref, live_half_ref,
                 live_own_ref, upright_ref, u_ref, rhs_ref, held_ref, slope_ref, samples_ref,
                 extra_ref, head_ref, flux_ref, flags_ref, duals_ref, sems):
    F, T, _, O, R, C = dims
    W, rows, full = 2 * O, C * O, flags_ref.shape[2]
    row = lax.axis_index("row")
    col = lax.axis_index("col")
    copies = [
        pltpu.make_async_copy(flags_hbm, flags_ref, sems.at[0]),
        pltpu.make_async_copy(duals_hbm, duals_ref, sems.at[1]),
        pltpu.make_async_copy(flux_hbm, flux_ref, sems.at[2]),
        pltpu.make_async_copy(vis_hbm.at[pl.ds(0, HEAD)], head_ref, sems.at[3]),
    ]
    for copy in copies:
        copy.start()
    copies[0].wait()
    counts = jnp.zeros((T, full), jnp.float32)
    stacked = []
    for f in range(F):
        live = flags_ref[f].astype(jnp.float32)
        at = slice(f * T, (f + 1) * T)
        mine = pick(row, [live[:, r * rows : (r + 1) * rows] for r in range(R)])
        blocks = [mine[:, c * O : (c + 1) * O] for c in range(C)]
        live_col_ref[at, :] = pick(col, [live[:, c * cols : (c + 1) * cols] for c in range(C)])
        even = jnp.concatenate([blocks[0], blocks[2]], axis=1)
        odd = jnp.concatenate([blocks[1], blocks[3]], axis=1)
        live_half_ref[at, :] = pick(col % 2, [even, odd])
        own = pick(col, blocks)
        live_own_ref[at, :] = jnp.concatenate([own, own], axis=1)
        stacked.append(mine)
        count = jnp.sum(live, axis=1, keepdims=True)
        counts = counts + live * (count - 1.0)
    stacked = jnp.concatenate(stacked + [jnp.zeros((W - F * T, rows), jnp.float32)], axis=0)
    upright_ref[...] = jnp.transpose(stacked)
    samples = jnp.sum(counts, axis=0, keepdims=True)
    samples = jnp.sum(samples, axis=1, keepdims=True) / (R * C)
    copies[1].wait()
    copies[2].wait()
    for f in range(F):
        for t in range(T):
            u_ref[f * T + t] = jnp.concatenate([duals_ref[f, t, 0], duals_ref[f, t, 1]], axis=-1)
    fit_sums(dims, lambda f, t: u_ref[f * T + t] + g_ref[f * T + t], rhs_ref)
    own = own_terms(dims, flux_ref, live_own_ref, g_ref, held_ref, slope_ref)
    lanes = lax.broadcasted_iota(jnp.int32, own.shape, 1)
    samples = jnp.where(lanes == O, samples, 0.0)
    samples_ref[...] = samples
    extra_ref[...] = samples - jnp.where(low_lanes(own.shape), own, 0.0)
    copies[3].wait()


def again_kernel(dims, flux_ref, vis_hbm, samples_ref, live_ref, u_ref, g_ref,
                 rhs_ref, held_ref, slope_ref, extra_ref, head_ref, sem):
    _, T, _, _, _, _ = dims
    copy = pltpu.make_async_copy(vis_hbm.at[pl.ds(0, HEAD)], head_ref, sem.at[0])
    copy.start()
    fit_sums(dims, lambda f, t: u_ref[f * T + t] + g_ref[f * T + t], rhs_ref)
    own = own_terms(dims, flux_ref, live_ref, g_ref, held_ref, slope_ref)
    extra_ref[...] = samples_ref[...] - jnp.where(low_lanes(own.shape), own, 0.0)
    copy.wait()


def add_kernel(a_ref, b_ref, out_ref):
    out_ref[...] = a_ref[...] + b_ref[...]


def target_kernel(dims, first_pass, u_ref, g_ref, *refs):
    F, T, _, _, _, _ = dims
    rhs_refs, outs = refs[:2], refs[2:]
    for t in range(T):
        coeffs = solve(dims, rhs_refs, t)
        for f in range(F):
            ft = f * T + t
            smooth = curve(coeffs, place(dims, f))
            u = u_ref[ft]
            if not first_pass:
                u = u + g_ref[ft] - smooth
                outs[1][ft] = u
            outs[0][ft] = smooth - u


def halves(x):
    high = x.astype(jnp.bfloat16)
    return high, (x - high.astype(jnp.float32)).astype(jnp.bfloat16)


def product(a, b):
    (a0, a1), (b0, b1) = halves(a), halves(b)
    out = jnp.dot(a0, b1, preferred_element_type=jnp.float32)
    out = out + jnp.dot(a1, b0, preferred_element_type=jnp.float32)
    return out + jnp.dot(a0, b0, preferred_element_type=jnp.float32)


def block_mask(size):
    shape = (8 * size, 8 * size)
    a = lax.broadcasted_iota(jnp.int32, shape, 0) // size
    b = lax.broadcasted_iota(jnp.int32, shape, 1) // size
    return a == b


def sum_kernel(dims, skip, flux_hbm, vis_hbm, live_ref, a_ref, b_ref, *refs):
    F, T, D, O, _, _ = dims
    F = F // 2
    head_ref, refs = (None, refs) if skip else (refs[0], refs[1:])
    HEAD = 0 if skip else head_ref.shape[0]
    upright_ref, refs = (refs[0], refs[1:]) if len(refs) == 8 else (None, refs)
    keep_ref, send_ref, refs = refs[0], refs[1], refs[2:]
    power_ref, refs = (refs[0], refs[1:]) if upright_ref is not None else (None, refs)
    vis_ref, distinct, flux_ref, sems = refs
    rows, cols = vis_ref.shape[3], vis_ref.shape[4]
    row = lax.axis_index("row")
    col = lax.axis_index("col")
    parity = col % 2

    def vis_copy(f):
        return pltpu.make_async_copy(vis_hbm.at[skip + f], vis_ref.at[f], sems.at[f])

    flux_copy = pltpu.make_async_copy(flux_hbm, flux_ref, sems.at[F])
    flux_copy.start()
    for f in range(HEAD, F):
        vis_copy(f).start()
    p = lax.broadcasted_iota(jnp.int32, (rows, cols), 0) + row * rows
    q = lax.broadcasted_iota(jnp.int32, (rows, cols), 1) + col * cols
    distinct[...] = jnp.where(p == q, 0.0, 1.0).astype(jnp.bfloat16)
    group = 8 // T
    blocks = block_mask(2 * D)
    nt = (((1,), (1,)), ((), ()))

    def body(step, power, source):
        highs, lows = [], []
        lives = live_ref[pl.ds(skip * T + step * 8, 8), :]
        mask = distinct[...]
        for i in range(group):
            f = step * group + i
            scale = column(flux_ref, skip + f, D, cols)
            for t in range(T):
                j = i * T + t
                ft = step * 8 + j
                a, b = a_ref[ft], b_ref[ft]
                first = jnp.where(row == 0, a, b)
                second = jnp.where(row == 0, b, a)
                weight = scale * lives[j : j + 1, :]
                re = join_low(first, second) * weight
                im = join_high(first, second) * weight
                x = jnp.concatenate(
                    [jnp.concatenate([re, -im], axis=1), jnp.concatenate([im, re], axis=1)], axis=0
                )
                high = x.astype(jnp.bfloat16)
                low = (x - high.astype(jnp.float32)).astype(jnp.bfloat16)
                highs.append(high)
                lows.append(low)
                both = jnp.concatenate([high, low], axis=0)
                seen = [source[f, t, part] * mask for part in range(2)]
                v = lax.dot_general(
                    both, jnp.concatenate(seen, axis=1), nt, preferred_element_type=jnp.float32
                )
                v = v[: 2 * D] + v[2 * D :]
                v0, v1 = v[:, : 2 * O], v[:, 2 * O :]
                even, odd = join_low(v0, v1), join_high(v0, v1)
                keep_ref[step * 9 + j] = jnp.where(parity == 0, even, odd)
                send_ref[step * 9 + j] = jnp.where(parity == 0, odd, even)
                if upright_ref is not None:
                    square = [x.astype(jnp.float32) for x in seen]
                    square = square[0] * square[0] + square[1] * square[1]
                    at = jnp.full(square.shape, skip * T + ft, jnp.int32)
                    square = square * jnp.take_along_axis(
                        upright_ref[...], at, axis=1, mode="promise_in_bounds"
                    )
                    square = jnp.sum(square.reshape(rows // 8, 8, cols), axis=0)
                    power = power + square * lives[j : j + 1, :]
        high = jnp.concatenate(highs, axis=0)
        low = jnp.concatenate(lows, axis=0)
        gram = lax.dot_general(high, high, nt, preferred_element_type=jnp.float32)
        gram = gram + lax.dot_general(high, low, nt, preferred_element_type=jnp.float32)
        gram = gram + lax.dot_general(low, high, nt, preferred_element_type=jnp.float32)
        gram = jnp.where(blocks, gram, 0.0)
        folded = gram[: 2 * D]
        for i in range(1, 8):
            folded = folded + gram[i * 2 * D : (i + 1) * 2 * D]
        keep_ref[step * 9 + 8] = folded
        send_ref[step * 9 + 8] = folded
        return power

    def chunk(c, power):
        for i in range(CHUNK):
            vis_copy(c * CHUNK + i).wait()

        for j in range(CHUNK // group):
            power = body(c * (CHUNK // group) + j, power, vis_ref)
        return power

    flux_copy.wait()
    power = jnp.zeros((8, cols), jnp.float32)
    for j in range(CHUNK // group):
        inside = (j + 1) * group <= HEAD
        if not inside:
            for i in range(group):
                vis_copy(j * group + i).wait()
        power = body(j, power, head_ref if inside else vis_ref)
    power = lax.fori_loop(1, F // CHUNK, chunk, power)
    if power_ref is not None:
        power = jnp.sum(power, axis=0, keepdims=True)
        power_ref[...] = jnp.where(low_lanes(power.shape), power + swap(power), 0.0)


def residual_kernel(dims, live_ref, extra_ref, power0_ref, power1_ref, kept0_ref, kept1_ref,
                    other0_ref, other1_ref, mine_ref, theirs_ref, passed0_ref, passed1_ref,
                    got0_ref, got1_ref, keep_ref, send_ref, scalar_hbm, num_ref, scalar_ref, sem):
    F, T, D, O, _, _ = dims
    W = 2 * O
    row = lax.axis_index("row")
    col = lax.axis_index("col")
    near = col // 2 == 0
    away = col // 2 != row
    held = col % 2 != row
    mask = block_mask(2 * D)
    eye = lax.broadcasted_iota(jnp.int32, (2 * D, W), 0) == (
        lax.broadcasted_iota(jnp.int32, (2 * D, W), 1) % (2 * D)
    )

    def body(whole_group, total):
        late = whole_group >= F * T // 16
        kept_ref, other_ref, passed_ref, got_ref = (
            (kept1_ref, other1_ref, passed1_ref, got1_ref) if late
            else (kept0_ref, other0_ref, passed0_ref, got0_ref)
        )
        group = whole_group % (F * T // 16)
        gram = kept_ref[group * 9 + 8] + other_ref[group * 9 + 8]
        diagonal = jnp.sum(jnp.where(eye, gram, 0.0), axis=0, keepdims=True)
        keep_ref[F * T, pl.ds(whole_group, 1), :] = diagonal
        send_ref[F * T, pl.ds(whole_group, 1), :] = diagonal
        spread = jnp.where(mask, jnp.concatenate([gram] * 8, axis=0), 0.0)
        station = []
        for i in range(8):
            ft, at = whole_group * 8 + i, group * 8 + i
            a = mine_ref[ft]
            b = jnp.where(away, theirs_ref[ft], jnp.where(held, got_ref[at], passed_ref[at]))
            first = jnp.where(near, a, b)
            second = jnp.where(near, b, a)
            station += [join_low(first, second), join_high(first, second)]
        model = product(spread, jnp.concatenate(station, axis=0))
        lives = live_ref[pl.ds(whole_group * 8, 8), :]
        for i in range(8):
            ft = whole_group * 8 + i
            live = lives[i : i + 1, :]
            v = kept_ref[group * 9 + i] + other_ref[group * 9 + i]
            num = (v - model[i * 2 * D : (i + 1) * 2 * D]) * live
            z = jnp.concatenate(station[2 * i : 2 * i + 2], axis=0)
            total = total + z * (v * live + num)
            num_ref[ft] = num
        return total

    total = jnp.zeros((2 * D, W), jnp.float32)
    for group in range(F * T // 8):
        total = body(group, total)
    squares = -jnp.sum(total, axis=0, keepdims=True)
    squares = squares + swap(squares)
    scalar = jnp.where(low_lanes(squares.shape), squares, 0.0) + extra_ref[...] + power0_ref[...] + power1_ref[...]
    scalar_ref[...] = jnp.broadcast_to(scalar, scalar_ref.shape)
    copy = pltpu.make_async_copy(scalar_ref, scalar_hbm, sem.at[0])
    copy.start()
    for ft in range(F * T):
        num = num_ref[ft]
        low, high = join_low(num[:D], num[D:]), join_high(num[:D], num[D:])
        keep_ref[ft] = jnp.where(near, low, high)
        send_ref[ft] = jnp.where(near, high, low)
    copy.wait()


def merge_kernel(dims, keep_ref, come_ref, live_ref, e_ref, g_ref, held_ref, slope_ref,
                 num_ref, den_ref):
    F, T, D, O, _, _ = dims
    W = 2 * O
    shape = (8 * D, W)
    a = lax.broadcasted_iota(jnp.int32, shape, 0)
    b = lax.broadcasted_iota(jnp.int32, shape, 1)
    eye = a // D * (2 * D) + a % D == b
    ones = jnp.ones((W, W), jnp.bfloat16)
    for group in range(F * T // 8):
        diagonal = keep_ref[F * T, group : group + 1, :] + come_ref[F * T, group : group + 1, :]
        rest, spread = jnp.where(eye, diagonal, 0.0), 0.0
        for _ in range(3):
            high = rest.astype(jnp.bfloat16)
            rest = rest - high.astype(jnp.float32)
            spread = spread + jnp.dot(high, ones, preferred_element_type=jnp.float32)
        for i in range(8):
            ft = group * 8 + i
            around = live_ref[ft : ft + 1, :] * spread[i * D : (i + 1) * D]
            num = counter_rotated(keep_ref[ft] + come_ref[ft], e_ref[ft])
            num_ref[ft] = num + held_ref[ft] + around * g_ref[ft]
            den_ref[ft] = around + slope_ref[ft]


def update_kernel(dims, last, full, *refs):
    F, T, D, O, _, _ = dims
    scalar_ref, num_ref, den_ref, target_ref, g_ref, other_ref = refs[:6]
    W = 2 * O
    sums = jnp.sum(scalar_ref[...], axis=0, keepdims=True)
    low = low_lanes(sums.shape)
    squares = jnp.sum(jnp.where(low, sums, 0.0), axis=1, keepdims=True)
    samples = jnp.sum(jnp.where(low, 0.0, sums), axis=1, keepdims=True)
    squares = jnp.maximum(squares, 0.0)
    rho = PENALTY * full * (squares / samples + 1e-06)
    rho = jnp.broadcast_to(rho, (D, W))
    for t in range(T):
        acc = [jnp.zeros((D, W), jnp.float32) for _ in range(4)]
        for f in range(F):
            ft = f * T + t
            fresh = (num_ref[ft] + rho * target_ref[ft]) / (den_ref[ft] + rho)
            g = 0.5 * (g_ref[ft] + fresh)
            if last:
                out_ref, total_ref, rhs_ref = refs[6:]
                out_ref[ft] = g
                total = other_ref[ft] + g
                total_ref[ft] = total
                x = place(dims, f)
                for k in range(4):
                    acc[k] = acc[k] + total
                    total = total * x if k < 3 else total
            else:
                refs[6][ft] = g
                store_parts(ft, rotated(g, other_ref[ft]), *refs[7:])
        if last:
            for k in range(4):
                rhs_ref[k * T + t] = acc[k]


def write_out(dims, value, out_hbm, out_ref, sems):
    F, T, _, O, _, _ = dims
    copies = []
    for part in range(F // CHUNK):
        for f in range(part * CHUNK, (part + 1) * CHUNK):
            for t in range(T):
                x = value(f, t)
                out_ref[f, t, 0] = x[:, :O]
                out_ref[f, t, 1] = x[:, O:]
        at = pl.ds(part * CHUNK, CHUNK)
        copies.append(pltpu.make_async_copy(out_ref.at[at], out_hbm.at[at], sems.at[part]))
        copies[-1].start()
    for copy in copies:
        copy.wait()


def emit_kernel(dims, g_ref, out_hbm, out_ref, sems):
    write_out(dims, lambda f, t: g_ref[f * dims[1] + t], out_hbm, out_ref, sems)


def final_kernel(dims, total_ref, *refs):
    T = dims[1]
    coeffs = [solve(dims, refs[:-3], t) for t in range(T)]
    write_out(
        dims, lambda f, t: total_ref[f * T + t] - curve(coeffs[t], place(dims, f)), *refs[-3:]
    )


def shards(sizes, vis, flags, positions, lmn, flux, gains, duals):
    R, C, Z = sizes
    F, T, _, D, O = gains.shape
    rows, cols = vis.shape[3], vis.shape[4]
    full = flags.shape[2]
    FT, W = F * T, 2 * O
    dims = (F, T, D, O, R, C)
    f32 = jnp.float32
    smem = pl.BlockSpec(memory_space=pltpu.SMEM)
    vmem = pl.BlockSpec(memory_space=pltpu.VMEM)
    hbm = pl.BlockSpec(memory_space=pltpu.HBM)

    def array(*shape):
        return jax.ShapeDtypeStruct(shape, f32)

    def far(x):
        return pltpu.with_memory_space_constraint(x, pltpu.HBM)

    def call(kernel, outs, scalars, arrays, scratch=()):
        return pl.pallas_call(
            kernel,
            out_shape=outs,
            in_specs=[smem] * len(scalars) + [vmem] * len(arrays),
            out_specs=[vmem] * len(outs),
            scratch_shapes=list(scratch),
            compiler_params=LIMIT,
        )(*scalars, *arrays)

    def where(r, c, z):
        return (r * C + c) * Z + z

    def permute(x, move, some=lambda r, c: True):
        pairs = [
            (where(r, c, z), where(*move(r, c, z)))
            for r in range(R) for c in range(C) for z in range(Z) if some(r, c)
        ]
        return lax.ppermute(x, AXES, pairs)

    def gather(x, m):
        return permute(x, lambda r, c, z: (((r * C + c) % R + m) % R, (r * C + c) // R, z))

    def bands(x):
        return [x] + [permute(x, lambda r, c, z, k=k: (r, c, z ^ k)) for k in range(1, Z)]

    part = array(FT // 2, D, W)
    whole, line, fit = array(FT, D, W), array(FT + 1, D, W), array(4 * T, D, W)
    pair, text = array(FT // 8 * 9, 2 * D, W), array(1, W)
    flux_t = flux.T
    start = jax.ShapeDtypeStruct((HEAD,) + vis.shape[1:], vis.dtype)
    rot, g, p, *parts = pl.pallas_call(
        functools.partial(start_kernel, dims),
        out_shape=[whole] * 3 + [part] * 2,
        in_specs=[hbm] * 3,
        out_specs=[vmem] * 5,
        scratch_shapes=[
            pltpu.VMEM((3, T, full), f32),
            pltpu.SMEM(lmn.shape, f32),
            pltpu.VMEM(gains.shape, f32),
            pltpu.SemaphoreType.DMA((2 + PARTS,)),
        ],
        compiler_params=LIMIT,
        name="start",
    )(far(positions.transpose(1, 0, 2)), far(lmn), far(gains))
    for step in range(ITERS):
        last = step == ITERS - 1
        got = [[gather(x, m) for m in range(R)] for x in parts]
        if step == 0:
            (live_col, live_half, live_own, upright, u, rhs, held, slope, samples, extra, head) = (
                pl.pallas_call(
                    functools.partial(setup_kernel, dims, cols),
                    out_shape=[
                        array(FT, cols), array(FT, W), array(FT, W), array(rows, W), whole,
                        fit, whole, whole, text, text, start,
                    ],
                    in_specs=[hbm] * 4 + [vmem],
                    out_specs=[vmem] * 11,
                    scratch_shapes=[
                        pltpu.SMEM(flux_t.shape, f32),
                        pltpu.VMEM(flags.shape, flags.dtype),
                        pltpu.VMEM(duals.shape, f32),
                        pltpu.SemaphoreType.DMA((4,)),
                    ],
                    compiler_params=LIMIT,
                    name="setup",
                )(far(flux_t), far(flags), far(duals), far(vis), g)
            )
        else:
            rhs, held, slope, extra, head = pl.pallas_call(
                functools.partial(again_kernel, dims),
                out_shape=[fit, whole, whole, text, start],
                in_specs=[smem, hbm] + [vmem] * 4,
                out_specs=[vmem] * 5,
                scratch_shapes=[pltpu.SemaphoreType.DMA((1,))],
                compiler_params=LIMIT,
                name="again",
            )(flux_t, far(vis), samples, live_own, u, g)
        rhs_near = permute(rhs, lambda r, c, z: (r, c, z ^ 1))
        theirs = permute(p, lambda r, c, z: (r, c ^ 2, z), lambda r, c: r == c // 2)
        (rhs,) = call(add_kernel, [fit], [], [rhs, rhs_near])
        rhs_far = permute(rhs, lambda r, c, z: (r, c, z ^ 2))
        pair = array(FT // 16 * 9, 2 * D, W)
        keeps, others, passed = [], [], []
        for i in range(2):
            more = ([] if i else [head]) + ([] if step else [upright])
            keep, send, *found = pl.pallas_call(
                functools.partial(sum_kernel, dims, i * (F // 2)),
                out_shape=[pair, pair] + ([] if step else [array(1, cols)]),
                in_specs=[hbm] * 2 + [vmem] * (3 + len(more)),
                out_specs=[vmem] * (2 + len([] if step else [upright])),
                scratch_shapes=[
                    pltpu.VMEM((F // 2,) + vis.shape[1:], vis.dtype),
                    pltpu.VMEM((rows, cols), vis.dtype),
                    pltpu.SMEM(flux_t.shape, f32),
                    pltpu.SemaphoreType.DMA((F // 2 + 1,)),
                ],
                compiler_params=LIMIT,
            )(far(flux_t), far(vis), live_col, *got[i], *more)
            if not step:
                powers = [*found] if i == 0 else powers + [*found]
            keeps.append(keep)
            others.append(permute(send, lambda r, c, z: (r, c ^ 1, z)))
            passed.append(permute(
                got[i][0], lambda r, c, z: (r, c ^ 1, z),
                lambda r, c: c == 3 * r + (1 - 2 * r),
            ))
        everyone = array(R * C * Z, W)
        keep, send, scalar = pl.pallas_call(
            functools.partial(residual_kernel, dims),
            out_shape=[line, line, everyone],
            in_specs=[vmem] * 14,
            out_specs=[vmem, vmem, hbm],
            scratch_shapes=[
                pltpu.VMEM((FT, 2 * D, W), f32), pltpu.VMEM(everyone.shape, f32),
                pltpu.SemaphoreType.DMA((1,)),
            ],
            compiler_params=LIMIT,
            name="residual",
        )(live_half, extra, *powers, *keeps, *others, p, theirs, *passed, got[0][1], got[1][1])
        come = permute(send, lambda r, c, z: (r, c ^ 2, z))
        scalar = lax.all_to_all(scalar, AXES, 0, 0, tiled=True)
        target = call(
            functools.partial(target_kernel, dims, step == 0),
            [whole] * (1 if step == 0 else 2), [], [u, g, rhs, rhs_far],
        )
        num, den = call(
            functools.partial(merge_kernel, dims), [whole, whole], [],
            [keep, come, live_own, rot, g, held, slope],
        )
        update = functools.partial(update_kernel, dims, last, float(full))
        arrays = [scalar, num, den, target[0], g]
        if last:
            g, total, rhs = call(
                update, [whole, whole, fit], [],
                arrays + [target[1]],
            )
        else:
            g, p, *parts = call(update, [whole, whole, part, part], [], arrays + [rot])

    def write(kernel, arrays):
        return pl.pallas_call(
            functools.partial(kernel, dims),
            out_shape=array(*gains.shape),
            in_specs=[vmem] * len(arrays),
            out_specs=hbm,
            scratch_shapes=[pltpu.VMEM(gains.shape, f32), pltpu.SemaphoreType.DMA((F // CHUNK,))],
            compiler_params=LIMIT,
        )(*arrays)

    rhs_all = bands(rhs)
    gain = write(emit_kernel, [g])
    dual = write(final_kernel, [total, *rhs_all])
    return (gain, dual)


def basis(count):
    grid = 2.0 * jnp.arange(count, dtype=jnp.float32) / (count - 1) - 1.0
    return jnp.stack([grid**power for power in range(4)], axis=1)


def rotate(positions, lmn, freq):
    geometry = jnp.einsum("tks,kd->tds", positions, lmn, precision=HIGH)
    angle = 2.0 * math.pi * freq[:, None, None, None] * geometry[None]
    return (jnp.cos(angle), -jnp.sin(angle))


def complex_mul(a_re, a_im, b_re, b_im):
    return (a_re * b_re - a_im * b_im, a_re * b_im + a_im * b_re)


def solve_fit(rhs, total_f):
    full = basis(total_f)
    gram = jnp.dot(full.T, full, precision=HIGH)
    factor = jnp.linalg.cholesky(gram)
    flat = rhs.reshape(rhs.shape[0], -1)
    return jax.scipy.linalg.cho_solve((factor, True), flat).reshape(rhs.shape)


def plain_shards(vis, flags, positions, lmn, flux, gains, duals):
    width = gains.shape[0]
    total_f = width * lax.axis_size("band")
    first = lax.axis_index("band") * width
    local_basis = lax.dynamic_slice_in_dim(basis(total_f), first, width, 0)
    freq = 1.0 + (first + jnp.arange(width, dtype=jnp.int32)).astype(jnp.float32) / total_f
    row_index = lax.axis_index("row")
    col_index = lax.axis_index("col")
    row_count = vis.shape[3]
    col_count = vis.shape[4]
    owned = gains.shape[4]
    own_start = (row_index * lax.axis_size("col") + col_index) * owned
    row_start = row_index * row_count
    col_start = col_index * col_count
    own_cos, own_sin = rotate(lax.dynamic_slice_in_dim(positions, own_start, owned, 2), lmn, freq)
    row_cos, row_sin = rotate(
        lax.dynamic_slice_in_dim(positions, row_start, row_count, 2), lmn, freq
    )
    col_cos, col_sin = rotate(
        lax.dynamic_slice_in_dim(positions, col_start, col_count, 2), lmn, freq
    )
    all_live = flags.astype(jnp.float32)
    row_live = lax.dynamic_slice_in_dim(all_live, row_start, row_count, 2)
    col_live = lax.dynamic_slice_in_dim(all_live, col_start, col_count, 2)
    own_live = lax.dynamic_slice_in_dim(all_live, own_start, owned, 2)
    row_ids = row_start + jnp.arange(row_count, dtype=jnp.int32)
    col_ids = col_start + jnp.arange(col_count, dtype=jnp.int32)
    distinct = (row_ids[:, None] != col_ids[None, :]).astype(jnp.float32)
    weight = row_live[:, :, :, None] * col_live[:, :, None, :] * distinct
    vis_re = vis[:, :, 0].astype(jnp.float32)
    vis_im = vis[:, :, 1].astype(jnp.float32)
    scale = flux[:, None, :, None]

    def fit(gain, dual):
        rhs = jnp.einsum("fk,ftcds->ktcds", local_basis, gain + dual, precision=HIGH)
        return solve_fit(lax.psum(rhs, "band"), total_f)

    gain, dual = (gains, duals)
    coeffs = fit(gain, dual)
    for _ in range(ITERS):
        target = jnp.einsum("fk,ktcds->ftcds", local_basis, coeffs, precision=HIGH) - dual
        every = lax.all_gather(gain, ("row", "col"), axis=4, tiled=True)
        row_gain = lax.dynamic_slice_in_dim(every, row_start, row_count, 4)
        col_gain = lax.dynamic_slice_in_dim(every, col_start, col_count, 4)
        row_re, row_im = complex_mul(row_gain[:, :, 0], row_gain[:, :, 1], row_cos, row_sin)
        col_re, col_im = complex_mul(col_gain[:, :, 0], col_gain[:, :, 1], col_cos, col_sin)
        col_re = scale * col_re
        col_im = scale * col_im
        model_re = jnp.einsum("ftdp,ftdq->ftpq", row_re, col_re, precision=HIGH) + jnp.einsum(
            "ftdp,ftdq->ftpq", row_im, col_im, precision=HIGH
        )
        model_im = jnp.einsum("ftdp,ftdq->ftpq", row_im, col_re, precision=HIGH) - jnp.einsum(
            "ftdp,ftdq->ftpq", row_re, col_im, precision=HIGH
        )
        resid_re = weight * (vis_re - model_re)
        resid_im = weight * (vis_im - model_im)
        squares, samples = lax.psum(
            (jnp.sum(resid_re * resid_re + resid_im * resid_im), jnp.sum(weight)),
            ("row", "col", "band"),
        )
        sum_re = jnp.einsum("ftpq,ftdq->ftdp", resid_re, col_re, precision=HIGH) - jnp.einsum(
            "ftpq,ftdq->ftdp", resid_im, col_im, precision=HIGH
        )
        sum_im = jnp.einsum("ftpq,ftdq->ftdp", resid_re, col_im, precision=HIGH) + jnp.einsum(
            "ftpq,ftdq->ftdp", resid_im, col_re, precision=HIGH
        )
        pairs = lax.psum_scatter(
            jnp.stack([sum_re, sum_im], axis=2), "col", scatter_dimension=4, tiled=True
        )
        every_mag = every[:, :, 0] * every[:, :, 0] + every[:, :, 1] * every[:, :, 1]
        total_mag = jnp.einsum("ftds,fts->ftd", every_mag, all_live, precision=HIGH)
        own_mag = gain[:, :, 0] * gain[:, :, 0] + gain[:, :, 1] * gain[:, :, 1]
        own_flag = own_live[:, :, None, :]
        own_denom = (scale * scale * own_flag * (total_mag[:, :, :, None] - own_flag * own_mag))[
            :, :, None
        ]
        num_re, num_im = complex_mul(own_cos, -own_sin, pairs[:, :, 0], pairs[:, :, 1])
        numer = jnp.stack([num_re, num_im], axis=2)
        rho = PENALTY * flags.shape[2] * (squares / samples + 1e-06)
        fresh = (numer + own_denom * gain + rho * target) / (own_denom + rho)
        gain = 0.5 * (gain + fresh)
        coeffs = fit(gain, dual)
        dual = dual + gain - jnp.einsum("fk,ktcds->ftcds", local_basis, coeffs, precision=HIGH)
    return (gain, dual)


def solution(mesh):
    sizes = tuple(mesh.shape[a] for a in AXES)

    fits = sizes == (2, 4, 4)

    def body(*args):
        gains = args[5]
        if fits and gains.shape[3:] == (8, 64) and 8 % gains.shape[1] == 0:
            return shards(sizes, *args)
        return plain_shards(*args)

    return jax.shard_map(
        body,
        mesh=mesh,
        in_specs=(
            P("band", None, None, "row", "col"),
            P("band", None, None),
            P(),
            P(),
            P("band", None),
            P("band", None, None, None, ("row", "col")),
            P("band", None, None, None, ("row", "col")),
        ),
        out_specs=(
            P("band", None, None, None, ("row", "col")),
            P("band", None, None, None, ("row", "col")),
        ),
        check_vma=False,
    )
```

```python
import functools
import math

import jax
import jax.numpy as jnp
import numpy as np
from jax import lax
from jax.experimental import pallas as pl
from jax.experimental.pallas import tpu as pltpu
from jax.sharding import PartitionSpec as P

ITERS = 2
PENALTY = 0.05
HIGH = lax.Precision.HIGHEST
AXES = ("row", "col", "band")
CHUNK = 4
PARTS = 4
HEAD = 4
LIMIT = pltpu.CompilerParams(vmem_limit_bytes=16 * 2**20)


def swap(x):
    half = x.shape[-1] // 2
    return pltpu.roll(x, half, x.ndim - 1)


def low_lanes(shape):
    return lax.broadcasted_iota(jnp.int32, shape, len(shape) - 1) < shape[-1] // 2


def join_low(a, b):
    return jnp.where(low_lanes(a.shape), a, swap(b))


def join_high(a, b):
    return jnp.where(low_lanes(a.shape), swap(a), b)


def column(ref, index, dirs, lanes):
    rows = lax.broadcasted_iota(jnp.int32, (dirs, lanes), 0)
    out = jnp.full((dirs, lanes), ref[0, index], jnp.float32)
    for d in range(1, dirs):
        out = jnp.where(rows == d, ref[d, index], out)
    return out


def cos_turns(r):
    t = 0.25 - jnp.abs(r)
    x = t * t
    coef = [(-1) ** n * (2.0 * math.pi) ** (2 * n + 1) / math.factorial(2 * n + 1) for n in range(7)]
    out = jnp.full_like(x, coef[-1])
    for c in coef[-2::-1]:
        out = out * x + c
    return out * t


def rotated(g, e):
    low = low_lanes(e.shape)
    turned = swap(e)
    cos2 = jnp.where(low, e, turned)
    sin2 = jnp.where(low, -turned, e)
    return g * cos2 + swap(g) * sin2


def counter_rotated(g, e):
    low = low_lanes(e.shape)
    turned = swap(e)
    cos2 = jnp.where(low, e, turned)
    sin2 = jnp.where(low, -turned, e)
    return g * cos2 - swap(g) * sin2


def start_kernel(dims, pos_hbm, lmn_hbm, gains_hbm, e_ref, g_ref, p_ref, pos_ref, lmn_ref, gains_ref, sems):
    F, T, D, O, R, C = dims
    W = 2 * O
    copies = [
        pltpu.make_async_copy(pos_hbm, pos_ref, sems.at[0]),
        pltpu.make_async_copy(lmn_hbm, lmn_ref, sems.at[1]),
    ]
    part = F // PARTS
    for i in range(PARTS):
        at = pl.ds(i * part, part)
        copies.append(pltpu.make_async_copy(gains_hbm.at[at], gains_ref.at[at], sems.at[2 + i]))
    for copy in copies:
        copy.start()
    own = lax.axis_index("row") * C + lax.axis_index("col")
    first = lax.axis_index("band") * F
    low = low_lanes((D, W))
    rows = lax.broadcasted_iota(jnp.int32, (D, W), 0)
    shift = jnp.where(low, 0.0, 0.25)
    copies[0].wait()
    copies[1].wait()
    pos = pos_ref[:, :, :O]
    for k in range(1, R * C):
        pos = jnp.where(own == k, pos_ref[:, :, k * O : (k + 1) * O], pos)
    pos = jnp.concatenate([pos, pos], axis=-1)
    geometry = []
    for t in range(T):
        total = jnp.zeros((D, W), jnp.float32)
        for k in range(3):
            lm = jnp.full((D, W), lmn_ref[k, 0], jnp.float32)
            for d in range(1, D):
                lm = jnp.where(rows == d, lmn_ref[k, d], lm)
            total = total + lm * pos[k, t : t + 1, :]
        geometry.append(total)
    total_f = F * lax.axis_size("band")
    for f in range(F):
        nu = 1.0 + (first + f).astype(jnp.float32) * (1.0 / total_f)
        for t in range(T):
            ft = f * T + t
            turns = nu * geometry[t]
            r = turns - jnp.round(turns) + shift
            e_ref[ft] = cos_turns(r - jnp.round(r))
    for f in range(F):
        if f % part == 0:
            copies[2 + f // part].wait()
        for t in range(T):
            ft = f * T + t
            g = jnp.concatenate([gains_ref[f, t, 0], gains_ref[f, t, 1]], axis=-1)
            g_ref[ft] = g
            p_ref[ft] = rotated(g, e_ref[ft])


def own_terms(dims, flux_ref, live_ref, g_ref, held_ref, slope_ref):
    F, T, D, O, _, _ = dims
    total = jnp.zeros((1, 2 * O), jnp.float32)
    for f in range(F):
        flux = column(flux_ref, f, D, 2 * O)
        for t in range(T):
            ft = f * T + t
            live = live_ref[ft : ft + 1, :]
            g = g_ref[ft]
            power = g * g
            power = (power + swap(power)) * flux
            own = jnp.sum(power, axis=0, keepdims=True)
            total = total + live * own * own
            power = power * flux
            slope_ref[ft] = -live * power
            held_ref[ft] = live * (own * flux - power) * g
    return total


def place(dims, f):
    F = dims[0]
    full = F * lax.axis_size("band")
    at = (lax.axis_index("band") * F + f).astype(jnp.float32)
    return at * (2.0 / (full - 1)) - 1.0


def fit_sums(dims, value, rhs_ref):
    F, T, D, O, _, _ = dims
    for t in range(T):
        acc = [jnp.zeros((D, 2 * O), jnp.float32) for _ in range(4)]
        for f in range(F):
            total = value(f, t)
            x = place(dims, f)
            for k in range(4):
                acc[k] = acc[k] + total
                total = total * x if k < 3 else total
        for k in range(4):
            rhs_ref[k * T + t] = acc[k]


def solve(dims, rhs_refs, t):
    T = dims[1]
    full = dims[0] * lax.axis_size("band")
    grid = 2.0 * np.arange(full, dtype=np.float64) / (full - 1) - 1.0
    basis = np.stack([grid**k for k in range(4)], axis=1)
    inverse = np.linalg.inv(basis.T @ basis)
    rhs = [sum(ref[k * T + t] for ref in rhs_refs) for k in range(4)]
    out = []
    for k in range(4):
        total = float(inverse[k, 0]) * rhs[0]
        for j in range(1, 4):
            total = total + float(inverse[k, j]) * rhs[j]
        out.append(total)
    return out


def curve(coeffs, x):
    return coeffs[0] + x * (coeffs[1] + x * (coeffs[2] + x * coeffs[3]))


def pick(index, parts):
    out = parts[0]
    for k in range(1, len(parts)):
        out = jnp.where(index == k, parts[k], out)
    return out


def setup_kernel(dims, cols, flux_hbm, flags_hbm, duals_hbm, vis_hbm, g_ref, live_col_ref, live_half_ref,
                 live_own_ref, upright_ref, u_ref, rhs_ref, held_ref, slope_ref, samples_ref,
                 extra_ref, head_ref, flux_ref, flags_ref, duals_ref, sems):
    F, T, _, O, R, C = dims
    W, rows, full = 2 * O, C * O, flags_ref.shape[2]
    row = lax.axis_index("row")
    col = lax.axis_index("col")
    copies = [
        pltpu.make_async_copy(flags_hbm, flags_ref, sems.at[0]),
        pltpu.make_async_copy(duals_hbm, duals_ref, sems.at[1]),
        pltpu.make_async_copy(flux_hbm, flux_ref, sems.at[2]),
        pltpu.make_async_copy(vis_hbm.at[pl.ds(0, HEAD)], head_ref, sems.at[3]),
    ]
    for copy in copies:
        copy.start()
    copies[0].wait()
    counts = jnp.zeros((T, full), jnp.float32)
    stacked = []
    for f in range(F):
        live = flags_ref[f].astype(jnp.float32)
        at = slice(f * T, (f + 1) * T)
        mine = pick(row, [live[:, r * rows : (r + 1) * rows] for r in range(R)])
        blocks = [mine[:, c * O : (c + 1) * O] for c in range(C)]
        live_col_ref[at, :] = pick(col, [live[:, c * cols : (c + 1) * cols] for c in range(C)])
        even = jnp.concatenate([blocks[0], blocks[2]], axis=1)
        odd = jnp.concatenate([blocks[1], blocks[3]], axis=1)
        live_half_ref[at, :] = pick(col % 2, [even, odd])
        own = pick(col, blocks)
        live_own_ref[at, :] = jnp.concatenate([own, own], axis=1)
        stacked.append(mine)
        count = jnp.sum(live, axis=1, keepdims=True)
        counts = counts + live * (count - 1.0)
    stacked = jnp.concatenate(stacked + [jnp.zeros((W - F * T, rows), jnp.float32)], axis=0)
    upright_ref[...] = jnp.transpose(stacked)
    samples = jnp.sum(counts, axis=0, keepdims=True)
    samples = jnp.sum(samples, axis=1, keepdims=True) / (R * C)
    copies[1].wait()
    copies[2].wait()
    for f in range(F):
        for t in range(T):
            u_ref[f * T + t] = jnp.concatenate([duals_ref[f, t, 0], duals_ref[f, t, 1]], axis=-1)
    fit_sums(dims, lambda f, t: u_ref[f * T + t] + g_ref[f * T + t], rhs_ref)
    own = own_terms(dims, flux_ref, live_own_ref, g_ref, held_ref, slope_ref)
    lanes = lax.broadcasted_iota(jnp.int32, own.shape, 1)
    samples = jnp.where(lanes == O, samples, 0.0)
    samples_ref[...] = samples
    extra_ref[...] = samples - jnp.where(low_lanes(own.shape), own, 0.0)
    copies[3].wait()


def again_kernel(dims, flux_ref, vis_hbm, samples_ref, live_ref, u_ref, g_ref,
                 rhs_ref, held_ref, slope_ref, extra_ref, head_ref, sem):
    _, T, _, _, _, _ = dims
    copy = pltpu.make_async_copy(vis_hbm.at[pl.ds(0, HEAD)], head_ref, sem.at[0])
    copy.start()
    fit_sums(dims, lambda f, t: u_ref[f * T + t] + g_ref[f * T + t], rhs_ref)
    own = own_terms(dims, flux_ref, live_ref, g_ref, held_ref, slope_ref)
    extra_ref[...] = samples_ref[...] - jnp.where(low_lanes(own.shape), own, 0.0)
    copy.wait()


def add_kernel(a_ref, b_ref, out_ref):
    out_ref[...] = a_ref[...] + b_ref[...]


def target_kernel(dims, first_pass, u_ref, g_ref, *refs):
    F, T, _, _, _, _ = dims
    rhs_refs, outs = refs[:2], refs[2:]
    for t in range(T):
        coeffs = solve(dims, rhs_refs, t)
        for f in range(F):
            ft = f * T + t
            smooth = curve(coeffs, place(dims, f))
            u = u_ref[ft]
            if not first_pass:
                u = u + g_ref[ft] - smooth
                outs[1][ft] = u
            outs[0][ft] = smooth - u


def halves(x):
    high = x.astype(jnp.bfloat16)
    return high, (x - high.astype(jnp.float32)).astype(jnp.bfloat16)


def product(a, b):
    (a0, a1), (b0, b1) = halves(a), halves(b)
    out = jnp.dot(a0, b1, preferred_element_type=jnp.float32)
    out = out + jnp.dot(a1, b0, preferred_element_type=jnp.float32)
    return out + jnp.dot(a0, b0, preferred_element_type=jnp.float32)


def block_mask(size):
    shape = (8 * size, 8 * size)
    a = lax.broadcasted_iota(jnp.int32, shape, 0) // size
    b = lax.broadcasted_iota(jnp.int32, shape, 1) // size
    return a == b


def sum_kernel(dims, flux_hbm, vis_hbm, live_ref, a_ref, b_ref, head_ref, *refs):
    F, T, D, O, _, _ = dims
    upright_ref, refs = (refs[0], refs[1:]) if len(refs) == 8 else (None, refs)
    keep_ref, send_ref, refs = refs[0], refs[1], refs[2:]
    power_ref, refs = (refs[0], refs[1:]) if upright_ref is not None else (None, refs)
    vis_ref, distinct, flux_ref, sems = refs
    rows, cols = vis_ref.shape[3], vis_ref.shape[4]
    row = lax.axis_index("row")
    col = lax.axis_index("col")
    parity = col % 2

    def vis_copy(f):
        return pltpu.make_async_copy(vis_hbm.at[f], vis_ref.at[f], sems.at[f])

    flux_copy = pltpu.make_async_copy(flux_hbm, flux_ref, sems.at[F])
    flux_copy.start()
    for f in range(HEAD, F):
        vis_copy(f).start()
    p = lax.broadcasted_iota(jnp.int32, (rows, cols), 0) + row * rows
    q = lax.broadcasted_iota(jnp.int32, (rows, cols), 1) + col * cols
    distinct[...] = jnp.where(p == q, 0.0, 1.0).astype(jnp.bfloat16)
    group = 8 // T
    blocks = block_mask(2 * D)
    nt = (((1,), (1,)), ((), ()))

    def body(step, power, source):
        highs, lows = [], []
        lives = live_ref[pl.ds(step * 8, 8), :]
        mask = distinct[...]
        for i in range(group):
            f = step * group + i
            scale = column(flux_ref, f, D, cols)
            for t in range(T):
                j = i * T + t
                ft = step * 8 + j
                a, b = a_ref[ft], b_ref[ft]
                first = jnp.where(row == 0, a, b)
                second = jnp.where(row == 0, b, a)
                weight = scale * lives[j : j + 1, :]
                re = join_low(first, second) * weight
                im = join_high(first, second) * weight
                x = jnp.concatenate(
                    [jnp.concatenate([re, -im], axis=1), jnp.concatenate([im, re], axis=1)], axis=0
                )
                high = x.astype(jnp.bfloat16)
                low = (x - high.astype(jnp.float32)).astype(jnp.bfloat16)
                highs.append(high)
                lows.append(low)
                both = jnp.concatenate([high, low], axis=0)
                seen = [source[f, t, part] * mask for part in range(2)]
                v = lax.dot_general(
                    both, jnp.concatenate(seen, axis=1), nt, preferred_element_type=jnp.float32
                )
                v = v[: 2 * D] + v[2 * D :]
                v0, v1 = v[:, : 2 * O], v[:, 2 * O :]
                even, odd = join_low(v0, v1), join_high(v0, v1)
                keep_ref[step * 9 + j] = jnp.where(parity == 0, even, odd)
                send_ref[step * 9 + j] = jnp.where(parity == 0, odd, even)
                if upright_ref is not None:
                    square = [x.astype(jnp.float32) for x in seen]
                    square = square[0] * square[0] + square[1] * square[1]
                    at = jnp.full(square.shape, ft, jnp.int32)
                    square = square * jnp.take_along_axis(
                        upright_ref[...], at, axis=1, mode="promise_in_bounds"
                    )
                    square = jnp.sum(square.reshape(rows // 8, 8, cols), axis=0)
                    power = power + square * lives[j : j + 1, :]
        high = jnp.concatenate(highs, axis=0)
        low = jnp.concatenate(lows, axis=0)
        gram = lax.dot_general(high, high, nt, preferred_element_type=jnp.float32)
        gram = gram + lax.dot_general(high, low, nt, preferred_element_type=jnp.float32)
        gram = gram + lax.dot_general(low, high, nt, preferred_element_type=jnp.float32)
        gram = jnp.where(blocks, gram, 0.0)
        folded = gram[: 2 * D]
        for i in range(1, 8):
            folded = folded + gram[i * 2 * D : (i + 1) * 2 * D]
        keep_ref[step * 9 + 8] = folded
        send_ref[step * 9 + 8] = folded
        return power

    def chunk(c, power):
        for i in range(CHUNK):
            vis_copy(c * CHUNK + i).wait()

        for j in range(CHUNK // group):
            power = body(c * (CHUNK // group) + j, power, vis_ref)
        return power

    flux_copy.wait()
    power = jnp.zeros((8, cols), jnp.float32)
    for j in range(CHUNK // group):
        inside = (j + 1) * group <= HEAD
        if not inside:
            for i in range(group):
                vis_copy(j * group + i).wait()
        power = body(j, power, head_ref if inside else vis_ref)
    power = lax.fori_loop(1, F // CHUNK, chunk, power)
    if power_ref is not None:
        power = jnp.sum(power, axis=0, keepdims=True)
        power_ref[...] = jnp.where(low_lanes(power.shape), power + swap(power), 0.0)


def residual_kernel(dims, live_ref, extra_ref, power_ref, kept_ref, other_ref, mine_ref, theirs_ref,
                    passed_ref, got_ref, keep_ref, send_ref, scalar_hbm, num_ref, scalar_ref, sem):
    F, T, D, O, _, _ = dims
    W = 2 * O
    row = lax.axis_index("row")
    col = lax.axis_index("col")
    near = col // 2 == 0
    away = col // 2 != row
    held = col % 2 != row
    mask = block_mask(2 * D)
    eye = lax.broadcasted_iota(jnp.int32, (2 * D, W), 0) == (
        lax.broadcasted_iota(jnp.int32, (2 * D, W), 1) % (2 * D)
    )

    def body(group, total):
        gram = kept_ref[group * 9 + 8] + other_ref[group * 9 + 8]
        diagonal = jnp.sum(jnp.where(eye, gram, 0.0), axis=0, keepdims=True)
        keep_ref[F * T, pl.ds(group, 1), :] = diagonal
        send_ref[F * T, pl.ds(group, 1), :] = diagonal
        spread = jnp.where(mask, jnp.concatenate([gram] * 8, axis=0), 0.0)
        station = []
        for i in range(8):
            ft = group * 8 + i
            a = mine_ref[ft]
            b = jnp.where(away, theirs_ref[ft], jnp.where(held, got_ref[ft], passed_ref[ft]))
            first = jnp.where(near, a, b)
            second = jnp.where(near, b, a)
            station += [join_low(first, second), join_high(first, second)]
        model = product(spread, jnp.concatenate(station, axis=0))
        lives = live_ref[pl.ds(group * 8, 8), :]
        for i in range(8):
            ft = group * 8 + i
            live = lives[i : i + 1, :]
            v = kept_ref[group * 9 + i] + other_ref[group * 9 + i]
            num = (v - model[i * 2 * D : (i + 1) * 2 * D]) * live
            z = jnp.concatenate(station[2 * i : 2 * i + 2], axis=0)
            total = total + z * (v * live + num)
            num_ref[ft] = num
        return total

    total = jnp.zeros((2 * D, W), jnp.float32)
    for group in range(F * T // 8):
        total = body(group, total)
    squares = -jnp.sum(total, axis=0, keepdims=True)
    squares = squares + swap(squares)
    scalar = jnp.where(low_lanes(squares.shape), squares, 0.0) + extra_ref[...] + power_ref[...]
    scalar_ref[...] = jnp.broadcast_to(scalar, scalar_ref.shape)
    copy = pltpu.make_async_copy(scalar_ref, scalar_hbm, sem.at[0])
    copy.start()
    for ft in range(F * T):
        num = num_ref[ft]
        low, high = join_low(num[:D], num[D:]), join_high(num[:D], num[D:])
        keep_ref[ft] = jnp.where(near, low, high)
        send_ref[ft] = jnp.where(near, high, low)
    copy.wait()


def merge_kernel(dims, keep_ref, come_ref, live_ref, e_ref, g_ref, held_ref, slope_ref,
                 num_ref, den_ref):
    F, T, D, O, _, _ = dims
    W = 2 * O
    shape = (8 * D, W)
    a = lax.broadcasted_iota(jnp.int32, shape, 0)
    b = lax.broadcasted_iota(jnp.int32, shape, 1)
    eye = a // D * (2 * D) + a % D == b
    ones = jnp.ones((W, W), jnp.bfloat16)
    for group in range(F * T // 8):
        diagonal = keep_ref[F * T, group : group + 1, :] + come_ref[F * T, group : group + 1, :]
        rest, spread = jnp.where(eye, diagonal, 0.0), 0.0
        for _ in range(3):
            high = rest.astype(jnp.bfloat16)
            rest = rest - high.astype(jnp.float32)
            spread = spread + jnp.dot(high, ones, preferred_element_type=jnp.float32)
        for i in range(8):
            ft = group * 8 + i
            around = live_ref[ft : ft + 1, :] * spread[i * D : (i + 1) * D]
            num = counter_rotated(keep_ref[ft] + come_ref[ft], e_ref[ft])
            num_ref[ft] = num + held_ref[ft] + around * g_ref[ft]
            den_ref[ft] = around + slope_ref[ft]


def update_kernel(dims, last, full, *refs):
    F, T, D, O, _, _ = dims
    scalar_ref, num_ref, den_ref, target_ref, g_ref, other_ref = refs[:6]
    W = 2 * O
    sums = jnp.sum(scalar_ref[...], axis=0, keepdims=True)
    low = low_lanes(sums.shape)
    squares = jnp.sum(jnp.where(low, sums, 0.0), axis=1, keepdims=True)
    samples = jnp.sum(jnp.where(low, 0.0, sums), axis=1, keepdims=True)
    squares = jnp.maximum(squares, 0.0)
    rho = PENALTY * full * (squares / samples + 1e-06)
    rho = jnp.broadcast_to(rho, (D, W))
    for t in range(T):
        acc = [jnp.zeros((D, W), jnp.float32) for _ in range(4)]
        for f in range(F):
            ft = f * T + t
            fresh = (num_ref[ft] + rho * target_ref[ft]) / (den_ref[ft] + rho)
            g = 0.5 * (g_ref[ft] + fresh)
            if last:
                out_ref, total_ref, rhs_ref = refs[6:]
                out_ref[ft] = g
                total = other_ref[ft] + g
                total_ref[ft] = total
                x = place(dims, f)
                for k in range(4):
                    acc[k] = acc[k] + total
                    total = total * x if k < 3 else total
            else:
                g_out, p_out = refs[6:]
                g_out[ft] = g
                p_out[ft] = rotated(g, other_ref[ft])
        if last:
            for k in range(4):
                rhs_ref[k * T + t] = acc[k]


def write_out(dims, value, out_hbm, out_ref, sems):
    F, T, _, O, _, _ = dims
    copies = []
    for part in range(F // CHUNK):
        for f in range(part * CHUNK, (part + 1) * CHUNK):
            for t in range(T):
                x = value(f, t)
                out_ref[f, t, 0] = x[:, :O]
                out_ref[f, t, 1] = x[:, O:]
        at = pl.ds(part * CHUNK, CHUNK)
        copies.append(pltpu.make_async_copy(out_ref.at[at], out_hbm.at[at], sems.at[part]))
        copies[-1].start()
    for copy in copies:
        copy.wait()


def emit_kernel(dims, g_ref, out_hbm, out_ref, sems):
    write_out(dims, lambda f, t: g_ref[f * dims[1] + t], out_hbm, out_ref, sems)


def final_kernel(dims, total_ref, *refs):
    T = dims[1]
    coeffs = [solve(dims, refs[:-3], t) for t in range(T)]
    write_out(
        dims, lambda f, t: total_ref[f * T + t] - curve(coeffs[t], place(dims, f)), *refs[-3:]
    )


def shards(sizes, vis, flags, positions, lmn, flux, gains, duals):
    R, C, Z = sizes
    F, T, _, D, O = gains.shape
    rows, cols = vis.shape[3], vis.shape[4]
    full = flags.shape[2]
    FT, W = F * T, 2 * O
    dims = (F, T, D, O, R, C)
    f32 = jnp.float32
    smem = pl.BlockSpec(memory_space=pltpu.SMEM)
    vmem = pl.BlockSpec(memory_space=pltpu.VMEM)
    hbm = pl.BlockSpec(memory_space=pltpu.HBM)

    def array(*shape):
        return jax.ShapeDtypeStruct(shape, f32)

    def far(x):
        return pltpu.with_memory_space_constraint(x, pltpu.HBM)

    def call(kernel, outs, scalars, arrays, scratch=()):
        return pl.pallas_call(
            kernel,
            out_shape=outs,
            in_specs=[smem] * len(scalars) + [vmem] * len(arrays),
            out_specs=[vmem] * len(outs),
            scratch_shapes=list(scratch),
            compiler_params=LIMIT,
        )(*scalars, *arrays)

    def where(r, c, z):
        return (r * C + c) * Z + z

    def permute(x, move, some=lambda r, c: True):
        pairs = [
            (where(r, c, z), where(*move(r, c, z)))
            for r in range(R) for c in range(C) for z in range(Z) if some(r, c)
        ]
        return lax.ppermute(x, AXES, pairs)

    def gather(x, m):
        return permute(x, lambda r, c, z: (((r * C + c) % R + m) % R, (r * C + c) // R, z))

    def bands(x):
        return [x] + [permute(x, lambda r, c, z, k=k: (r, c, z ^ k)) for k in range(1, Z)]

    whole, line, fit = array(FT, D, W), array(FT + 1, D, W), array(4 * T, D, W)
    pair, text = array(FT // 8 * 9, 2 * D, W), array(1, W)
    flux_t = flux.T
    start = jax.ShapeDtypeStruct((HEAD,) + vis.shape[1:], vis.dtype)
    rot, g, p = pl.pallas_call(
        functools.partial(start_kernel, dims),
        out_shape=[whole] * 3,
        in_specs=[hbm] * 3,
        out_specs=[vmem] * 3,
        scratch_shapes=[
            pltpu.VMEM((3, T, full), f32),
            pltpu.SMEM(lmn.shape, f32),
            pltpu.VMEM(gains.shape, f32),
            pltpu.SemaphoreType.DMA((2 + PARTS,)),
        ],
        compiler_params=LIMIT,
        name="start",
    )(far(positions.transpose(1, 0, 2)), far(lmn), far(gains))
    for step in range(ITERS):
        last = step == ITERS - 1
        got = [gather(p, m) for m in range(R)]
        if step == 0:
            (live_col, live_half, live_own, upright, u, rhs, held, slope, samples, extra, head) = (
                pl.pallas_call(
                    functools.partial(setup_kernel, dims, cols),
                    out_shape=[
                        array(FT, cols), array(FT, W), array(FT, W), array(rows, W), whole,
                        fit, whole, whole, text, text, start,
                    ],
                    in_specs=[hbm] * 4 + [vmem],
                    out_specs=[vmem] * 11,
                    scratch_shapes=[
                        pltpu.SMEM(flux_t.shape, f32),
                        pltpu.VMEM(flags.shape, flags.dtype),
                        pltpu.VMEM(duals.shape, f32),
                        pltpu.SemaphoreType.DMA((4,)),
                    ],
                    compiler_params=LIMIT,
                    name="setup",
                )(far(flux_t), far(flags), far(duals), far(vis), g)
            )
        else:
            rhs, held, slope, extra, head = pl.pallas_call(
                functools.partial(again_kernel, dims),
                out_shape=[fit, whole, whole, text, start],
                in_specs=[smem, hbm] + [vmem] * 4,
                out_specs=[vmem] * 5,
                scratch_shapes=[pltpu.SemaphoreType.DMA((1,))],
                compiler_params=LIMIT,
                name="again",
            )(flux_t, far(vis), samples, live_own, u, g)
        rhs_near = permute(rhs, lambda r, c, z: (r, c, z ^ 1))
        theirs = permute(p, lambda r, c, z: (r, c ^ 2, z), lambda r, c: r == c // 2)
        more = [] if step else [upright]
        keep, send, *found = pl.pallas_call(
            functools.partial(sum_kernel, dims),
            out_shape=[pair, pair] + ([] if step else [array(1, cols)]),
            in_specs=[hbm] * 2 + [vmem] * (4 + len(more)),
            out_specs=[vmem] * (2 + len(more)),
            scratch_shapes=[
                pltpu.VMEM(vis.shape, vis.dtype),
                pltpu.VMEM((rows, cols), vis.dtype),
                pltpu.SMEM(flux_t.shape, f32),
                pltpu.SemaphoreType.DMA((F + 1,)),
            ],
            compiler_params=LIMIT,
            name="sums",
        )(far(flux_t), far(vis), live_col, *got, head, *more)
        power = power if step else found[0]
        passed = permute(
            got[0], lambda r, c, z: (r, c ^ 1, z), lambda r, c: c == 3 * r + (1 - 2 * r)
        )
        other = permute(send, lambda r, c, z: (r, c ^ 1, z))
        (rhs,) = call(add_kernel, [fit], [], [rhs, rhs_near])
        rhs_far = permute(rhs, lambda r, c, z: (r, c, z ^ 2))
        everyone = array(R * C * Z, W)
        keep, send, scalar = pl.pallas_call(
            functools.partial(residual_kernel, dims),
            out_shape=[line, line, everyone],
            in_specs=[vmem] * 9,
            out_specs=[vmem, vmem, hbm],
            scratch_shapes=[
                pltpu.VMEM((FT, 2 * D, W), f32), pltpu.VMEM(everyone.shape, f32),
                pltpu.SemaphoreType.DMA((1,)),
            ],
            compiler_params=LIMIT,
            name="residual",
        )(live_half, extra, power, keep, other, p, theirs, passed, got[1])
        come = permute(send, lambda r, c, z: (r, c ^ 2, z))
        scalar = lax.all_to_all(scalar, AXES, 0, 0, tiled=True)
        target = call(
            functools.partial(target_kernel, dims, step == 0),
            [whole] * (1 if step == 0 else 2), [], [u, g, rhs, rhs_far],
        )
        num, den = call(
            functools.partial(merge_kernel, dims), [whole, whole], [],
            [keep, come, live_own, rot, g, held, slope],
        )
        update = functools.partial(update_kernel, dims, last, float(full))
        arrays = [scalar, num, den, target[0], g]
        if last:
            g, total, rhs = call(
                update, [whole, whole, fit], [],
                arrays + [target[1]],
            )
        else:
            g, p = call(update, [whole, whole], [], arrays + [rot])

    def write(kernel, arrays):
        return pl.pallas_call(
            functools.partial(kernel, dims),
            out_shape=array(*gains.shape),
            in_specs=[vmem] * len(arrays),
            out_specs=hbm,
            scratch_shapes=[pltpu.VMEM(gains.shape, f32), pltpu.SemaphoreType.DMA((F // CHUNK,))],
            compiler_params=LIMIT,
        )(*arrays)

    rhs_all = bands(rhs)
    gain = write(emit_kernel, [g])
    dual = write(final_kernel, [total, *rhs_all])
    return (gain, dual)


def basis(count):
    grid = 2.0 * jnp.arange(count, dtype=jnp.float32) / (count - 1) - 1.0
    return jnp.stack([grid**power for power in range(4)], axis=1)


def rotate(positions, lmn, freq):
    geometry = jnp.einsum("tks,kd->tds", positions, lmn, precision=HIGH)
    angle = 2.0 * math.pi * freq[:, None, None, None] * geometry[None]
    return (jnp.cos(angle), -jnp.sin(angle))


def complex_mul(a_re, a_im, b_re, b_im):
    return (a_re * b_re - a_im * b_im, a_re * b_im + a_im * b_re)


def solve_fit(rhs, total_f):
    full = basis(total_f)
    gram = jnp.dot(full.T, full, precision=HIGH)
    factor = jnp.linalg.cholesky(gram)
    flat = rhs.reshape(rhs.shape[0], -1)
    return jax.scipy.linalg.cho_solve((factor, True), flat).reshape(rhs.shape)


def plain_shards(vis, flags, positions, lmn, flux, gains, duals):
    width = gains.shape[0]
    total_f = width * lax.axis_size("band")
    first = lax.axis_index("band") * width
    local_basis = lax.dynamic_slice_in_dim(basis(total_f), first, width, 0)
    freq = 1.0 + (first + jnp.arange(width, dtype=jnp.int32)).astype(jnp.float32) / total_f
    row_index = lax.axis_index("row")
    col_index = lax.axis_index("col")
    row_count = vis.shape[3]
    col_count = vis.shape[4]
    owned = gains.shape[4]
    own_start = (row_index * lax.axis_size("col") + col_index) * owned
    row_start = row_index * row_count
    col_start = col_index * col_count
    own_cos, own_sin = rotate(lax.dynamic_slice_in_dim(positions, own_start, owned, 2), lmn, freq)
    row_cos, row_sin = rotate(
        lax.dynamic_slice_in_dim(positions, row_start, row_count, 2), lmn, freq
    )
    col_cos, col_sin = rotate(
        lax.dynamic_slice_in_dim(positions, col_start, col_count, 2), lmn, freq
    )
    all_live = flags.astype(jnp.float32)
    row_live = lax.dynamic_slice_in_dim(all_live, row_start, row_count, 2)
    col_live = lax.dynamic_slice_in_dim(all_live, col_start, col_count, 2)
    own_live = lax.dynamic_slice_in_dim(all_live, own_start, owned, 2)
    row_ids = row_start + jnp.arange(row_count, dtype=jnp.int32)
    col_ids = col_start + jnp.arange(col_count, dtype=jnp.int32)
    distinct = (row_ids[:, None] != col_ids[None, :]).astype(jnp.float32)
    weight = row_live[:, :, :, None] * col_live[:, :, None, :] * distinct
    vis_re = vis[:, :, 0].astype(jnp.float32)
    vis_im = vis[:, :, 1].astype(jnp.float32)
    scale = flux[:, None, :, None]

    def fit(gain, dual):
        rhs = jnp.einsum("fk,ftcds->ktcds", local_basis, gain + dual, precision=HIGH)
        return solve_fit(lax.psum(rhs, "band"), total_f)

    gain, dual = (gains, duals)
    coeffs = fit(gain, dual)
    for _ in range(ITERS):
        target = jnp.einsum("fk,ktcds->ftcds", local_basis, coeffs, precision=HIGH) - dual
        every = lax.all_gather(gain, ("row", "col"), axis=4, tiled=True)
        row_gain = lax.dynamic_slice_in_dim(every, row_start, row_count, 4)
        col_gain = lax.dynamic_slice_in_dim(every, col_start, col_count, 4)
        row_re, row_im = complex_mul(row_gain[:, :, 0], row_gain[:, :, 1], row_cos, row_sin)
        col_re, col_im = complex_mul(col_gain[:, :, 0], col_gain[:, :, 1], col_cos, col_sin)
        col_re = scale * col_re
        col_im = scale * col_im
        model_re = jnp.einsum("ftdp,ftdq->ftpq", row_re, col_re, precision=HIGH) + jnp.einsum(
            "ftdp,ftdq->ftpq", row_im, col_im, precision=HIGH
        )
        model_im = jnp.einsum("ftdp,ftdq->ftpq", row_im, col_re, precision=HIGH) - jnp.einsum(
            "ftdp,ftdq->ftpq", row_re, col_im, precision=HIGH
        )
        resid_re = weight * (vis_re - model_re)
        resid_im = weight * (vis_im - model_im)
        squares, samples = lax.psum(
            (jnp.sum(resid_re * resid_re + resid_im * resid_im), jnp.sum(weight)),
            ("row", "col", "band"),
        )
        sum_re = jnp.einsum("ftpq,ftdq->ftdp", resid_re, col_re, precision=HIGH) - jnp.einsum(
            "ftpq,ftdq->ftdp", resid_im, col_im, precision=HIGH
        )
        sum_im = jnp.einsum("ftpq,ftdq->ftdp", resid_re, col_im, precision=HIGH) + jnp.einsum(
            "ftpq,ftdq->ftdp", resid_im, col_re, precision=HIGH
        )
        pairs = lax.psum_scatter(
            jnp.stack([sum_re, sum_im], axis=2), "col", scatter_dimension=4, tiled=True
        )
        every_mag = every[:, :, 0] * every[:, :, 0] + every[:, :, 1] * every[:, :, 1]
        total_mag = jnp.einsum("ftds,fts->ftd", every_mag, all_live, precision=HIGH)
        own_mag = gain[:, :, 0] * gain[:, :, 0] + gain[:, :, 1] * gain[:, :, 1]
        own_flag = own_live[:, :, None, :]
        own_denom = (scale * scale * own_flag * (total_mag[:, :, :, None] - own_flag * own_mag))[
            :, :, None
        ]
        num_re, num_im = complex_mul(own_cos, -own_sin, pairs[:, :, 0], pairs[:, :, 1])
        numer = jnp.stack([num_re, num_im], axis=2)
        rho = PENALTY * flags.shape[2] * (squares / samples + 1e-06)
        fresh = (numer + own_denom * gain + rho * target) / (own_denom + rho)
        gain = 0.5 * (gain + fresh)
        coeffs = fit(gain, dual)
        dual = dual + gain - jnp.einsum("fk,ktcds->ftcds", local_basis, coeffs, precision=HIGH)
    return (gain, dual)


def solution(mesh):
    sizes = tuple(mesh.shape[a] for a in AXES)

    fits = sizes == (2, 4, 4)

    def body(*args):
        gains = args[5]
        if fits and gains.shape[3:] == (8, 64) and 8 % gains.shape[1] == 0:
            return shards(sizes, *args)
        return plain_shards(*args)

    return jax.shard_map(
        body,
        mesh=mesh,
        in_specs=(
            P("band", None, None, "row", "col"),
            P("band", None, None),
            P(),
            P(),
            P("band", None),
            P("band", None, None, None, ("row", "col")),
            P("band", None, None, None, ("row", "col")),
        ),
        out_specs=(
            P("band", None, None, None, ("row", "col")),
            P("band", None, None, None, ("row", "col")),
        ),
        check_vma=False,
    )
```
